32 devices in a mesh: rep: 2 (over y), tm: 8 (over z, x), col: 2 (over core).
Axes of the slice: x: 2, y: 2, z: 4, core: 2. Of those that a mesh axis runs over, the one named last changes fastest.
Arguments:
- diagonal_block_inverse: float32 [32, 512, 512], P(('rep', 'tm'), None, 'col'), parts along dimension 0, may hold values from -0.1 to 4.5, as said below
- step_map: bfloat16 [32, 512, 512], P(('rep', 'tm'), None, 'col'), parts along dimension 0, may hold values from -1.1 to 1.1
- arrow_map: bfloat16 [32, 32, 512], P(('rep', 'tm'), None, 'col'), parts along dimension 0, may hold values from -0.1796875 to 0.1796875
- arrow_cov: float32 [64, 32], P('rep'), parts along dimension 0, may hold values from -0.5 to 2.5, as said below
Outputs:
- blocks: float32 [32, 512, 512], P(('rep', 'tm'), None, 'col'), parts along dimension 0
- cross: float32 [32, 32, 512], P(('rep', 'tm'), None, 'col'), parts along dimension 0
The draws below stay inside these ranges and needn't reach their ends.
There are 2 independent parts, one for each index of `rep`. The reference program is written for one: setup_inputs(seed, part) draws one part's arguments, and reference() takes and returns one part's arrays. A program takes and returns all parts, laid end to end along the dimension named above; each array names one. Nothing has to cross between parts.
Inputs may be any that keep to these rules, and one draw needn't show every extreme that they name: `diagonal_block_inverse`: symmetric in its last two dimensions. `arrow_cov`: symmetric.
All inputs are finite; a program needn't handle non-finite values.
Results may differ from the reference program's by a relative error of at most 0.019.
Values may be sent and summed in bfloat16 or wider, within the bound.
A program may use at most 384 MiB of HBM per device.

```python
import math
import jax
import jax.numpy as jnp
from jax import lax

NODES = 512
FIXED_EFFECTS = 32
TOTAL_TIME_STEPS = 16


def slow_pairs(key):
    share = 0.5
    return jax.random.uniform(jax.random.fold_in(key, 5), (NODES // 2,), jnp.float32) < share


def draw_diagonal_block_inverse(key, part):
    base = jax.random.fold_in(key, 11)
    first = jax.random.fold_in(base, 0)
    second = jax.random.fold_in(base, 1)
    fourth = jax.random.fold_in(base, 3)
    slow = jnp.tile(slow_pairs(key), 2)
    slow_levels = jnp.exp(jax.random.uniform(first, (TOTAL_TIME_STEPS, NODES), jnp.float32, math.log(0.5), math.log(2.0))) / TOTAL_TIME_STEPS
    fast_levels = jnp.exp(jax.random.uniform(fourth, (TOTAL_TIME_STEPS, NODES), jnp.float32, math.log(0.2), math.log(1.0)))
    levels = jnp.where(slow[None, :], slow_levels, fast_levels)
    noise = jax.random.normal(second, (TOTAL_TIME_STEPS, NODES, NODES), jnp.float32) * (0.2 / math.sqrt(NODES))
    mirrored = noise + jnp.swapaxes(noise, 1, 2)
    ident = (lax.broadcasted_iota(jnp.int32, (NODES, NODES), 0) == lax.broadcasted_iota(jnp.int32, (NODES, NODES), 1)).astype(jnp.float32)
    return ident[None] * levels[:, :, None] + 0.02 * mirrored


def draw_step_map(key, part):
    base = jax.random.fold_in(key, 23)
    random_key_list = jax.random.split(base, 6)
    half = NODES // 2
    slow = slow_pairs(key)
    slow_rate = 0.3 ** (1.0 / (2 * TOTAL_TIME_STEPS))
    fast_rate = jnp.exp(jax.random.uniform(random_key_list[1], (half,), jnp.float32, math.log(0.3), math.log(0.8)))
    paired_rate_value = jnp.where(slow, slow_rate, fast_rate)
    sudden_jump = jax.random.uniform(random_key_list[2], (TOTAL_TIME_STEPS, 1), jnp.float32) < 3.0 / TOTAL_TIME_STEPS
    discarded_items = jax.random.uniform(random_key_list[3], (TOTAL_TIME_STEPS, 1), jnp.float32, 0.7, 0.9)
    rate_values = paired_rate_value[None, :] * jnp.where(sudden_jump, discarded_items, 1.0)
    angles = jax.random.uniform(random_key_list[4], (TOTAL_TIME_STEPS, half), jnp.float32, -math.pi, math.pi)
    cosine = jnp.tile(rate_values * jnp.cos(angles), (1, 2))[:, :, None]
    sine = jnp.tile(rate_values * jnp.sin(angles), (1, 2))[:, :, None]
    rows = lax.broadcasted_iota(jnp.int32, (NODES, NODES), 0)
    cols = lax.broadcasted_iota(jnp.int32, (NODES, NODES), 1)
    same_pair = (rows % half == cols % half)[None]
    on_diag = (rows == cols)[None]
    upper_row = (rows < half)[None]
    rotation = jnp.where(on_diag, cosine, jnp.where(same_pair, jnp.where(upper_row, -sine, sine), 0.0))
    noise = jax.random.normal(random_key_list[5], (TOTAL_TIME_STEPS, NODES, NODES), jnp.float32) * (0.08 / math.sqrt(NODES))
    return (rotation + noise).astype(jnp.bfloat16)


def draw_arrow_cov(key, part):
    base = jax.random.fold_in(key, 37)
    first, second = jax.random.split(base, 2)
    levels = jax.random.uniform(first, (FIXED_EFFECTS,), jnp.float32, 1.0, 2.0)
    noise = jax.random.normal(second, (FIXED_EFFECTS, FIXED_EFFECTS), jnp.float32) * 0.05
    ident = (lax.broadcasted_iota(jnp.int32, (FIXED_EFFECTS, FIXED_EFFECTS), 0) == lax.broadcasted_iota(jnp.int32, (FIXED_EFFECTS, FIXED_EFFECTS), 1)).astype(jnp.float32)
    return ident * levels[None, :] + noise + noise.T


def level_of(stream_key, shape, pieces, least, top_value):
    def one(position, shards_of):
        draws = jax.random.uniform(jax.random.fold_in(jax.random.fold_in(stream_key, 6), position), (shards_of,), jnp.float32, least / len(pieces), top_value / len(pieces))
        return jnp.repeat(jnp.exp(draws), shape[position] // shards_of).reshape((-1,) + (1,) * (len(shape) - position - 1))

    gain = one(*pieces[0])
    for cut in pieces[1:]:
        gain = gain * one(*cut)
    return gain


def bell_draw(own_key, extent, deviation, limit, cuts=(), dtype=jnp.bfloat16):
    result = jax.random.normal(own_key, extent, jnp.float32) * deviation
    if len(cuts) > 0:
        result = level_of(own_key, extent, cuts, -0.22, 0.18) * result
    return jnp.clip(result, min=-limit, max=limit).astype(dtype)


def setup_inputs(seed: int = 0, part: int = 0) -> dict:
    key_of = jax.random.split(jax.random.key(seed), 5)
    own_keys = jax.random.split(jax.random.fold_in(key_of[4], part), 5)
    return {
        "diagonal_block_inverse": draw_diagonal_block_inverse(jax.random.fold_in(jax.random.fold_in(key_of[4], part), 71), part),
        "step_map": draw_step_map(jax.random.fold_in(jax.random.fold_in(key_of[4], part), 71), part),
        "arrow_map": bell_draw(own_keys[2], (TOTAL_TIME_STEPS, FIXED_EFFECTS, NODES), 0.03, 0.1796875, ((0, 8), (2, 2))),
        "arrow_cov": draw_arrow_cov(jax.random.fold_in(jax.random.fold_in(key_of[4], part), 71), part),
    }


def product(left, right):
    return jnp.dot(left.astype(jnp.bfloat16), right.astype(jnp.bfloat16), preferred_element_type=jnp.float32)


def reference(diagonal_block_inverse, step_map, arrow_map, arrow_cov):
    def advance(carry, inputs):
        current, cross = carry
        diag_block, coupling, arrow_rows = inputs
        lower = product(cross, coupling) + product(arrow_cov, arrow_rows)
        upper = product(current, coupling) + product(cross.T, arrow_rows)
        fresh = diag_block + product(coupling.T, upper) + product(arrow_rows.T, lower)
        return (fresh, -lower), (fresh, -lower)

    start = (jnp.zeros((NODES, NODES), jnp.float32), jnp.zeros((FIXED_EFFECTS, NODES), jnp.float32))
    final, output_results = lax.scan(advance, start, (diagonal_block_inverse, step_map, arrow_map), reverse=True)
    return output_results[0], output_results[1]
```

```python
import jax
import jax.numpy as jnp
from jax import lax
from jax.experimental import pallas as pl
from jax.experimental.pallas import tpu as pltpu
from jax.sharding import PartitionSpec as P

MESH = pl.DeviceIdType.MESH
F32 = jnp.float32
BF16 = jnp.bfloat16
SEMS = 96


def mm(left, right):
    return jnp.dot(left, right, preferred_element_type=F32)


def mt(left, right):
    return lax.dot_general(left, right, (((0,), (0,)), ((), ())), preferred_element_type=F32)


class Slots:
    def __init__(self):
        self.found = {}
        self.used = 0

    def __call__(self, name, width=1):
        if name not in self.found:
            self.found[name] = self.used
            self.used += width
            assert self.used <= SEMS
        return self.found[name]


def kernel(
    d_hbm, g_hbm, h_hbm, a_hbm, out_ref, cross_ref,
    d_ref, h_ref, a_ref, g0f, g1f, dh1f, gk, t0, t1, m0, m1, xm0, xm1, pm0, pm1,
    zs, zy, zr, zc, gc, full, kb,
    send, recv, load,
):
    rows = g0f.shape[1]
    wide = g0f.shape[2]
    tall = gk.shape[1]
    half = wide // 2
    early = 3 * half
    edge_rows = tall - rows
    tm = lax.axis_index("tm")
    c = lax.axis_index("col")
    o = 1 - c
    quads = lax.axis_size("tm") // 4
    q = tm // 4
    i = tm % 4
    top = q == quads - 1
    inner = jnp.logical_not(top)
    passes = q > 0
    near = c == 1
    i0, i1, i2, i3 = (i == n for n in range(4))
    mate = {"col": o}
    sends, recvs = Slots(), Slots()

    def at(step):
        return {"tm": tm + step, "col": 1}

    def copy(src, dst, sem, sem_there, device):
        return pltpu.make_async_remote_copy(
            src_ref=src, dst_ref=dst, send_sem=send.at[sem], recv_sem=recv.at[sem_there],
            device_id=device, device_id_type=MESH,
        )

    loads = [
        pltpu.make_async_copy(d_hbm.at[1], d_ref.at[1], load.at[0]),
        pltpu.make_async_copy(h_hbm, h_ref, load.at[1]),
        pltpu.make_async_copy(g_hbm.at[0], g0f.at[c], load.at[2]),
        pltpu.make_async_copy(g_hbm.at[1], g1f.at[c], load.at[3]),
        pltpu.make_async_copy(d_hbm.at[0], d_ref.at[0], load.at[4]),
        pltpu.make_async_copy(a_hbm, a_ref, load.at[5]),
    ]
    for one in loads:
        one.start()

    barrier = pltpu.get_barrier_semaphore()
    pl.semaphore_signal(barrier, inc=1, device_id=mate, device_id_type=MESH)

    def greet(when, steps):
        @pl.when(near & when)
        def _():
            for step in steps:
                for core in range(2):
                    pl.semaphore_signal(
                        barrier, inc=1, device_id={"tm": tm + step, "col": core}, device_id_type=MESH
                    )

    greet(i0, (1, 2))
    greet(i0 & inner, (3, 4))
    greet(i1, (-1,))
    greet(i1 & inner, (2,))
    greet(i1 & top, (1,))
    greet(i2, (1,))
    greet(i2 & inner, (2,))
    greet(i3 & inner, (2,))

    def one_if(flag):
        return jnp.where(flag, 1, 0)

    targets = (
        1 + 2 * one_if(i3 & inner) + one_if(i2 & top) + one_if(i1 & passes) + 2 * one_if(i0 & passes)
    )

    loads[0].wait()
    loads[1].wait()
    dh1f[c, :rows] = d_ref[1].astype(BF16)
    dh1f[c, rows:] = h_ref[1]
    pl.semaphore_wait(barrier, 1 + targets)

    def swap(name, src, dst):
        return copy(src, dst, sends(name), recvs(name), mate)

    first = [
        swap("dh1", dh1f.at[c], dh1f.at[c]),
        swap("g0", g_hbm.at[0], g0f.at[c]),
        swap("g1", g_hbm.at[1], g1f.at[c]),
    ]
    for one in first:
        one.start()
    for one in loads[2:]:
        one.wait()
    first[0].wait_recv()

    def times(left, span, right):
        return mm(jnp.concatenate([left[0, span], left[1, span]], axis=1), right)

    body = pl.ds(0, rows)
    whole = pl.ds(0, tall)
    mine = pl.ds(pl.multiple_of(c * wide, wide), wide)
    other = pl.ds(pl.multiple_of(o * wide, wide), wide)
    first_rows = early + 2 * edge_rows
    top_span = pl.ds(0, first_rows)
    low_span = pl.ds(first_rows, zs.shape[0] - first_rows)
    spans = (top_span, low_span)

    def pack_first(p, edge):
        r = pl.multiple_of(c * wide, wide)
        zs[:half] = p[pl.ds(r, half), :half].astype(BF16)
        zs[half : 2 * half] = p[pl.ds(r + half, half), half:].astype(BF16)
        zs[2 * half : early] = p[pl.ds(r, half), half:].astype(BF16)
        zs[early : early + edge_rows] = edge[:, :half].astype(BF16)
        zs[early + edge_rows : first_rows] = edge[:, half:].astype(BF16)

    def pack_second(p):
        @pl.when(c == 0)
        def _():
            zs[first_rows : first_rows + half] = p[wide : wide + half, :half].astype(BF16)
            zs[first_rows + half :] = p[wide + half :, :half].astype(BF16)

        @pl.when(c == 1)
        def _():
            zs[first_rows : first_rows + half] = p[half:wide, :half].astype(BF16)
            zs[first_rows + half :] = p[half:wide, half:].astype(BF16)

    def unpack_first(z):
        for j in range(2):
            base = j * wide
            lo = pl.ds(base, half)
            hi = pl.ds(base + half, half)
            full[lo, lo] = z[j, :half]
            full[hi, hi] = z[j, half : 2 * half]
            side = z[j, 2 * half : early]
            full[lo, hi] = side
            full[hi, lo] = side.T
            for n in range(2):
                full[rows:, pl.ds(base + n * half, half)] = z[
                    j, early + n * edge_rows : early + (n + 1) * edge_rows
                ]

    def unpack_second(z):
        for j in range(2):
            close = pl.ds(j * half, half)
            for n in range(2):
                outer = z[j, first_rows + n * half : first_rows + (n + 1) * half]
                far = pl.ds(wide + n * half, half)
                if j == 0:
                    full[far, close] = outer
                    full[close, far] = outer.T
                else:
                    full[close, far] = outer
                    full[far, close] = outer.T

    pending = []

    def emit_copies(when, copies):
        @pl.when(when)
        def _():
            for one in copies:
                one.start()

        pending.append((when, copies))

    def packed_to(name, n, buffer, there, step):
        return copy(
            zs.at[spans[n]], buffer.at[c, spans[n]],
            sends((name, "out", step, n)), recvs((there, n), 2) + c, at(step),
        )

    def map_to(slot, step):
        return copy(
            gk.at[c, body], gc.at[slot, c],
            sends(("map", step)), recvs(("map", slot), 2) + c, at(step),
        )

    own0 = g0f[c]
    w = times(dh1f, whole, own0)
    wb = w[:rows].astype(BF16)
    kappa = w[rows:] - h_ref[0].astype(F32)
    pm0[mine] = d_ref[0, mine] + mt(g0f[c], wb)

    raw_targets = (
        (i3 & inner, 2, (-1, -2, -3)),
        (i2 & inner, 1, (-2,)),
        (i1, 0, (-1,)),
    )

    def start_raw(n):
        emit_copies(i3 & top, [packed_to("y", n, zy, "y", -1)])
        for when, slot, steps in raw_targets:
            emit_copies(
                when, [packed_to("raw", n, zc.at[slot], ("raw", slot), step) for step in steps]
            )

    pack_first(pm0, kappa)
    start_raw(0)
    first[1].wait_recv()
    pm0[other] = d_ref[0, other] + mt(g0f[o], wb)
    pack_second(pm0)
    start_raw(1)

    first[2].wait_recv()
    gk[c, :rows] = times(g1f, body, own0).astype(BF16)
    gk[c, rows:] = kappa.astype(BF16)
    for when, slot, steps in raw_targets:
        emit_copies(when, [map_to(slot, step) for step in steps])

    join = swap("gk", gk.at[c], gk.at[c])
    join.start()
    pm1[...] = d_ref[1]
    join.wait_recv()
    m0[...] = gk[...]
    m1[:, :rows] = g1f[...]
    m1[:, rows:] = -dh1f[:, rows:]

    def turn():
        for j in range(2):
            span = pl.ds(j * wide, wide)
            t0[span, :] = m0[j, :rows].T
            t1[span, :] = m1[j, :rows].T

    turn()

    def take(when, name, src, relay=None, relay_when=None):
        arrivals, onward, handed = [], [], []
        for h in range(2):
            ref = src(h)
            number = recvs(name, 2) + h
            arrivals.append(copy(ref, ref, sends("none"), number, mate))
            onward.append(copy(ref, ref, sends((name, "mate"), 2) + h, recvs((name, "mate"), 2) + h, mate))
            if relay is not None:
                step, dst, there = relay
                handed.append(
                    copy(ref, dst(h), sends((name, "relay"), 2) + h, recvs(there, 2) + h, at(step))
                )

        @pl.when(when & near)
        def _():
            for h in range(2):
                arrivals[h].wait_recv()
                onward[h].start()
                if relay is not None:

                    @pl.when(relay_when)
                    def _():
                        handed[h].start()

        @pl.when(when & (c == 0))
        def _():
            for h in range(2):
                onward[h].wait_recv()

        pending.append((when & near, onward))
        if relay is not None:
            pending.append((when & near & relay_when, handed))

    def take_raw(when, slot, relay=None):
        for n in range(2):
            go = None
            if relay is not None:
                go = (relay[0], lambda h, n=n: zc.at[slot, h, spans[n]], (("raw", slot), n))
            take(
                when, (("raw", slot), n), lambda h, n=n: zc.at[slot, h, spans[n]], go,
                None if relay is None else relay[1],
            )
        go = None
        if relay is not None:
            go = (relay[0], lambda h: gc.at[slot, h], ("map", slot))
        take(when, ("map", slot), lambda h: gc.at[slot, h], go, None if relay is None else relay[1])

    def absorb(slot):
        unpack_first(zc.at[slot])
        unpack_second(zc.at[slot])
        new = [swap(("m0", slot), xm0.at[slot, c], xm0.at[slot, c]),
               swap(("m1", slot), xm1.at[slot, c], xm1.at[slot, c])]
        for n, (m, x, t, p, sign) in enumerate(((m0, xm0, t0, pm0, 1.0), (m1, xm1, t1, pm1, -1.0))):
            own = m[c, :rows]
            w = mm(full[...], own)
            x[slot, c, rows:] = (m[c, rows:].astype(F32) + sign * w[rows:]).astype(BF16)
            x[slot, c, :rows] = times(gc.at[slot], body, own).astype(BF16)
            new[n].start()
            wb = w[:rows].astype(BF16)
            for j in range(2):
                span = pl.ds(j * wide, wide)
                p[span] += mm(t[span, :], wb)
        for one in new:
            one.wait_recv()
        m0[...] = xm0[slot]
        m1[...] = xm1[slot]
        turn()
        return new

    uses = (i0, inner & (i0 | i1), inner & jnp.logical_not(i3))
    take_raw(uses[0], 0)
    take_raw(uses[1], 1, (1, i0))
    for slot in range(3):
        if slot == 2:
            take_raw(uses[2], 2)

        @pl.when(uses[slot])
        def _():
            for one in absorb(slot):
                one.wait_send()

    started = jnp.logical_not(i3 & top)
    cov = a_ref[...].astype(BF16)

    def take_y(n):
        take(
            started, ("y", n), lambda h: zy.at[h, spans[n]],
            (1, lambda h: zy.at[h, spans[n]], ("y", n)), i0 & inner,
        )

    def edges(step, sign, m):
        for j in range(2):
            kb[step, j] = sign * mm(full[rows:], m[j, :rows]) + m[j, rows:].astype(F32)

    @pl.when(jnp.logical_not(started))
    def _():
        full[...] = jnp.zeros_like(full)

    take_y(0)

    @pl.when(started)
    def _():
        unpack_first(zy)

    edges(0, 1.0, m0)
    edges(1, -1.0, m1)
    for step in range(2):
        cross_ref[step] = mm(cov, kb[step, c].astype(BF16))

    take_y(1)

    @pl.when(started)
    def _():
        unpack_second(zy)

    def state(m):
        return mm(full[:rows], m[c, :rows]).astype(BF16)

    def emit(step, p):
        edge = cross_ref[step].astype(BF16)
        for j in range(2):
            span = pl.ds(j * wide, wide)
            out_ref[step, span] = p[span] + mt(kb[step, j].astype(BF16), edge)

    leads = i0 & passes
    heads = i2 & top

    def start_y(n):
        emit_copies(heads, [packed_to("y", n, zy, "y", -2)])
        emit_copies(leads, [packed_to("y", n, zy, "y", -4), packed_to("y", n, zr, "r", 1)])

    w = state(m0)
    pm0[mine] += mm(t0[mine, :], w)

    @pl.when(leads | heads)
    def _():
        pack_first(pm0, kb[0, c])

    start_y(0)
    pm0[other] += mm(t0[other, :], w)

    @pl.when(leads | heads)
    def _():
        pack_second(pm0)

    start_y(1)
    emit_copies(heads, [packed_to("y2", n, zy, "y", -1) for n in range(2)])
    emit_copies(leads, [packed_to("y2", n, zy, "y", -2) for n in range(2)])

    emit(0, pm0)
    w = state(m1)
    for j in range(2):
        span = pl.ds(j * wide, wide)
        pm1[span] += mm(t1[span, :], w)
    emit(1, pm1)

    for n in range(2):
        ins, outs = [], []
        for h in range(2):
            ref = zr.at[h, spans[n]]
            ins.append(copy(ref, ref, sends("none"), recvs(("r", n), 2) + h, mate))
            outs.append(
                copy(ref, zy.at[h, spans[n]], sends(("r", "out", n), 2) + h, recvs(("y", n), 2) + h, at(-2))
            )

        @pl.when(i1 & passes & near)
        def _():
            for h in range(2):
                ins[h].wait_recv()
                outs[h].start()

        pending.append((i1 & passes & near, outs))

    for one in first:
        one.wait_send()
    join.wait_send()
    for when, copies in pending:

        @pl.when(when)
        def _():
            for one in copies:
                one.wait_send()


def shards(diagonal_block_inverse, step_map, arrow_map, arrow_cov):
    count, nodes, wide = diagonal_block_inverse.shape
    effects = arrow_map.shape[1]
    tall = nodes + effects
    packed = 5 * (wide // 2) + 2 * effects
    vmem = pl.BlockSpec(memory_space=pltpu.VMEM)
    return pl.pallas_call(
        kernel,
        out_shape=(
            jax.ShapeDtypeStruct((count, nodes, wide), F32),
            jax.ShapeDtypeStruct((count, effects, wide), F32),
        ),
        in_specs=[pl.BlockSpec(memory_space=pltpu.HBM)] * 4,
        out_specs=(vmem, vmem),
        scratch_shapes=[
            pltpu.VMEM((count, nodes, wide), F32),
            pltpu.VMEM((count, effects, wide), BF16),
            pltpu.VMEM((effects, effects), F32),
            pltpu.VMEM((2, nodes, wide), BF16),
            pltpu.VMEM((2, nodes, wide), BF16),
            pltpu.VMEM((2, tall, wide), BF16),
            pltpu.VMEM((2, tall, wide), BF16),
            pltpu.VMEM((nodes, nodes), BF16),
            pltpu.VMEM((nodes, nodes), BF16),
            pltpu.VMEM((2, tall, wide), BF16),
            pltpu.VMEM((2, tall, wide), BF16),
            pltpu.VMEM((3, 2, tall, wide), BF16),
            pltpu.VMEM((3, 2, tall, wide), BF16),
            pltpu.VMEM((nodes, wide), F32),
            pltpu.VMEM((nodes, wide), F32),
            pltpu.VMEM((packed, wide // 2), BF16),
            pltpu.VMEM((2, packed, wide // 2), BF16),
            pltpu.VMEM((2, packed, wide // 2), BF16),
            pltpu.VMEM((3, 2, packed, wide // 2), BF16),
            pltpu.VMEM((3, 2, nodes, wide), BF16),
            pltpu.VMEM((tall, nodes), BF16),
            pltpu.VMEM((count, 2, effects, wide), F32),
            pltpu.SemaphoreType.DMA((SEMS,)),
            pltpu.SemaphoreType.DMA((SEMS,)),
            pltpu.SemaphoreType.DMA((6,)),
        ],
        compiler_params=pltpu.CompilerParams(
            collective_id=0, has_side_effects=True, vmem_limit_bytes=63 * 1024 * 1024
        ),
    )(diagonal_block_inverse, step_map, arrow_map, arrow_cov)


def solution(mesh):
    return jax.shard_map(
        shards,
        mesh=mesh,
        in_specs=(
            P(("rep", "tm"), None, "col"),
            P(("rep", "tm"), None, "col"),
            P(("rep", "tm"), None, "col"),
            P("rep", None),
        ),
        out_specs=(P(("rep", "tm"), None, "col"), P(("rep", "tm"), None, "col")),
        check_vma=False,
    )
```

```python
import jax
import jax.numpy as jnp
from jax import lax
from jax.experimental import pallas as pl
from jax.experimental.pallas import tpu as pltpu
from jax.sharding import PartitionSpec as P

MESH = pl.DeviceIdType.MESH
F32 = jnp.float32
BF16 = jnp.bfloat16
SEMS = 96


def mm(left, right):
    return jnp.dot(left, right, preferred_element_type=F32)


def mt(left, right):
    return lax.dot_general(left, right, (((0,), (0,)), ((), ())), preferred_element_type=F32)


class Slots:
    def __init__(self):
        self.found = {}
        self.used = 0

    def __call__(self, name, width=1):
        if name not in self.found:
            self.found[name] = self.used
            self.used += width
            assert self.used <= SEMS
        return self.found[name]


def kernel(
    d_hbm, g_hbm, h_hbm, a_hbm,
    full, m1, t1, pm0, pm1, kb, cross_ref,
    d_ref, h_ref, a_ref, g0f, g1f, dh1f, gk, t0, m0, xm0, xm1,
    zs, zy, zr, zc, gc,
    send, recv, load,
):
    rows = g0f.shape[1]
    wide = g0f.shape[2]
    tall = gk.shape[1]
    half = wide // 2
    early = 3 * half
    edge_rows = tall - rows
    tm = lax.axis_index("tm")
    c = lax.axis_index("col")
    o = 1 - c
    quads = lax.axis_size("tm") // 4
    q = tm // 4
    i = tm % 4
    top = q == quads - 1
    inner = jnp.logical_not(top)
    passes = q > 0
    near = c == 1
    i0, i1, i2, i3 = (i == n for n in range(4))
    mate = {"col": o}
    sends, recvs = Slots(), Slots()

    def at(step):
        return {"tm": tm + step, "col": 1}

    def copy(src, dst, sem, sem_there, device):
        return pltpu.make_async_remote_copy(
            src_ref=src, dst_ref=dst, send_sem=send.at[sem], recv_sem=recv.at[sem_there],
            device_id=device, device_id_type=MESH,
        )

    loads = [
        pltpu.make_async_copy(d_hbm.at[1], d_ref.at[1], load.at[0]),
        pltpu.make_async_copy(h_hbm, h_ref, load.at[1]),
        pltpu.make_async_copy(g_hbm.at[0], g0f.at[c], load.at[2]),
        pltpu.make_async_copy(g_hbm.at[1], g1f.at[c], load.at[3]),
        pltpu.make_async_copy(d_hbm.at[0], d_ref.at[0], load.at[4]),
        pltpu.make_async_copy(a_hbm, a_ref, load.at[5]),
    ]
    for one in loads:
        one.start()

    barrier = pltpu.get_barrier_semaphore()
    pl.semaphore_signal(barrier, inc=1, device_id=mate, device_id_type=MESH)

    def greet(when, steps):
        @pl.when(near & when)
        def _():
            for step in steps:
                for core in range(2):
                    pl.semaphore_signal(
                        barrier, inc=1, device_id={"tm": tm + step, "col": core}, device_id_type=MESH
                    )

    greet(i0, (1, 2))
    greet(i0 & inner, (3, 4))
    greet(i1, (-1,))
    greet(i1 & inner, (2,))
    greet(i1 & top, (1,))
    greet(i2, (1,))
    greet(i2 & inner, (2,))
    greet(i3 & inner, (2,))

    def one_if(flag):
        return jnp.where(flag, 1, 0)

    targets = (
        1 + 2 * one_if(i3 & inner) + one_if(i2 & top) + one_if(i1 & passes) + 2 * one_if(i0 & passes)
    )

    loads[0].wait()
    loads[1].wait()
    dh1f[c, :rows] = d_ref[1].astype(BF16)
    dh1f[c, rows:] = h_ref[1]
    pl.semaphore_wait(barrier, 1 + targets)

    def swap(name, src, dst):
        return copy(src, dst, sends(name), recvs(name), mate)

    first = [
        swap("dh1", dh1f.at[c], dh1f.at[c]),
        swap("g0", g_hbm.at[0], g0f.at[c]),
        swap("g1", g_hbm.at[1], g1f.at[c]),
    ]
    for one in first:
        one.start()
    for one in loads[2:]:
        one.wait()
    first[0].wait_recv()

    def times(left, span, right):
        return mm(jnp.concatenate([left[0, span], left[1, span]], axis=1), right)

    body = pl.ds(0, rows)
    whole = pl.ds(0, tall)
    mine = pl.ds(pl.multiple_of(c * wide, wide), wide)
    other = pl.ds(pl.multiple_of(o * wide, wide), wide)
    first_rows = early + 2 * edge_rows
    top_span = pl.ds(0, first_rows)
    low_span = pl.ds(first_rows, zs.shape[0] - first_rows)
    spans = (top_span, low_span)

    def pack_first(p, edge):
        r = pl.multiple_of(c * wide, wide)
        zs[:half] = p[pl.ds(r, half), :half].astype(BF16)
        zs[half : 2 * half] = p[pl.ds(r + half, half), half:].astype(BF16)
        zs[2 * half : early] = p[pl.ds(r, half), half:].astype(BF16)
        zs[early : early + edge_rows] = edge[:, :half].astype(BF16)
        zs[early + edge_rows : first_rows] = edge[:, half:].astype(BF16)

    def pack_second(p):
        @pl.when(c == 0)
        def _():
            zs[first_rows : first_rows + half] = p[wide : wide + half, :half].astype(BF16)
            zs[first_rows + half :] = p[wide + half :, :half].astype(BF16)

        @pl.when(c == 1)
        def _():
            zs[first_rows : first_rows + half] = p[half:wide, :half].astype(BF16)
            zs[first_rows + half :] = p[half:wide, half:].astype(BF16)

    def unpack_first(z):
        for j in range(2):
            base = j * wide
            lo = pl.ds(base, half)
            hi = pl.ds(base + half, half)
            full[lo, lo] = z[j, :half]
            full[hi, hi] = z[j, half : 2 * half]
            side = z[j, 2 * half : early]
            full[lo, hi] = side
            full[hi, lo] = side.T
            for n in range(2):
                full[rows:, pl.ds(base + n * half, half)] = z[
                    j, early + n * edge_rows : early + (n + 1) * edge_rows
                ]

    def unpack_second(z):
        for j in range(2):
            close = pl.ds(j * half, half)
            for n in range(2):
                outer = z[j, first_rows + n * half : first_rows + (n + 1) * half]
                far = pl.ds(wide + n * half, half)
                if j == 0:
                    full[far, close] = outer
                    full[close, far] = outer.T
                else:
                    full[close, far] = outer
                    full[far, close] = outer.T

    pending = []

    def emit_copies(when, copies):
        @pl.when(when)
        def _():
            for one in copies:
                one.start()

        pending.append((when, copies))

    def packed_to(name, n, buffer, there, step):
        return copy(
            zs.at[spans[n]], buffer.at[c, spans[n]],
            sends((name, "out", step, n)), recvs((there, n), 2) + c, at(step),
        )

    parts = (pl.ds(0, wide), pl.ds(wide, wide))

    def map_to(slot, step):
        return [
            copy(
                gk.at[c, parts[n]], gc.at[slot, c, parts[n]],
                sends(("map", step, n)), recvs((("map", slot), n), 2) + c, at(step),
            )
            for n in range(2)
        ]

    own0 = g0f[c]
    w = times(dh1f, whole, own0)
    wb = w[:rows].astype(BF16)
    kappa = w[rows:] - h_ref[0].astype(F32)
    pm0[mine] = d_ref[0, mine] + mt(g0f[c], wb)

    raw_targets = (
        (i3 & inner, 2, (-1, -2)),
        (i2 & inner, 1, (-2,)),
        (i1, 0, (-1,)),
    )

    def start_raw(n):
        for when, slot, steps in raw_targets:
            emit_copies(
                when, [packed_to("raw", n, zc.at[slot], ("raw", slot), step) for step in steps]
            )

    pack_first(pm0, kappa)
    emit_copies(i3 & top, [packed_to("y", 0, zy, "y", -1)])
    start_raw(0)
    first[1].wait_recv()
    pm0[other] = d_ref[0, other] + mt(g0f[o], wb)
    pack_second(pm0)
    emit_copies(i3 & top, [packed_to("y", 1, zy, "y", -1)])

    first[2].wait_recv()
    gk[c, :rows] = times(g1f, body, own0).astype(BF16)
    gk[c, rows:] = kappa.astype(BF16)
    ahead_of_late = map_to(2, -2)
    late = map_to(2, -3)
    emit_copies(i3 & inner, map_to(2, -1))
    emit_copies(i2 & inner, map_to(1, -2))
    emit_copies(i1, map_to(0, -1))

    @pl.when(i3 & inner)
    def _():
        for one in ahead_of_late:
            one.start()

    start_raw(1)

    join = swap("gk", gk.at[c], gk.at[c])
    join.start()
    pm1[...] = d_ref[1]
    join.wait_recv()
    m0[...] = gk[...]
    m1[:, :rows] = g1f[...]
    m1[:, rows:] = -dh1f[:, rows:]

    def turn():
        for j in range(2):
            span = pl.ds(j * wide, wide)
            t0[span, :] = m0[j, :rows].T
            t1[span, :] = m1[j, :rows].T

    turn()

    def take(when, name, src, relay=None, relay_when=None):
        arrivals, onward, handed = [], [], []
        for h in range(2):
            ref = src(h)
            number = recvs(name, 2) + h
            arrivals.append(copy(ref, ref, sends("none"), number, mate))
            onward.append(copy(ref, ref, sends((name, "mate"), 2) + h, recvs((name, "mate"), 2) + h, mate))
            if relay is not None:
                handed.append(copy(ref, ref, sends((name, "relay"), 2) + h, number, at(relay)))

        @pl.when(when & near)
        def _():
            for h in range(2):
                arrivals[h].wait_recv()
                onward[h].start()
                if relay is not None:

                    @pl.when(relay_when)
                    def _():
                        handed[h].start()

        @pl.when(when & (c == 0))
        def _():
            for h in range(2):
                onward[h].wait_recv()

        pending.append((when & near, onward))
        if relay is not None:
            pending.append((when & near & relay_when, handed))

    uses = (i0, inner & (i0 | i1), inner & jnp.logical_not(i3))
    relays = ((None, None), (1, i0), (-2, i2))

    def take_block(slot, n):
        take(
            uses[slot], (("raw", slot), n), lambda h: zc.at[slot, h, spans[n]],
            relays[slot][0], relays[slot][1],
        )

    def take_map(slot):
        relay = relays[slot] if slot == 1 else (None, None)
        for n in range(2):
            take(uses[slot], (("map", slot), n), lambda h: gc.at[slot, h, parts[n]], relay[0], relay[1])

    def swaps(slot):
        return [
            swap(("m0", slot), xm0.at[slot, c], xm0.at[slot, c]),
            swap(("m1", slot), xm1.at[slot, c], xm1.at[slot, c]),
        ]

    def compose(slot):
        @pl.when(uses[slot])
        def _():
            unpack_first(zc.at[slot])
            for one, m, x, sign in zip(swaps(slot), (m0, m1), (xm0, xm1), (1.0, -1.0)):
                own = m[c, :rows]
                edge = mm(full[rows:], own)
                x[slot, c, rows:] = (m[c, rows:].astype(F32) + sign * edge).astype(BF16)
                x[slot, c, :rows] = times(gc.at[slot], body, own).astype(BF16)
                one.start()

    def absorb(slot):
        @pl.when(uses[slot])
        def _():
            unpack_second(zc.at[slot])
            for one, m, x, t, p in zip(swaps(slot), (m0, m1), (xm0, xm1), (t0, t1), (pm0, pm1)):
                wb = mm(full[:rows], m[c, :rows]).astype(BF16)
                for j in range(2):
                    span = pl.ds(j * wide, wide)
                    p[span] += mm(t[span, :], wb)
                one.wait_recv()
                m[...] = x[slot]
                for j in range(2):
                    t[pl.ds(j * wide, wide), :] = m[j, :rows].T
            for one in swaps(slot):
                one.wait_send()

    take_block(0, 0)
    take_block(1, 0)
    take_map(0)
    take_map(1)
    compose(0)
    take_block(0, 1)
    take_block(1, 1)
    absorb(0)
    compose(1)
    absorb(1)
    take_block(2, 0)
    take_block(2, 1)
    take_map(2)
    compose(2)
    absorb(2)

    @pl.when(i3 & inner)
    def _():
        for one in ahead_of_late:
            one.wait_send()
        for one in late:
            one.start()

    pending.append((i3 & inner, late))

    started = jnp.logical_not(i3 & top)
    cov = a_ref[...].astype(BF16)

    def take_y(n):
        take(
            started, ("y", n), lambda h: zy.at[h, spans[n]], 1, i0 & inner,
        )

    def edges(step, sign, m):
        for j in range(2):
            kb[step, j] = sign * mm(full[rows:], m[j, :rows]) + m[j, rows:].astype(F32)

    @pl.when(jnp.logical_not(started))
    def _():
        full[...] = jnp.zeros_like(full)

    take_y(0)

    @pl.when(started)
    def _():
        unpack_first(zy)

    edges(0, 1.0, m0)
    edges(1, -1.0, m1)
    for step in range(2):
        cross_ref[step] = mm(cov, kb[step, c].astype(BF16))

    take_y(1)

    @pl.when(started)
    def _():
        unpack_second(zy)

    def state(m):
        return mm(full[:rows], m[c, :rows]).astype(BF16)

    leads = i0 & passes
    heads = i2 & top

    def start_y(n):
        emit_copies(heads, [packed_to("y", n, zy, "y", -2)])
        emit_copies(leads, [packed_to("y", n, zy, "y", -4), packed_to("y", n, zr, "r", 1)])

    w = state(m0)
    pm0[mine] += mm(t0[mine, :], w)

    @pl.when(leads | heads)
    def _():
        pack_first(pm0, kb[0, c])

    start_y(0)
    pm0[other] += mm(t0[other, :], w)

    @pl.when(leads | heads)
    def _():
        pack_second(pm0)

    start_y(1)
    emit_copies(heads, [packed_to("y2", n, zy, "y", -1) for n in range(2)])
    emit_copies(leads, [packed_to("y2", n, zy, "y", -2) for n in range(2)])

    for n in range(2):
        ins, outs = [], []
        for h in range(2):
            ref = zr.at[h, spans[n]]
            ins.append(copy(ref, ref, sends("none"), recvs(("r", n), 2) + h, mate))
            outs.append(
                copy(ref, zy.at[h, spans[n]], sends(("r", "out", n), 2) + h, recvs(("y", n), 2) + h, at(-2))
            )

        @pl.when(i1 & passes & near)
        def _():
            for h in range(2):
                ins[h].wait_recv()
                outs[h].start()

        pending.append((i1 & passes & near, outs))

    for one in first:
        one.wait_send()
    join.wait_send()
    for when, copies in pending:

        @pl.when(when)
        def _():
            for one in copies:
                one.wait_send()


def finish(full, m1, t1, pm0, pm1, kb, cross_ref, out_hbm, cross_hbm, out, store):
    rows, wide = out.shape[1], out.shape[2]
    c = lax.axis_index("col")
    ends = pltpu.make_async_copy(cross_ref, cross_hbm, store.at[4])
    ends.start()
    stores = []

    def emit(step, j, value):
        span = pl.ds(j * wide, wide)
        out[step, span] = value + mt(kb[step, j].astype(BF16), cross_ref[step].astype(BF16))
        one = pltpu.make_async_copy(out.at[step, span], out_hbm.at[step, span], store.at[2 * step + j])
        one.start()
        stores.append(one)

    for j in range(2):
        emit(0, j, pm0[pl.ds(j * wide, wide)])
    w = mm(full[:rows], m1[c, :rows]).astype(BF16)
    for j in range(2):
        span = pl.ds(j * wide, wide)
        emit(1, j, pm1[span] + mm(t1[span, :], w))
    ends.wait()
    for one in stores:
        one.wait()


def shards(diagonal_block_inverse, step_map, arrow_map, arrow_cov):
    count, nodes, wide = diagonal_block_inverse.shape
    effects = arrow_map.shape[1]
    tall = nodes + effects
    packed = 5 * (wide // 2) + 2 * effects
    vmem = pl.BlockSpec(memory_space=pltpu.VMEM)
    hbm = pl.BlockSpec(memory_space=pltpu.HBM)
    held = pl.pallas_call(
        kernel,
        out_shape=(
            jax.ShapeDtypeStruct((tall, nodes), BF16),
            jax.ShapeDtypeStruct((2, tall, wide), BF16),
            jax.ShapeDtypeStruct((nodes, nodes), BF16),
            jax.ShapeDtypeStruct((nodes, wide), F32),
            jax.ShapeDtypeStruct((nodes, wide), F32),
            jax.ShapeDtypeStruct((count, 2, effects, wide), F32),
            jax.ShapeDtypeStruct((count, effects, wide), F32),
        ),
        in_specs=[hbm] * 4,
        out_specs=(vmem,) * 7,
        scratch_shapes=[
            pltpu.VMEM((count, nodes, wide), F32),
            pltpu.VMEM((count, effects, wide), BF16),
            pltpu.VMEM((effects, effects), F32),
            pltpu.VMEM((2, nodes, wide), BF16),
            pltpu.VMEM((2, nodes, wide), BF16),
            pltpu.VMEM((2, tall, wide), BF16),
            pltpu.VMEM((2, tall, wide), BF16),
            pltpu.VMEM((nodes, nodes), BF16),
            pltpu.VMEM((2, tall, wide), BF16),
            pltpu.VMEM((3, 2, tall, wide), BF16),
            pltpu.VMEM((3, 2, tall, wide), BF16),
            pltpu.VMEM((packed, wide // 2), BF16),
            pltpu.VMEM((2, packed, wide // 2), BF16),
            pltpu.VMEM((2, packed, wide // 2), BF16),
            pltpu.VMEM((3, 2, packed, wide // 2), BF16),
            pltpu.VMEM((3, 2, nodes, wide), BF16),
            pltpu.SemaphoreType.DMA((SEMS,)),
            pltpu.SemaphoreType.DMA((SEMS,)),
            pltpu.SemaphoreType.DMA((6,)),
        ],
        compiler_params=pltpu.CompilerParams(
            collective_id=0, has_side_effects=True, vmem_limit_bytes=28 * 1024 * 1024
        ),
    )(*(
        pltpu.with_memory_space_constraint(array, pltpu.HBM)
        for array in (diagonal_block_inverse, step_map, arrow_map, arrow_cov)
    ))
    return pl.pallas_call(
        finish,
        out_shape=(
            jax.ShapeDtypeStruct((count, nodes, wide), F32),
            jax.ShapeDtypeStruct((count, effects, wide), F32),
        ),
        in_specs=[vmem] * 7,
        out_specs=(hbm, hbm),
        scratch_shapes=[
            pltpu.VMEM((count, nodes, wide), F32),
            pltpu.SemaphoreType.DMA((5,)),
        ],
        compiler_params=pltpu.CompilerParams(vmem_limit_bytes=28 * 1024 * 1024),
    )(*held)


def solution(mesh):
    return jax.shard_map(
        shards,
        mesh=mesh,
        in_specs=(
            P(("rep", "tm"), None, "col"),
            P(("rep", "tm"), None, "col"),
            P(("rep", "tm"), None, "col"),
            P("rep", None),
        ),
        out_specs=(P(("rep", "tm"), None, "col"), P(("rep", "tm"), None, "col")),
        check_vma=False,
    )
```

```python
import jax
import jax.numpy as jnp
from jax import lax
from jax.experimental import pallas as pl
from jax.experimental.pallas import tpu as pltpu
from jax.sharding import PartitionSpec as P

MESH = pl.DeviceIdType.MESH
F32 = jnp.float32
BF16 = jnp.bfloat16
SENDS = 28
RECVS = 40
MARK = 16


def mm(left, right):
    return jnp.dot(left, right, preferred_element_type=F32)


def mt(left, right):
    return lax.dot_general(left, right, (((0,), (0,)), ((), ())), preferred_element_type=F32)


class Slots:
    def __init__(self, start, end):
        self.found = {}
        self.free = start
        self.end = end

    def __call__(self, name, width=1):
        if name not in self.found:
            self.found[name] = self.free
            self.free += width
            assert self.free <= self.end
        return self.found[name]


def kernel(
    d_hbm, g_hbm, h_hbm, a_hbm,
    full, m1, t1, pm0, pm1, kb, cross_ref,
    d_ref, h_ref, a_ref, g0f, g1f, dh1f, gk, t0, m0, xm0, xm1,
    zs, zy, zr, zc, gc,
    send, recv, load,
):
    rows = g0f.shape[1]
    wide = g0f.shape[2]
    tall = gk.shape[1]
    half = wide // 2
    edge_rows = tall - rows
    tm = lax.axis_index("tm")
    c = lax.axis_index("col")
    o = 1 - c
    quads = lax.axis_size("tm") // 4
    q = tm // 4
    i = tm % 4
    top = q == quads - 1
    inner = jnp.logical_not(top)
    passes = q > 0
    i0, i1, i2, i3 = (i == n for n in range(4))
    mate = {"col": o}
    recvs = Slots(0, RECVS)
    sends = Slots(0, 14)
    place = [Slots(14, SENDS) for _ in range(4)]

    def at(step):
        return {"tm": tm + step}

    def copy(src, dst, sem, sem_there, device):
        return pltpu.make_async_remote_copy(
            src_ref=src, dst_ref=dst, send_sem=send.at[sem], recv_sem=recv.at[sem_there],
            device_id=device, device_id_type=MESH,
        )

    loads = [
        pltpu.make_async_copy(d_hbm.at[1], d_ref.at[1], load.at[0]),
        pltpu.make_async_copy(h_hbm, h_ref, load.at[1]),
        pltpu.make_async_copy(g_hbm.at[0], g0f.at[c], load.at[2]),
        pltpu.make_async_copy(g_hbm.at[1], g1f.at[c], load.at[3]),
        pltpu.make_async_copy(d_hbm.at[0], d_ref.at[0], load.at[4]),
        pltpu.make_async_copy(a_hbm, a_ref, load.at[5]),
    ]
    for one in loads:
        one.start()

    barrier = pltpu.get_barrier_semaphore()
    pl.semaphore_signal(barrier, inc=1, device_id=mate, device_id_type=MESH)

    def greet(when, steps):
        @pl.when(when)
        def _():
            for step in steps:
                pl.semaphore_signal(barrier, inc=1, device_id=at(step), device_id_type=MESH)

    greet(i0, (1, 2))
    greet(i0 & inner, (3, 4))
    greet(i1, (-1,))
    greet(i1 & inner, (2,))
    greet(i1 & top, (1,))
    greet(i2, (1,))
    greet(i2 & inner, (2,))
    greet(i3 & inner, (2,))

    def one_if(flag):
        return jnp.where(flag, 1, 0)

    targets = (
        1 + 2 * one_if(i3 & inner) + one_if(i2 & top) + one_if(i1 & passes) + 2 * one_if(i0 & passes)
    )

    loads[0].wait()
    loads[1].wait()
    dh1f[c, :rows] = d_ref[1].astype(BF16)
    dh1f[c, rows:] = h_ref[1]
    pl.semaphore_wait(barrier, 1 + targets)

    def swap(name, src, dst):
        return copy(src, dst, sends(name), recvs(name), mate)

    first = [
        swap("dh1", dh1f.at[c], dh1f.at[c]),
        swap("g0", g_hbm.at[0], g0f.at[c]),
        swap("g1", g_hbm.at[1], g1f.at[c]),
    ]
    for one in first:
        one.start()
    for one in loads[2:]:
        one.wait()
    first[0].wait_recv()

    def times(left, span, right):
        return mm(jnp.concatenate([left[0, span], left[1, span]], axis=1), right)

    body = pl.ds(0, rows)
    whole = pl.ds(0, tall)
    mine = pl.ds(pl.multiple_of(c * wide, wide), wide)
    other = pl.ds(pl.multiple_of(o * wide, wide), wide)
    edge_base = 2 * half
    mark_base = edge_base + 2 * edge_rows
    first_rows = mark_base + MARK
    top_span = pl.ds(0, first_rows)
    low_span = pl.ds(first_rows, zs.shape[0] - first_rows)
    spans = (top_span, low_span)
    across = lax.broadcasted_iota(jnp.int32, (half, half), 1)
    down = lax.broadcasted_iota(jnp.int32, (half, half), 0)

    def pack_first(p, edge):
        r = pl.multiple_of(c * wide, wide)
        one = p[pl.ds(r, half), :half]
        two = p[pl.ds(r + half, half), half:]
        zs[:half] = jnp.where(down >= across, one, two).astype(BF16)
        zs[half:edge_base] = p[pl.ds(r, half), half:].astype(BF16)
        zs[edge_base : edge_base + edge_rows] = edge[:, :half].astype(BF16)
        zs[edge_base + edge_rows : mark_base] = edge[:, half:].astype(BF16)
        mark = jnp.sum(jnp.where(down == across, two, 0.0), axis=0, keepdims=True)
        zs[mark_base:first_rows] = jnp.broadcast_to(mark, (MARK, half)).astype(BF16)

    def pack_second(p):
        @pl.when(c == 0)
        def _():
            zs[first_rows : first_rows + half] = p[wide : wide + half, :half].astype(BF16)
            zs[first_rows + half :] = p[wide + half :, :half].astype(BF16)

        @pl.when(c == 1)
        def _():
            zs[first_rows : first_rows + half] = p[half:wide, :half].astype(BF16)
            zs[first_rows + half :] = p[half:wide, half:].astype(BF16)

    def unpack_first(z):
        for j in range(2):
            base = j * wide
            lo = pl.ds(base, half)
            hi = pl.ds(base + half, half)
            both = z[j, :half].astype(F32)
            turned = both.T
            mark = z[j, mark_base:first_rows].astype(F32)[:1]
            full[lo, lo] = jnp.where(down >= across, both, turned).astype(BF16)
            full[hi, hi] = jnp.where(
                down < across, both, jnp.where(down == across, mark, turned)
            ).astype(BF16)
            side = z[j, half:edge_base]
            full[lo, hi] = side
            full[hi, lo] = side.T
            for n in range(2):
                full[rows:, pl.ds(base + n * half, half)] = z[
                    j, edge_base + n * edge_rows : edge_base + (n + 1) * edge_rows
                ]

    def unpack_second(z):
        for j in range(2):
            close = pl.ds(j * half, half)
            for n in range(2):
                outer = z[j, first_rows + n * half : first_rows + (n + 1) * half]
                far = pl.ds(wide + n * half, half)
                if j == 0:
                    full[far, close] = outer
                    full[close, far] = outer.T
                else:
                    full[close, far] = outer
                    full[far, close] = outer.T

    pending = []

    def emit_copies(when, copies):
        @pl.when(when)
        def _():
            for one in copies:
                one.start()

        pending.append((when, copies))

    def packed_to(where, n, buffer, there, step):
        return copy(
            zs.at[spans[n]], buffer.at[c, spans[n]],
            place[where]((there, step, n)), recvs((there, n), 1 if there == "r" else 2), at(step),
        )

    parts = (pl.ds(0, wide), pl.ds(wide, wide))

    def map_to(slot, step):
        return [
            copy(
                gk.at[c, parts[n]], gc.at[slot, c, parts[n]],
                place[slot + 1](("map", step, n)), recvs((("map", slot), n), 2), at(step),
            )
            for n in range(2)
        ]

    own0 = g0f[c]
    w = times(dh1f, whole, own0)
    wb = w[:rows].astype(BF16)
    kappa = w[rows:] - h_ref[0].astype(F32)
    pm0[mine] = d_ref[0, mine] + mt(g0f[c], wb)

    raw_targets = (
        (i3 & inner, 2, (-1, -2)),
        (i2 & inner, 1, (-2,)),
        (i1, 0, (-1,)),
    )

    def start_raw(n):
        for when, slot, steps in raw_targets:
            emit_copies(
                when, [packed_to(slot + 1, n, zc.at[slot], ("raw", slot), step) for step in steps]
            )

    pack_first(pm0, kappa)
    emit_copies(i3 & top, [packed_to(3, 0, zy, "y", -1)])
    start_raw(0)
    first[1].wait_recv()
    pm0[other] = d_ref[0, other] + mt(g0f[o], wb)
    pack_second(pm0)
    emit_copies(i3 & top, [packed_to(3, 1, zy, "y", -1)])

    first[2].wait_recv()
    gk[c, :rows] = times(g1f, body, own0).astype(BF16)
    gk[c, rows:] = kappa.astype(BF16)
    ahead_of_late = map_to(2, -2)
    late = map_to(2, -3)
    emit_copies(i3 & inner, map_to(2, -1))
    emit_copies(i2 & inner, map_to(1, -2))
    emit_copies(i1, map_to(0, -1))

    @pl.when(i3 & inner)
    def _():
        for one in ahead_of_late:
            one.start()

    start_raw(1)

    join = swap("gk", gk.at[c], gk.at[c])
    join.start()
    pm1[...] = d_ref[1]
    join.wait_recv()
    m0[...] = gk[...]
    m1[:, :rows] = g1f[...]
    m1[:, rows:] = -dh1f[:, rows:]

    def turn():
        for j in range(2):
            span = pl.ds(j * wide, wide)
            t0[span, :] = m0[j, :rows].T
            t1[span, :] = m1[j, :rows].T

    turn()

    handoffs = {}

    def take(when, name, ref, number, relay=None):
        here, there = recvs(name, 2), recvs(name, 2) + 1
        onward = copy(ref(c), ref(c), sends(("on", number)), there, mate)
        handoffs[name] = onward

        @pl.when(when)
        def _():
            onward_in = copy(ref(c), ref(c), sends(("on", number)), here, mate)
            onward_in.wait_recv()
            onward.start()

        if relay is not None:
            step, where = relay
            handed = copy(ref(c), ref(c), place[where](("relay", name)), here, at(step))
            emit_copies(when & (i == where), [handed])

        @pl.when(when)
        def _():
            onward.wait_recv()

    uses = (i0, inner & (i0 | i1), inner & jnp.logical_not(i3))
    relays = (None, (1, 0), (-2, 2))

    def take_block(slot, n):
        take(
            uses[slot], (("raw", slot), n), lambda h: zc.at[slot, h, spans[n]],
            (slot % 2) * 4 + n, relays[slot],
        )

    def take_map(slot):
        for n in range(2):
            take(
                uses[slot], (("map", slot), n), lambda h: gc.at[slot, h, parts[n]],
                (slot % 2) * 4 + 2 + n, relays[slot] if slot == 1 else None,
            )

    def handed_on(slot):
        for n in range(2):
            handoffs[("raw", slot), n].wait_send()
            handoffs[("map", slot), n].wait_send()

    def swaps(slot):
        return [
            copy(xm0.at[slot, c], xm0.at[slot, c], sends("m0"), recvs(("m0", slot)), mate),
            copy(xm1.at[slot, c], xm1.at[slot, c], sends("m1"), recvs(("m1", slot)), mate),
        ]

    def compose(slot):
        @pl.when(uses[slot])
        def _():
            unpack_first(zc.at[slot])
            for one, m, x, sign in zip(swaps(slot), (m0, m1), (xm0, xm1), (1.0, -1.0)):
                own = m[c, :rows]
                edge = mm(full[rows:], own)
                x[slot, c, rows:] = (m[c, rows:].astype(F32) + sign * edge).astype(BF16)
                x[slot, c, :rows] = times(gc.at[slot], body, own).astype(BF16)
                one.start()

    def absorb(slot):
        @pl.when(uses[slot])
        def _():
            unpack_second(zc.at[slot])
            for one, m, x, t, p in zip(swaps(slot), (m0, m1), (xm0, xm1), (t0, t1), (pm0, pm1)):
                wb = mm(full[:rows], m[c, :rows]).astype(BF16)
                for j in range(2):
                    span = pl.ds(j * wide, wide)
                    p[span] += mm(t[span, :], wb)
                one.wait_recv()
                m[...] = x[slot]
                for j in range(2):
                    t[pl.ds(j * wide, wide), :] = m[j, :rows].T
            for one in swaps(slot):
                one.wait_send()
            handed_on(slot)

    take_block(0, 0)
    take_block(1, 0)
    take_map(0)
    take_map(1)
    compose(0)
    take_block(0, 1)
    take_block(1, 1)
    absorb(0)
    compose(1)
    absorb(1)
    take_block(2, 0)
    take_block(2, 1)
    take_map(2)
    compose(2)
    absorb(2)

    @pl.when(i3 & inner)
    def _():
        for one in ahead_of_late:
            one.wait_send()
        for one in late:
            one.start()

    pending.append((i3 & inner, late))

    started = jnp.logical_not(i3 & top)
    cov = a_ref[...].astype(BF16)

    def take_y(n):
        take(started, ("y", n), lambda h: zy.at[h, spans[n]], 4 + n)

    def edges(step, sign, m):
        for j in range(2):
            kb[step, j] = sign * mm(full[rows:], m[j, :rows]) + m[j, rows:].astype(F32)

    @pl.when(jnp.logical_not(started))
    def _():
        full[...] = jnp.zeros_like(full)

    def pass_on(n):
        ref = zy.at[c, spans[n]]
        emit_copies(i0 & inner, [copy(ref, ref, place[0](("relay", n)), recvs(("y", n), 2), at(1))])

    take_y(0)
    pass_on(0)

    @pl.when(started)
    def _():
        unpack_first(zy)

    edges(0, 1.0, m0)
    edges(1, -1.0, m1)
    for step in range(2):
        cross_ref[step] = mm(cov, kb[step, c].astype(BF16))

    take_y(1)
    pass_on(1)

    @pl.when(started)
    def _():
        unpack_second(zy)

    def state(m):
        return mm(full[:rows], m[c, :rows]).astype(BF16)

    leads = i0 & passes
    heads = i2 & top

    def start_y(n):
        emit_copies(heads, [packed_to(2, n, zy, "y", -2)])
        emit_copies(leads, [packed_to(0, n, zy, "y", -4), packed_to(0, n, zr, "r", 1)])

    w = state(m0)
    pm0[mine] += mm(t0[mine, :], w)

    @pl.when(leads | heads)
    def _():
        pack_first(pm0, kb[0, c])

    start_y(0)
    pm0[other] += mm(t0[other, :], w)

    @pl.when(leads | heads)
    def _():
        pack_second(pm0)

    start_y(1)
    emit_copies(heads, [packed_to(2, n, zy, "y", -1) for n in range(2)])
    emit_copies(leads, [packed_to(0, n, zy, "y", -2) for n in range(2)])

    for n in range(2):
        ref = zr.at[c, spans[n]]
        there = zy.at[c, spans[n]]
        forth = copy(ref, there, place[1](("r", n)), recvs(("y", n), 2), at(-2))

        @pl.when(i1 & passes)
        def _():
            copy(ref, ref, place[1](("r", n)), recvs(("r", n)), at(-2)).wait_recv()

        emit_copies(i1 & passes, [forth])

    @pl.when(started)
    def _():
        for n in range(2):
            handoffs["y", n].wait_send()

    for one in first:
        one.wait_send()
    join.wait_send()
    for when, copies in pending:

        @pl.when(when)
        def _():
            for one in copies:
                one.wait_send()


def finish(full, m1, t1, pm0, pm1, kb, cross_ref, out_hbm, cross_hbm, out, store):
    rows, wide = out.shape[1], out.shape[2]
    c = lax.axis_index("col")
    ends = pltpu.make_async_copy(cross_ref, cross_hbm, store.at[4])
    ends.start()
    stores = []

    def emit(step, j, value):
        span = pl.ds(j * wide, wide)
        out[step, span] = value + mt(kb[step, j].astype(BF16), cross_ref[step].astype(BF16))
        one = pltpu.make_async_copy(out.at[step, span], out_hbm.at[step, span], store.at[2 * step + j])
        one.start()
        stores.append(one)

    for j in range(2):
        emit(0, j, pm0[pl.ds(j * wide, wide)])
    w = mm(full[:rows], m1[c, :rows]).astype(BF16)
    for j in range(2):
        span = pl.ds(j * wide, wide)
        emit(1, j, pm1[span] + mm(t1[span, :], w))
    ends.wait()
    for one in stores:
        one.wait()


def shards(diagonal_block_inverse, step_map, arrow_map, arrow_cov):
    count, nodes, wide = diagonal_block_inverse.shape
    effects = arrow_map.shape[1]
    tall = nodes + effects
    packed = 4 * (wide // 2) + 2 * effects + MARK
    vmem = pl.BlockSpec(memory_space=pltpu.VMEM)
    hbm = pl.BlockSpec(memory_space=pltpu.HBM)
    held = pl.pallas_call(
        kernel,
        out_shape=(
            jax.ShapeDtypeStruct((tall, nodes), BF16),
            jax.ShapeDtypeStruct((2, tall, wide), BF16),
            jax.ShapeDtypeStruct((nodes, nodes), BF16),
            jax.ShapeDtypeStruct((nodes, wide), F32),
            jax.ShapeDtypeStruct((nodes, wide), F32),
            jax.ShapeDtypeStruct((count, 2, effects, wide), F32),
            jax.ShapeDtypeStruct((count, effects, wide), F32),
        ),
        in_specs=[hbm] * 4,
        out_specs=(vmem,) * 7,
        scratch_shapes=[
            pltpu.VMEM((count, nodes, wide), F32),
            pltpu.VMEM((count, effects, wide), BF16),
            pltpu.VMEM((effects, effects), F32),
            pltpu.VMEM((2, nodes, wide), BF16),
            pltpu.VMEM((2, nodes, wide), BF16),
            pltpu.VMEM((2, tall, wide), BF16),
            pltpu.VMEM((2, tall, wide), BF16),
            pltpu.VMEM((nodes, nodes), BF16),
            pltpu.VMEM((2, tall, wide), BF16),
            pltpu.VMEM((3, 2, tall, wide), BF16),
            pltpu.VMEM((3, 2, tall, wide), BF16),
            pltpu.VMEM((packed, wide // 2), BF16),
            pltpu.VMEM((2, packed, wide // 2), BF16),
            pltpu.VMEM((2, packed, wide // 2), BF16),
            pltpu.VMEM((3, 2, packed, wide // 2), BF16),
            pltpu.VMEM((3, 2, nodes, wide), BF16),
            pltpu.SemaphoreType.DMA((SENDS,)),
            pltpu.SemaphoreType.DMA((RECVS,)),
            pltpu.SemaphoreType.DMA((6,)),
        ],
        compiler_params=pltpu.CompilerParams(
            collective_id=0, has_side_effects=True, vmem_limit_bytes=28 * 1024 * 1024
        ),
    )(*(
        pltpu.with_memory_space_constraint(array, pltpu.HBM)
        for array in (diagonal_block_inverse, step_map, arrow_map, arrow_cov)
    ))
    return pl.pallas_call(
        finish,
        out_shape=(
            jax.ShapeDtypeStruct((count, nodes, wide), F32),
            jax.ShapeDtypeStruct((count, effects, wide), F32),
        ),
        in_specs=[vmem] * 7,
        out_specs=(hbm, hbm),
        scratch_shapes=[
            pltpu.VMEM((count, nodes, wide), F32),
            pltpu.SemaphoreType.DMA((5,)),
        ],
        compiler_params=pltpu.CompilerParams(vmem_limit_bytes=28 * 1024 * 1024),
    )(*held)


def solution(mesh):
    return jax.shard_map(
        shards,
        mesh=mesh,
        in_specs=(
            P(("rep", "tm"), None, "col"),
            P(("rep", "tm"), None, "col"),
            P(("rep", "tm"), None, "col"),
            P("rep", None),
        ),
        out_specs=(P(("rep", "tm"), None, "col"), P(("rep", "tm"), None, "col")),
        check_vma=False,
    )
```

```python
import jax
import jax.numpy as jnp
from jax import lax
from jax.experimental import pallas as pl
from jax.experimental.pallas import tpu as pltpu
from jax.sharding import PartitionSpec as P

MESH = pl.DeviceIdType.MESH
F32 = jnp.float32
BF16 = jnp.bfloat16
SENDS = 28
RECVS = 40
MARK = 16


def mm(left, right):
    return jnp.dot(left, right, preferred_element_type=F32)


def mt(left, right):
    return lax.dot_general(left, right, (((0,), (0,)), ((), ())), preferred_element_type=F32)


class Slots:
    def __init__(self, start, end):
        self.found = {}
        self.free = start
        self.end = end

    def __call__(self, name, width=1):
        if name not in self.found:
            self.found[name] = self.free
            self.free += width
            assert self.free <= self.end
        return self.found[name]


def kernel(
    d_hbm, g_hbm, h_hbm, a_hbm,
    full, m1, t1, pm0, pm1, kb, cross_ref,
    d_ref, h_ref, a_ref, g0f, g1f, dh1f, gk, t0, m0, xm0, xm1,
    zs, zy, zr, zc, gc, fc,
    send, recv, load,
):
    rows = g0f.shape[1]
    wide = g0f.shape[2]
    tall = gk.shape[1]
    half = wide // 2
    edge_rows = tall - rows
    tm = lax.axis_index("tm")
    c = lax.axis_index("col")
    o = 1 - c
    quads = lax.axis_size("tm") // 4
    q = tm // 4
    i = tm % 4
    top = q == quads - 1
    inner = jnp.logical_not(top)
    passes = q > 0
    i0, i1, i2, i3 = (i == n for n in range(4))
    mate = {"col": o}
    recvs = Slots(0, RECVS)
    sends = Slots(0, 14)
    place = [Slots(14, SENDS) for _ in range(4)]

    def at(step):
        return {"tm": tm + step}

    def copy(src, dst, sem, sem_there, device):
        return pltpu.make_async_remote_copy(
            src_ref=src, dst_ref=dst, send_sem=send.at[sem], recv_sem=recv.at[sem_there],
            device_id=device, device_id_type=MESH,
        )

    loads = [
        pltpu.make_async_copy(d_hbm.at[1], d_ref.at[1], load.at[0]),
        pltpu.make_async_copy(h_hbm, h_ref, load.at[1]),
        pltpu.make_async_copy(g_hbm.at[0], g0f.at[c], load.at[2]),
        pltpu.make_async_copy(g_hbm.at[1], g1f.at[c], load.at[3]),
        pltpu.make_async_copy(d_hbm.at[0], d_ref.at[0], load.at[4]),
        pltpu.make_async_copy(a_hbm, a_ref, load.at[5]),
    ]
    for one in loads:
        one.start()

    barrier = pltpu.get_barrier_semaphore()
    pl.semaphore_signal(barrier, inc=1, device_id=mate, device_id_type=MESH)

    def greet(when, steps):
        @pl.when(when)
        def _():
            for step in steps:
                pl.semaphore_signal(barrier, inc=1, device_id=at(step), device_id_type=MESH)

    greet(i0, (1, 2))
    greet(i0 & inner, (3, 4))
    greet(i1, (-1,))
    greet(i1 & inner, (2,))
    greet(i1 & top, (1,))
    greet(i2, (1,))
    greet(i2 & inner, (2,))
    greet(i3 & inner, (2,))

    def one_if(flag):
        return jnp.where(flag, 1, 0)

    targets = (
        1 + 2 * one_if(i3 & inner) + one_if(i2 & top) + one_if(i1 & passes) + 2 * one_if(i0 & passes)
    )

    loads[0].wait()
    loads[1].wait()
    dh1f[c, :rows] = d_ref[1].astype(BF16)
    dh1f[c, rows:] = h_ref[1]
    pl.semaphore_wait(barrier, 1 + targets)

    def swap(name, src, dst):
        return copy(src, dst, sends(name), recvs(name), mate)

    first = [
        swap("dh1", dh1f.at[c], dh1f.at[c]),
        swap("g0", g_hbm.at[0], g0f.at[c]),
        swap("g1", g_hbm.at[1], g1f.at[c]),
    ]
    for one in first:
        one.start()
    for one in loads[2:]:
        one.wait()
    first[0].wait_recv()

    def times(left, span, right):
        return mm(jnp.concatenate([left[0, span], left[1, span]], axis=1), right)

    body = pl.ds(0, rows)
    whole = pl.ds(0, tall)
    mine = pl.ds(pl.multiple_of(c * wide, wide), wide)
    other = pl.ds(pl.multiple_of(o * wide, wide), wide)
    edge_base = 2 * half
    mark_base = edge_base + 2 * edge_rows
    first_rows = mark_base + MARK
    top_span = pl.ds(0, first_rows)
    low_span = pl.ds(first_rows, zs.shape[0] - first_rows)
    spans = (top_span, low_span)
    across = lax.broadcasted_iota(jnp.int32, (half, half), 1)
    down = lax.broadcasted_iota(jnp.int32, (half, half), 0)

    def pack_first(p, edge):
        r = pl.multiple_of(c * wide, wide)
        one = p[pl.ds(r, half), :half]
        two = p[pl.ds(r + half, half), half:]
        zs[:half] = jnp.where(down >= across, one, two).astype(BF16)
        zs[half:edge_base] = p[pl.ds(r, half), half:].astype(BF16)
        zs[edge_base : edge_base + edge_rows] = edge[:, :half].astype(BF16)
        zs[edge_base + edge_rows : mark_base] = edge[:, half:].astype(BF16)
        mark = jnp.sum(jnp.where(down == across, two, 0.0), axis=0, keepdims=True)
        zs[mark_base:first_rows] = jnp.broadcast_to(mark, (MARK, half)).astype(BF16)

    def pack_second(p):
        @pl.when(c == 0)
        def _():
            zs[first_rows : first_rows + half] = p[wide : wide + half, :half].astype(BF16)
            zs[first_rows + half :] = p[wide + half :, :half].astype(BF16)

        @pl.when(c == 1)
        def _():
            zs[first_rows : first_rows + half] = p[half:wide, :half].astype(BF16)
            zs[first_rows + half :] = p[half:wide, half:].astype(BF16)

    def unpack_first(z, full):
        for j in range(2):
            base = j * wide
            lo = pl.ds(base, half)
            hi = pl.ds(base + half, half)
            both = z[j, :half].astype(F32)
            turned = both.T
            mark = z[j, mark_base:first_rows].astype(F32)[:1]
            full[lo, lo] = jnp.where(down >= across, both, turned).astype(BF16)
            full[hi, hi] = jnp.where(
                down < across, both, jnp.where(down == across, mark, turned)
            ).astype(BF16)
            side = z[j, half:edge_base]
            full[lo, hi] = side
            full[hi, lo] = side.T
            for n in range(2):
                full[rows:, pl.ds(base + n * half, half)] = z[
                    j, edge_base + n * edge_rows : edge_base + (n + 1) * edge_rows
                ]

    def unpack_second(z, full):
        for j in range(2):
            close = pl.ds(j * half, half)
            for n in range(2):
                outer = z[j, first_rows + n * half : first_rows + (n + 1) * half]
                far = pl.ds(wide + n * half, half)
                if j == 0:
                    full[far, close] = outer
                    full[close, far] = outer.T
                else:
                    full[close, far] = outer
                    full[far, close] = outer.T

    pending = []

    def emit_copies(when, copies):
        @pl.when(when)
        def _():
            for one in copies:
                one.start()

        pending.append((when, copies))

    def packed_to(where, n, buffer, there, step):
        return copy(
            zs.at[spans[n]], buffer.at[c, spans[n]],
            place[where]((there, step, n)), recvs((there, n), 1 if there == "r" else 2), at(step),
        )

    parts = (pl.ds(0, wide), pl.ds(wide, wide))

    def map_to(slot, step):
        return [
            copy(
                gk.at[c, parts[n]], gc.at[slot, c, parts[n]],
                place[slot + 1](("map", step, n)), recvs((("map", slot), n), 2), at(step),
            )
            for n in range(2)
        ]

    own0 = g0f[c]
    w = times(dh1f, whole, own0)
    wb = w[:rows].astype(BF16)
    kappa = w[rows:] - h_ref[0].astype(F32)
    pm0[mine] = d_ref[0, mine] + mt(g0f[c], wb)

    raw_targets = (
        (i3 & inner, 2, (-1, -2)),
        (i2 & inner, 1, (-2,)),
        (i1, 0, (-1,)),
    )

    def start_raw(n):
        for when, slot, steps in raw_targets:
            emit_copies(
                when, [packed_to(slot + 1, n, zc.at[slot], ("raw", slot), step) for step in steps]
            )

    pack_first(pm0, kappa)
    emit_copies(i3 & top, [packed_to(3, 0, zy, "y", -1)])
    start_raw(0)
    first[1].wait_recv()
    pm0[other] = d_ref[0, other] + mt(g0f[o], wb)
    pack_second(pm0)
    emit_copies(i3 & top, [packed_to(3, 1, zy, "y", -1)])

    first[2].wait_recv()
    gk[c, :rows] = times(g1f, body, own0).astype(BF16)
    gk[c, rows:] = kappa.astype(BF16)
    ahead_of_late = map_to(2, -2)
    late = map_to(2, -3)
    emit_copies(i3 & inner, map_to(2, -1))
    emit_copies(i2 & inner, map_to(1, -2))
    emit_copies(i1, map_to(0, -1))

    @pl.when(i3 & inner)
    def _():
        for one in ahead_of_late:
            one.start()

    start_raw(1)

    join = swap("gk", gk.at[c], gk.at[c])
    join.start()
    pm1[...] = d_ref[1]
    join.wait_recv()
    m0[...] = gk[...]
    m1[:, :rows] = g1f[...]
    m1[:, rows:] = -dh1f[:, rows:]

    def turn():
        for j in range(2):
            span = pl.ds(j * wide, wide)
            t0[span, :] = m0[j, :rows].T
            t1[span, :] = m1[j, :rows].T

    turn()

    handoffs = {}

    def arrive(when, name, ref, number, relay=None):
        here, there = recvs(name, 2), recvs(name, 2) + 1
        onward = copy(ref(c), ref(c), sends(("on", number)), there, mate)
        handoffs[name] = onward

        @pl.when(when)
        def _():
            copy(ref(c), ref(c), sends(("on", number)), here, mate).wait_recv()
            onward.start()

        if relay is not None:
            step, where = relay
            handed = copy(ref(c), ref(c), place[where](("relay", name)), here, at(step))
            emit_copies(when & (i == where), [handed])

    def collect(when, *names):
        @pl.when(when)
        def _():
            for name in names:
                handoffs[name].wait_recv()

    uses = (i0, inner & (i0 | i1), inner & jnp.logical_not(i3))
    relays = (None, (1, 0), (-2, 2))

    def block_arrives(slot, n, when=True):
        arrive(
            uses[slot] & when, (("raw", slot), n), lambda h: zc.at[slot, h, spans[n]],
            (slot % 2) * 4 + n, relays[slot],
        )

    def map_arrives(slot, when=True):
        for n in range(2):
            arrive(
                uses[slot] & when, (("map", slot), n), lambda h: gc.at[slot, h, parts[n]],
                (slot % 2) * 4 + 2 + n, relays[slot] if slot == 1 else None,
            )

    def handed_on(slot):
        for n in range(2):
            handoffs[("raw", slot), n].wait_send()
            handoffs[("map", slot), n].wait_send()

    def swaps(slot):
        return [
            copy(xm0.at[slot, c], xm0.at[slot, c], sends("m0"), recvs(("m0", slot)), mate),
            copy(xm1.at[slot, c], xm1.at[slot, c], sends("m1"), recvs(("m1", slot)), mate),
        ]

    maps = ((m0, xm0, t0, pm0, 1.0), (m1, xm1, t1, pm1, -1.0))

    def compose(slot, n):
        m, x, _, _, sign = maps[n]
        own = m[c, :rows]
        edge = mm(fc[rows:], own)
        x[slot, c, rows:] = (m[c, rows:].astype(F32) + sign * edge).astype(BF16)
        x[slot, c, :rows] = times(gc.at[slot], body, own).astype(BF16)
        swaps(slot)[n].start()

    def absorb(slot, n):
        m, x, t, p, _ = maps[n]
        one = swaps(slot)[n]
        wb = mm(fc[:rows], m[c, :rows]).astype(BF16)
        for j in range(2):
            span = pl.ds(j * wide, wide)
            p[span] += mm(t[span, :], wb)
        one.wait_recv()
        m[...] = x[slot]
        for j in range(2):
            t[pl.ds(j * wide, wide), :] = x[slot, j, :rows].T
        one.wait_send()

    later = i0 & top

    def merge(slot):
        raw, drawn = ("raw", slot), ("map", slot)
        collect(uses[slot], (raw, 0), (drawn, 0), (drawn, 1))

        @pl.when(uses[slot])
        def _():
            unpack_first(zc.at[slot], fc)
            compose(slot, 0)

            @pl.when(jnp.logical_not(later))
            def _():
                compose(slot, 1)

        if slot == 0:
            block_arrives(0, 1)
            block_arrives(1, 1)
            block_arrives(2, 0, i1)
            map_arrives(2, i1)
            block_arrives(2, 1, i1)
        collect(uses[slot], (raw, 1))

        @pl.when(uses[slot])
        def _():
            unpack_second(zc.at[slot], fc)
            absorb(slot, 0)

            @pl.when(jnp.logical_not(later))
            def _():
                absorb(slot, 1)

            handed_on(slot)

    block_arrives(0, 0)
    block_arrives(1, 0)
    map_arrives(0)
    map_arrives(1)
    merge(0)
    merge(1)
    early = jnp.logical_not(i1)
    block_arrives(2, 0, early)
    map_arrives(2, early)
    block_arrives(2, 1, early)
    merge(2)

    @pl.when(i3 & inner)
    def _():
        for one in ahead_of_late:
            one.wait_send()
        for one in late:
            one.start()

    pending.append((i3 & inner, late))

    started = jnp.logical_not(i3 & top)
    cov = a_ref[...].astype(BF16)

    def y_arrives(n):
        arrive(started, ("y", n), lambda h: zy.at[h, spans[n]], 4 + n)
        ref = zy.at[c, spans[n]]
        emit_copies(i0 & inner, [copy(ref, ref, place[0](("relay", n)), recvs(("y", n), 2), at(1))])

    def edges(step, sign, m):
        for j in range(2):
            kb[step, j] = sign * mm(full[rows:], m[j, :rows]) + m[j, rows:].astype(F32)
        cross_ref[step] = mm(cov, kb[step, c].astype(BF16))

    @pl.when(jnp.logical_not(started))
    def _():
        full[...] = jnp.zeros_like(full)

    y_arrives(0)
    collect(started, ("y", 0))

    @pl.when(started)
    def _():
        unpack_first(zy, full)

    y_arrives(1)
    edges(0, 1.0, m0)

    @pl.when(jnp.logical_not(later))
    def _():
        edges(1, -1.0, m1)

    collect(started, ("y", 1))

    @pl.when(started)
    def _():
        unpack_second(zy, full)

    def state(m):
        return mm(full[:rows], m[c, :rows]).astype(BF16)

    leads = i0 & passes
    heads = i2 & top

    def start_y(n):
        emit_copies(heads, [packed_to(2, n, zy, "y", -2)])
        emit_copies(leads, [packed_to(0, n, zy, "y", -4), packed_to(0, n, zr, "r", 1)])

    w = state(m0)
    pm0[mine] += mm(t0[mine, :], w)

    @pl.when(leads | heads)
    def _():
        pack_first(pm0, kb[0, c])

    start_y(0)
    pm0[other] += mm(t0[other, :], w)

    @pl.when(leads | heads)
    def _():
        pack_second(pm0)

    start_y(1)
    emit_copies(heads, [packed_to(2, n, zy, "y", -1) for n in range(2)])
    emit_copies(leads, [packed_to(0, n, zy, "y", -2) for n in range(2)])

    @pl.when(later)
    def _():
        compose(0, 1)
        absorb(0, 1)
        edges(1, -1.0, m1)

    for n in range(2):
        ref = zr.at[c, spans[n]]
        there = zy.at[c, spans[n]]
        forth = copy(ref, there, place[1](("r", n)), recvs(("y", n), 2), at(-2))

        @pl.when(i1 & passes)
        def _():
            copy(ref, ref, place[1](("r", n)), recvs(("r", n)), at(-2)).wait_recv()

        emit_copies(i1 & passes, [forth])

    @pl.when(started)
    def _():
        for n in range(2):
            handoffs["y", n].wait_send()

    for one in first:
        one.wait_send()
    join.wait_send()
    for when, copies in pending:

        @pl.when(when)
        def _():
            for one in copies:
                one.wait_send()


def finish(full, m1, t1, pm0, pm1, kb, cross_ref, out_hbm, cross_hbm, out, store):
    rows, wide = out.shape[1], out.shape[2]
    c = lax.axis_index("col")
    ends = pltpu.make_async_copy(cross_ref, cross_hbm, store.at[4])
    ends.start()
    stores = []

    def emit(step, j, value):
        span = pl.ds(j * wide, wide)
        out[step, span] = value + mt(kb[step, j].astype(BF16), cross_ref[step].astype(BF16))
        one = pltpu.make_async_copy(out.at[step, span], out_hbm.at[step, span], store.at[2 * step + j])
        one.start()
        stores.append(one)

    for j in range(2):
        emit(0, j, pm0[pl.ds(j * wide, wide)])
    w = mm(full[:rows], m1[c, :rows]).astype(BF16)
    for j in range(2):
        span = pl.ds(j * wide, wide)
        emit(1, j, pm1[span] + mm(t1[span, :], w))
    ends.wait()
    for one in stores:
        one.wait()


def shards(diagonal_block_inverse, step_map, arrow_map, arrow_cov):
    count, nodes, wide = diagonal_block_inverse.shape
    effects = arrow_map.shape[1]
    tall = nodes + effects
    packed = 4 * (wide // 2) + 2 * effects + MARK
    vmem = pl.BlockSpec(memory_space=pltpu.VMEM)
    hbm = pl.BlockSpec(memory_space=pltpu.HBM)
    held = pl.pallas_call(
        kernel,
        out_shape=(
            jax.ShapeDtypeStruct((tall, nodes), BF16),
            jax.ShapeDtypeStruct((2, tall, wide), BF16),
            jax.ShapeDtypeStruct((nodes, nodes), BF16),
            jax.ShapeDtypeStruct((nodes, wide), F32),
            jax.ShapeDtypeStruct((nodes, wide), F32),
            jax.ShapeDtypeStruct((count, 2, effects, wide), F32),
            jax.ShapeDtypeStruct((count, effects, wide), F32),
        ),
        in_specs=[hbm] * 4,
        out_specs=(vmem,) * 7,
        scratch_shapes=[
            pltpu.VMEM((count, nodes, wide), F32),
            pltpu.VMEM((count, effects, wide), BF16),
            pltpu.VMEM((effects, effects), F32),
            pltpu.VMEM((2, nodes, wide), BF16),
            pltpu.VMEM((2, nodes, wide), BF16),
            pltpu.VMEM((2, tall, wide), BF16),
            pltpu.VMEM((2, tall, wide), BF16),
            pltpu.VMEM((nodes, nodes), BF16),
            pltpu.VMEM((2, tall, wide), BF16),
            pltpu.VMEM((3, 2, tall, wide), BF16),
            pltpu.VMEM((3, 2, tall, wide), BF16),
            pltpu.VMEM((packed, wide // 2), BF16),
            pltpu.VMEM((2, packed, wide // 2), BF16),
            pltpu.VMEM((2, packed, wide // 2), BF16),
            pltpu.VMEM((3, 2, packed, wide // 2), BF16),
            pltpu.VMEM((3, 2, nodes, wide), BF16),
            pltpu.VMEM((tall, nodes), BF16),
            pltpu.SemaphoreType.DMA((SENDS,)),
            pltpu.SemaphoreType.DMA((RECVS,)),
            pltpu.SemaphoreType.DMA((6,)),
        ],
        compiler_params=pltpu.CompilerParams(
            collective_id=0, has_side_effects=True, vmem_limit_bytes=28 * 1024 * 1024
        ),
    )(*(
        pltpu.with_memory_space_constraint(array, pltpu.HBM)
        for array in (diagonal_block_inverse, step_map, arrow_map, arrow_cov)
    ))
    return pl.pallas_call(
        finish,
        out_shape=(
            jax.ShapeDtypeStruct((count, nodes, wide), F32),
            jax.ShapeDtypeStruct((count, effects, wide), F32),
        ),
        in_specs=[vmem] * 7,
        out_specs=(hbm, hbm),
        scratch_shapes=[
            pltpu.VMEM((count, nodes, wide), F32),
            pltpu.SemaphoreType.DMA((5,)),
        ],
        compiler_params=pltpu.CompilerParams(vmem_limit_bytes=28 * 1024 * 1024),
    )(*held)


def solution(mesh):
    return jax.shard_map(
        shards,
        mesh=mesh,
        in_specs=(
            P(("rep", "tm"), None, "col"),
            P(("rep", "tm"), None, "col"),
            P(("rep", "tm"), None, "col"),
            P("rep", None),
        ),
        out_specs=(P(("rep", "tm"), None, "col"), P(("rep", "tm"), None, "col")),
        check_vma=False,
    )
```

```python
import jax
import jax.numpy as jnp
from jax import lax
from jax.experimental import pallas as pl
from jax.experimental.pallas import tpu as pltpu
from jax.sharding import PartitionSpec as P

MESH = pl.DeviceIdType.MESH
F32 = jnp.float32
BF16 = jnp.bfloat16
SENDS = 31
RECVS = 43
MARK = 16


def mm(left, right):
    return jnp.dot(left, right, preferred_element_type=F32)


def mt(left, right):
    return lax.dot_general(left, right, (((0,), (0,)), ((), ())), preferred_element_type=F32)


class Slots:
    def __init__(self, start, end):
        self.found = {}
        self.free = start
        self.end = end

    def __call__(self, name, width=1):
        if name not in self.found:
            self.found[name] = self.free
            self.free += width
            assert self.free <= self.end
        return self.found[name]


def kernel(
    d_hbm, g_hbm, h_hbm, a_hbm,
    full, m1, t1, pm0, pm1, kb, cross_ref,
    d_ref, h_ref, a_ref, g0f, g1f, dh1f, gk, t0, m0, xm0, xm1,
    zs, zy, zr, zc, gc, fc,
    send, recv, load,
):
    rows = g0f.shape[1]
    wide = g0f.shape[2]
    tall = gk.shape[1]
    half = wide // 2
    edge_rows = tall - rows
    tm = lax.axis_index("tm")
    c = lax.axis_index("col")
    o = 1 - c
    quads = lax.axis_size("tm") // 4
    q = tm // 4
    i = tm % 4
    top = q == quads - 1
    inner = jnp.logical_not(top)
    passes = q > 0
    i0, i1, i2, i3 = (i == n for n in range(4))
    mate = {"col": o}
    recvs = Slots(0, RECVS)
    sends = Slots(0, 15)
    place = [Slots(15, SENDS) for _ in range(4)]

    def at(step):
        return {"tm": tm + step, "col": o}

    def copy(src, dst, sem, sem_there, device):
        return pltpu.make_async_remote_copy(
            src_ref=src, dst_ref=dst, send_sem=send.at[sem], recv_sem=recv.at[sem_there],
            device_id=device, device_id_type=MESH,
        )

    loads = [
        pltpu.make_async_copy(d_hbm.at[1], d_ref.at[1], load.at[0]),
        pltpu.make_async_copy(h_hbm, h_ref, load.at[1]),
        pltpu.make_async_copy(g_hbm.at[0], g0f.at[c], load.at[2]),
        pltpu.make_async_copy(g_hbm.at[1], g1f.at[c], load.at[3]),
        pltpu.make_async_copy(d_hbm.at[0], d_ref.at[0], load.at[4]),
        pltpu.make_async_copy(a_hbm, a_ref, load.at[5]),
    ]
    for one in loads:
        one.start()

    barrier = pltpu.get_barrier_semaphore()
    pl.semaphore_signal(barrier, inc=1, device_id=mate, device_id_type=MESH)

    def greet(when, steps):
        @pl.when(when)
        def _():
            for step in steps:
                pl.semaphore_signal(barrier, inc=1, device_id=at(step), device_id_type=MESH)

    greet(i0, (1, 2))
    greet(i0 & inner, (3, 4))
    greet(i1, (-1,))
    greet(i1 & inner, (2,))
    greet(i1 & top, (1,))
    greet(i2, (1,))
    greet(i2 & inner, (2,))
    greet(i3 & inner, (2,))

    def one_if(flag):
        return jnp.where(flag, 1, 0)

    targets = (
        1 + 2 * one_if(i3 & inner) + one_if(i2 & top) + one_if(i1 & passes) + 2 * one_if(i0 & passes)
    )

    loads[0].wait()
    loads[1].wait()
    dh1f[c, :rows] = d_ref[1].astype(BF16)
    dh1f[c, rows:] = h_ref[1]
    pl.semaphore_wait(barrier, 1 + targets)

    def swap(name, src, dst):
        return copy(src, dst, sends(name), recvs(name), mate)

    first = [
        swap("dh1", dh1f.at[c], dh1f.at[c]),
        swap("g0", g_hbm.at[0], g0f.at[c]),
        swap("g1", g_hbm.at[1], g1f.at[c]),
    ]
    for one in first:
        one.start()
    for one in loads[2:]:
        one.wait()
    first[0].wait_recv()

    def times(left, span, right):
        return mm(jnp.concatenate([left[0, span], left[1, span]], axis=1), right)

    body = pl.ds(0, rows)
    whole = pl.ds(0, tall)
    mine = pl.ds(pl.multiple_of(c * wide, wide), wide)
    other = pl.ds(pl.multiple_of(o * wide, wide), wide)
    edge_base = 2 * half
    mark_base = edge_base + 2 * edge_rows
    first_rows = mark_base + MARK
    top_span = pl.ds(0, first_rows)
    low_span = pl.ds(first_rows, zs.shape[0] - first_rows)
    spans = (top_span, low_span)
    fine = (top_span, pl.ds(first_rows, half), pl.ds(first_rows + half, half))
    across = lax.broadcasted_iota(jnp.int32, (half, half), 1)
    down = lax.broadcasted_iota(jnp.int32, (half, half), 0)

    def pack_first(p, edge):
        r = pl.multiple_of(c * wide, wide)
        one = p[pl.ds(r, half), :half]
        two = p[pl.ds(r + half, half), half:]
        zs[:half] = jnp.where(down >= across, one, two).astype(BF16)
        zs[half:edge_base] = p[pl.ds(r, half), half:].astype(BF16)
        zs[edge_base : edge_base + edge_rows] = edge[:, :half].astype(BF16)
        zs[edge_base + edge_rows : mark_base] = edge[:, half:].astype(BF16)
        mark = jnp.sum(jnp.where(down == across, two, 0.0), axis=0, keepdims=True)
        zs[mark_base:first_rows] = jnp.broadcast_to(mark, (MARK, half)).astype(BF16)

    def pack_outer(p, n):
        to = fine[1 + n]

        @pl.when(c == 0)
        def _():
            zs[to] = p[pl.ds(wide + n * half, half), :half].astype(BF16)

        @pl.when(c == 1)
        def _():
            zs[to] = p[half:wide, pl.ds(n * half, half)].astype(BF16)

    def unpack_first(z, full):
        for j in range(2):
            base = j * wide
            lo = pl.ds(base, half)
            hi = pl.ds(base + half, half)
            both = z[j, :half].astype(F32)
            turned = both.T
            mark = z[j, mark_base:first_rows].astype(F32)[:1]
            full[lo, lo] = jnp.where(down >= across, both, turned).astype(BF16)
            full[hi, hi] = jnp.where(
                down < across, both, jnp.where(down == across, mark, turned)
            ).astype(BF16)
            side = z[j, half:edge_base]
            full[lo, hi] = side
            full[hi, lo] = side.T
            for n in range(2):
                full[rows:, pl.ds(base + n * half, half)] = z[
                    j, edge_base + n * edge_rows : edge_base + (n + 1) * edge_rows
                ]

    def unpack_outer(z, full, n):
        far = pl.ds(wide + n * half, half)
        for j in range(2):
            close = pl.ds(j * half, half)
            outer = z[j, fine[1 + n]]
            if j == 0:
                full[far, close] = outer
                full[close, far] = outer.T
            else:
                full[close, far] = outer
                full[far, close] = outer.T

    pending = []

    def emit_copies(when, copies):
        @pl.when(when)
        def _():
            for one in copies:
                one.start()

        pending.append((when, copies))

    def packed_to(where, n, buffer, there, step):
        span = (spans if there[0] == "raw" else fine)[n]
        return copy(
            zs.at[span], buffer.at[c, span],
            place[where]((there, step, n)), recvs((there, n), 1 if there == "r" else 2), at(step),
        )

    parts = (pl.ds(0, wide), pl.ds(wide, wide))

    def map_to(slot, step):
        return [
            copy(
                gk.at[c, parts[n]], gc.at[slot, c, parts[n]],
                place[slot + 1](("map", step, n)), recvs((("map", slot), n), 2), at(step),
            )
            for n in range(2)
        ]

    own0 = g0f[c]
    w = times(dh1f, whole, own0)
    wb = w[:rows].astype(BF16)
    kappa = w[rows:] - h_ref[0].astype(F32)
    pm0[mine] = d_ref[0, mine] + mt(g0f[c], wb)

    raw_targets = (
        (i3 & inner, 2, (-1, -2)),
        (i2 & inner, 1, (-2,)),
        (i1, 0, (-1,)),
    )

    def start_raw(n):
        for when, slot, steps in raw_targets:
            emit_copies(
                when, [packed_to(slot + 1, n, zc.at[slot], ("raw", slot), step) for step in steps]
            )

    pack_first(pm0, kappa)
    emit_copies(i3 & top, [packed_to(3, 0, zy, "y", -1)])
    start_raw(0)
    first[1].wait_recv()
    pm0[other] = d_ref[0, other] + mt(g0f[o], wb)
    for n in range(2):
        pack_outer(pm0, n)
        emit_copies(i3 & top, [packed_to(3, 1 + n, zy, "y", -1)])

    first[2].wait_recv()
    gk[c, :rows] = times(g1f, body, own0).astype(BF16)
    gk[c, rows:] = kappa.astype(BF16)
    ahead_of_late = map_to(2, -2)
    late = map_to(2, -3)
    emit_copies(i3 & inner, map_to(2, -1))
    emit_copies(i2 & inner, map_to(1, -2))
    emit_copies(i1, map_to(0, -1))

    @pl.when(i3 & inner)
    def _():
        for one in ahead_of_late:
            one.start()

    start_raw(1)

    join = swap("gk", gk.at[c], gk.at[c])
    join.start()
    pm1[...] = d_ref[1]
    join.wait_recv()
    m0[...] = gk[...]
    m1[:, :rows] = g1f[...]
    m1[:, rows:] = -dh1f[:, rows:]

    def turn():
        for j in range(2):
            span = pl.ds(j * wide, wide)
            t0[span, :] = m0[j, :rows].T
            t1[span, :] = m1[j, :rows].T

    turn()

    handoffs = {}

    def arrive(when, name, ref, number, relay=None, relayed=None):
        here, there = recvs(name, 2), recvs(name, 2) + 1
        h = o if relayed is None else jnp.where(relayed, c, o)
        onward = copy(ref(h), ref(h), sends(("on", number)), there, mate)
        handoffs[name] = onward

        @pl.when(when)
        def _():
            copy(ref(h), ref(h), sends(("on", number)), here, mate).wait_recv()
            onward.start()

        if relay is not None:
            step, where = relay
            handed = copy(ref(h), ref(h), place[where](("relay", name)), here, at(step))
            emit_copies(when & (i == where), [handed])

    def collect(when, *names):
        @pl.when(when)
        def _():
            for name in names:
                handoffs[name].wait_recv()

    uses = (i0, inner & (i0 | i1), inner & jnp.logical_not(i3))
    relays = (None, (1, 0), (-2, 2))

    def block_arrives(slot, n, when=True):
        arrive(
            uses[slot] & when, (("raw", slot), n), lambda h: zc.at[slot, h, spans[n]],
            (slot % 2) * 4 + n, relays[slot], (None, i1, i0)[slot],
        )

    def map_arrives(slot, when=True):
        for n in range(2):
            arrive(
                uses[slot] & when, (("map", slot), n), lambda h: gc.at[slot, h, parts[n]],
                (slot % 2) * 4 + 2 + n, relays[slot] if slot == 1 else None, i1 if slot == 1 else None,
            )

    def handed_on(slot):
        for n in range(2):
            handoffs[("raw", slot), n].wait_send()
            handoffs[("map", slot), n].wait_send()

    def swaps(slot):
        return [
            copy(xm0.at[slot, c], xm0.at[slot, c], sends("m0"), recvs(("m0", slot)), mate),
            copy(xm1.at[slot, c], xm1.at[slot, c], sends("m1"), recvs(("m1", slot)), mate),
        ]

    maps = ((m0, xm0, t0, pm0, 1.0), (m1, xm1, t1, pm1, -1.0))

    def compose(slot, n):
        m, x, _, _, sign = maps[n]
        own = m[c, :rows]
        edge = mm(fc[rows:], own)
        x[slot, c, rows:] = (m[c, rows:].astype(F32) + sign * edge).astype(BF16)
        x[slot, c, :rows] = times(gc.at[slot], body, own).astype(BF16)
        swaps(slot)[n].start()

    def absorb(slot, n):
        m, x, t, p, _ = maps[n]
        one = swaps(slot)[n]
        wb = mm(fc[:rows], m[c, :rows]).astype(BF16)
        for j in range(2):
            span = pl.ds(j * wide, wide)
            p[span] += mm(t[span, :], wb)
        one.wait_recv()
        m[...] = x[slot]
        for j in range(2):
            t[pl.ds(j * wide, wide), :] = x[slot, j, :rows].T
        one.wait_send()

    later = i0 & top

    def merge(slot):
        raw, drawn = ("raw", slot), ("map", slot)
        collect(uses[slot], (raw, 0), (drawn, 0), (drawn, 1))

        @pl.when(uses[slot])
        def _():
            unpack_first(zc.at[slot], fc)
            compose(slot, 0)

            @pl.when(jnp.logical_not(later))
            def _():
                compose(slot, 1)

        if slot == 0:
            block_arrives(0, 1)
            block_arrives(1, 1)
            block_arrives(2, 0, i1)
            map_arrives(2, i1)
            block_arrives(2, 1, i1)
        collect(uses[slot], (raw, 1))

        @pl.when(uses[slot])
        def _():
            for n in range(2):
                unpack_outer(zc.at[slot], fc, n)
            absorb(slot, 0)

            @pl.when(jnp.logical_not(later))
            def _():
                absorb(slot, 1)

            handed_on(slot)

    block_arrives(0, 0)
    block_arrives(1, 0)
    map_arrives(0)
    map_arrives(1)
    merge(0)
    merge(1)
    early = jnp.logical_not(i1)
    block_arrives(2, 0, early)
    map_arrives(2, early)
    block_arrives(2, 1, early)
    merge(2)

    @pl.when(i3 & inner)
    def _():
        for one in ahead_of_late:
            one.wait_send()
        for one in late:
            one.start()

    pending.append((i3 & inner, late))

    started = jnp.logical_not(i3 & top)
    cov = a_ref[...].astype(BF16)

    def y_arrives(n):
        arrive(
            started, ("y", n), lambda h: zy.at[h, fine[n]], (4, 5, 8)[n], None, (i1 & inner) | i3
        )
        ref = zy.at[o, fine[n]]
        emit_copies(i0 & inner, [copy(ref, ref, place[0](("relay", n)), recvs(("y", n), 2), at(1))])

    def edges(step, sign, m):
        for j in range(2):
            kb[step, j] = sign * mm(full[rows:], m[j, :rows]) + m[j, rows:].astype(F32)
        cross_ref[step] = mm(cov, kb[step, c].astype(BF16))

    @pl.when(jnp.logical_not(started))
    def _():
        full[...] = jnp.zeros_like(full)

    y_arrives(0)
    y_arrives(1)
    collect(started, ("y", 0))

    @pl.when(started)
    def _():
        unpack_first(zy, full)

    y_arrives(2)
    edges(0, 1.0, m0)

    @pl.when(jnp.logical_not(later))
    def _():
        edges(1, -1.0, m1)

    for n in range(2):
        collect(started, ("y", 1 + n))

        @pl.when(started)
        def _():
            unpack_outer(zy, full, n)

    def state(m):
        return mm(full[:rows], m[c, :rows]).astype(BF16)

    leads = i0 & passes
    heads = i2 & top

    def start_y(n):
        emit_copies(heads, [packed_to(2, n, zy, "y", -2)])
        emit_copies(leads, [packed_to(0, n, zy, "y", -4), packed_to(0, n, zr, "r", 1)])

    w = state(m0)
    pm0[mine] += mm(t0[mine, :], w)

    @pl.when(leads | heads)
    def _():
        pack_first(pm0, kb[0, c])

    start_y(0)
    pm0[other] += mm(t0[other, :], w)

    for n in range(2):

        @pl.when(leads | heads)
        def _():
            pack_outer(pm0, n)

        start_y(1 + n)
    emit_copies(heads, [packed_to(2, n, zy, "y", -1) for n in range(3)])
    emit_copies(leads, [packed_to(0, n, zy, "y", -2) for n in range(3)])

    @pl.when(later)
    def _():
        compose(0, 1)
        absorb(0, 1)
        edges(1, -1.0, m1)

    for n in range(3):
        ref = zr.at[o, fine[n]]
        there = zy.at[o, fine[n]]
        forth = copy(ref, there, place[1](("r", n)), recvs(("y", n), 2), at(-2))

        @pl.when(i1 & passes)
        def _():
            copy(ref, ref, place[1](("r", n)), recvs(("r", n)), at(-2)).wait_recv()

        emit_copies(i1 & passes, [forth])

    @pl.when(started)
    def _():
        for n in range(3):
            handoffs["y", n].wait_send()

    for one in first:
        one.wait_send()
    join.wait_send()
    for when, copies in pending:

        @pl.when(when)
        def _():
            for one in copies:
                one.wait_send()


def finish(full, m1, t1, pm0, pm1, kb, cross_ref, out_hbm, cross_hbm, out, store):
    rows, wide = out.shape[1], out.shape[2]
    c = lax.axis_index("col")
    ends = pltpu.make_async_copy(cross_ref, cross_hbm, store.at[4])
    ends.start()
    stores = []

    def emit(step, j, value):
        span = pl.ds(j * wide, wide)
        out[step, span] = value + mt(kb[step, j].astype(BF16), cross_ref[step].astype(BF16))
        one = pltpu.make_async_copy(out.at[step, span], out_hbm.at[step, span], store.at[2 * step + j])
        one.start()
        stores.append(one)

    for j in range(2):
        emit(0, j, pm0[pl.ds(j * wide, wide)])
    w = mm(full[:rows], m1[c, :rows]).astype(BF16)
    for j in range(2):
        span = pl.ds(j * wide, wide)
        emit(1, j, pm1[span] + mm(t1[span, :], w))
    ends.wait()
    for one in stores:
        one.wait()


def shards(diagonal_block_inverse, step_map, arrow_map, arrow_cov):
    count, nodes, wide = diagonal_block_inverse.shape
    effects = arrow_map.shape[1]
    tall = nodes + effects
    packed = 4 * (wide // 2) + 2 * effects + MARK
    vmem = pl.BlockSpec(memory_space=pltpu.VMEM)
    hbm = pl.BlockSpec(memory_space=pltpu.HBM)
    held = pl.pallas_call(
        kernel,
        out_shape=(
            jax.ShapeDtypeStruct((tall, nodes), BF16),
            jax.ShapeDtypeStruct((2, tall, wide), BF16),
            jax.ShapeDtypeStruct((nodes, nodes), BF16),
            jax.ShapeDtypeStruct((nodes, wide), F32),
            jax.ShapeDtypeStruct((nodes, wide), F32),
            jax.ShapeDtypeStruct((count, 2, effects, wide), F32),
            jax.ShapeDtypeStruct((count, effects, wide), F32),
        ),
        in_specs=[hbm] * 4,
        out_specs=(vmem,) * 7,
        scratch_shapes=[
            pltpu.VMEM((count, nodes, wide), F32),
            pltpu.VMEM((count, effects, wide), BF16),
            pltpu.VMEM((effects, effects), F32),
            pltpu.VMEM((2, nodes, wide), BF16),
            pltpu.VMEM((2, nodes, wide), BF16),
            pltpu.VMEM((2, tall, wide), BF16),
            pltpu.VMEM((2, tall, wide), BF16),
            pltpu.VMEM((nodes, nodes), BF16),
            pltpu.VMEM((2, tall, wide), BF16),
            pltpu.VMEM((3, 2, tall, wide), BF16),
            pltpu.VMEM((3, 2, tall, wide), BF16),
            pltpu.VMEM((packed, wide // 2), BF16),
            pltpu.VMEM((2, packed, wide // 2), BF16),
            pltpu.VMEM((2, packed, wide // 2), BF16),
            pltpu.VMEM((3, 2, packed, wide // 2), BF16),
            pltpu.VMEM((3, 2, nodes, wide), BF16),
            pltpu.VMEM((tall, nodes), BF16),
            pltpu.SemaphoreType.DMA((SENDS,)),
            pltpu.SemaphoreType.DMA((RECVS,)),
            pltpu.SemaphoreType.DMA((6,)),
        ],
        compiler_params=pltpu.CompilerParams(
            collective_id=0, has_side_effects=True, vmem_limit_bytes=28 * 1024 * 1024
        ),
    )(*(
        pltpu.with_memory_space_constraint(array, pltpu.HBM)
        for array in (diagonal_block_inverse, step_map, arrow_map, arrow_cov)
    ))
    return pl.pallas_call(
        finish,
        out_shape=(
            jax.ShapeDtypeStruct((count, nodes, wide), F32),
            jax.ShapeDtypeStruct((count, effects, wide), F32),
        ),
        in_specs=[vmem] * 7,
        out_specs=(hbm, hbm),
        scratch_shapes=[
            pltpu.VMEM((count, nodes, wide), F32),
            pltpu.SemaphoreType.DMA((5,)),
        ],
        compiler_params=pltpu.CompilerParams(vmem_limit_bytes=28 * 1024 * 1024),
    )(*held)


def solution(mesh):
    return jax.shard_map(
        shards,
        mesh=mesh,
        in_specs=(
            P(("rep", "tm"), None, "col"),
            P(("rep", "tm"), None, "col"),
            P(("rep", "tm"), None, "col"),
            P("rep", None),
        ),
        out_specs=(P(("rep", "tm"), None, "col"), P(("rep", "tm"), None, "col")),
        check_vma=False,
    )
```

```python
import jax
import jax.numpy as jnp
from jax import lax
from jax.experimental import pallas as pl
from jax.experimental.pallas import tpu as pltpu
from jax.sharding import PartitionSpec as P

MESH = pl.DeviceIdType.MESH
F32 = jnp.float32
BF16 = jnp.bfloat16
SENDS = 32
RECVS = 43
MARK = 16


def mm(left, right):
    return jnp.dot(left, right, preferred_element_type=F32)


def mt(left, right):
    return lax.dot_general(left, right, (((0,), (0,)), ((), ())), preferred_element_type=F32)


class Slots:
    def __init__(self, start, end):
        self.found = {}
        self.free = start
        self.end = end

    def __call__(self, name, width=1):
        if name not in self.found:
            self.found[name] = self.free
            self.free += width
            assert self.free <= self.end
        return self.found[name]


def kernel(
    d_hbm, g_hbm, h_hbm, a_hbm,
    full, m1, t1, pm0, pm1, kb, cross_ref,
    d_ref, h_ref, a_ref, g0f, g1f, dh1f, gk, t0, m0, xm0, xm1,
    zs, zy, zr, zc, gc, fc,
    send, recv, load,
):
    rows = g0f.shape[1]
    wide = g0f.shape[2]
    tall = gk.shape[1]
    half = wide // 2
    edge_rows = tall - rows
    tm = lax.axis_index("tm")
    c = lax.axis_index("col")
    o = 1 - c
    quads = lax.axis_size("tm") // 4
    q = tm // 4
    i = tm % 4
    top = q == quads - 1
    inner = jnp.logical_not(top)
    passes = q > 0
    i0, i1, i2, i3 = (i == n for n in range(4))
    mate = {"col": o}
    recvs = Slots(0, RECVS)
    sends = Slots(0, 16)
    place = [Slots(16, SENDS) for _ in range(4)]

    def at(step):
        return {"tm": tm + step, "col": o}

    def copy(src, dst, sem, sem_there, device):
        return pltpu.make_async_remote_copy(
            src_ref=src, dst_ref=dst, send_sem=send.at[sem], recv_sem=recv.at[sem_there],
            device_id=device, device_id_type=MESH,
        )

    loads = [
        pltpu.make_async_copy(d_hbm.at[1], d_ref.at[1], load.at[0]),
        pltpu.make_async_copy(h_hbm, h_ref, load.at[1]),
        pltpu.make_async_copy(g_hbm.at[0], g0f.at[c], load.at[2]),
        pltpu.make_async_copy(g_hbm.at[1], g1f.at[c], load.at[3]),
        pltpu.make_async_copy(d_hbm.at[0], d_ref.at[0], load.at[4]),
        pltpu.make_async_copy(a_hbm, a_ref, load.at[5]),
    ]
    for one in loads:
        one.start()

    barrier = pltpu.get_barrier_semaphore()
    pl.semaphore_signal(barrier, inc=1, device_id=mate, device_id_type=MESH)

    def greet(when, steps):
        @pl.when(when)
        def _():
            for step in steps:
                pl.semaphore_signal(barrier, inc=1, device_id=at(step), device_id_type=MESH)

    greet(i0, (1, 2))
    greet(i0 & inner, (3, 4))
    greet(i1, (-1,))
    greet(i1 & inner, (2,))
    greet(i1 & top, (1,))
    greet(i2, (1,))
    greet(i2 & inner, (2,))
    greet(i3 & inner, (2,))

    def one_if(flag):
        return jnp.where(flag, 1, 0)

    targets = (
        1 + 2 * one_if(i3 & inner) + one_if(i2 & top) + one_if(i1 & passes) + 2 * one_if(i0 & passes)
    )

    loads[0].wait()
    loads[1].wait()
    dh1f[c, :rows] = d_ref[1].astype(BF16)
    dh1f[c, rows:] = h_ref[1]
    pl.semaphore_wait(barrier, 1 + targets)

    def swap(name, src, dst):
        return copy(src, dst, sends(name), recvs(name), mate)

    first = [
        swap("dh1", dh1f.at[c], dh1f.at[c]),
        swap("g0", g_hbm.at[0], g0f.at[c]),
        swap("g1", g_hbm.at[1], g1f.at[c]),
    ]
    for one in first:
        one.start()
    for one in loads[2:]:
        one.wait()
    first[0].wait_recv()

    def times(left, span, right):
        return mm(jnp.concatenate([left[0, span], left[1, span]], axis=1), right)

    body = pl.ds(0, rows)
    whole = pl.ds(0, tall)
    mine = pl.ds(pl.multiple_of(c * wide, wide), wide)
    other = pl.ds(pl.multiple_of(o * wide, wide), wide)
    edge_base = 2 * half
    mark_base = edge_base + 2 * edge_rows
    first_rows = mark_base + MARK
    top_span = pl.ds(0, first_rows)
    low_span = pl.ds(first_rows, zs.shape[0] - first_rows)
    spans = (top_span, low_span)
    fine = (top_span, pl.ds(first_rows, half), pl.ds(first_rows + half, half))
    across = lax.broadcasted_iota(jnp.int32, (half, half), 1)
    down = lax.broadcasted_iota(jnp.int32, (half, half), 0)

    def pack_first(p, edge):
        r = pl.multiple_of(c * wide, wide)
        one = p[pl.ds(r, half), :half]
        two = p[pl.ds(r + half, half), half:]
        zs[:half] = jnp.where(down >= across, one, two).astype(BF16)
        zs[half:edge_base] = p[pl.ds(r, half), half:].astype(BF16)
        zs[edge_base : edge_base + edge_rows] = edge[:, :half].astype(BF16)
        zs[edge_base + edge_rows : mark_base] = edge[:, half:].astype(BF16)
        mark = jnp.sum(jnp.where(down == across, two, 0.0), axis=0, keepdims=True)
        zs[mark_base:first_rows] = jnp.broadcast_to(mark, (MARK, half)).astype(BF16)

    def pack_outer(p, n):
        to = fine[1 + n]

        @pl.when(c == 0)
        def _():
            zs[to] = p[pl.ds(wide + n * half, half), :half].astype(BF16)

        @pl.when(c == 1)
        def _():
            zs[to] = p[half:wide, pl.ds(n * half, half)].astype(BF16)

    def unpack_first(z, full):
        for j in range(2):
            base = j * wide
            lo = pl.ds(base, half)
            hi = pl.ds(base + half, half)
            both = z[j, :half].astype(F32)
            turned = both.T
            mark = z[j, mark_base:first_rows].astype(F32)[:1]
            full[lo, lo] = jnp.where(down >= across, both, turned).astype(BF16)
            full[hi, hi] = jnp.where(
                down < across, both, jnp.where(down == across, mark, turned)
            ).astype(BF16)
            side = z[j, half:edge_base]
            full[lo, hi] = side
            full[hi, lo] = side.T
            for n in range(2):
                full[rows:, pl.ds(base + n * half, half)] = z[
                    j, edge_base + n * edge_rows : edge_base + (n + 1) * edge_rows
                ]

    def unpack_outer(z, full, n):
        far = pl.ds(wide + n * half, half)
        for j in range(2):
            close = pl.ds(j * half, half)
            outer = z[j, fine[1 + n]]
            if j == 0:
                full[far, close] = outer
                full[close, far] = outer.T
            else:
                full[close, far] = outer
                full[far, close] = outer.T

    pending = []

    def emit_copies(when, copies):
        @pl.when(when)
        def _():
            for one in copies:
                one.start()

        pending.append((when, copies))

    def packed_to(where, n, buffer, there, step):
        span = (spans if there[0] == "raw" else fine)[n]
        return copy(
            zs.at[span], buffer.at[c, span],
            place[where]((there, step, n)), recvs((there, n), 1 if there == "r" else 2), at(step),
        )

    parts = (pl.ds(0, wide), pl.ds(wide, wide))

    def map_to(slot, step):
        return [
            copy(
                gk.at[c, parts[n]], gc.at[slot, c, parts[n]],
                place[slot + 1](("map", step, n)), recvs((("map", slot), n), 2), at(step),
            )
            for n in range(2)
        ]

    own0 = g0f[c]
    w = times(dh1f, whole, own0)
    wb = w[:rows].astype(BF16)
    kappa = w[rows:] - h_ref[0].astype(F32)
    pm0[mine] = d_ref[0, mine] + mt(g0f[c], wb)

    raw_targets = (
        (i3 & inner, 2, (-1, -2)),
        (i2 & inner, 1, (-2,)),
        (i1, 0, (-1,)),
    )

    def start_raw(n):
        for when, slot, steps in raw_targets:
            emit_copies(
                when, [packed_to(slot + 1, n, zc.at[slot], ("raw", slot), step) for step in steps]
            )

    pack_first(pm0, kappa)
    emit_copies(i3 & top, [packed_to(3, 0, zy, "y", -1)])
    start_raw(0)
    first[1].wait_recv()
    pm0[other] = d_ref[0, other] + mt(g0f[o], wb)
    for n in range(2):
        pack_outer(pm0, n)
        emit_copies(i3 & top, [packed_to(3, 1 + n, zy, "y", -1)])

    first[2].wait_recv()
    gk[c, :rows] = times(g1f, body, own0).astype(BF16)
    gk[c, rows:] = kappa.astype(BF16)
    ahead_of_late = map_to(2, -2)
    late = map_to(2, -3)
    emit_copies(i3 & inner, map_to(2, -1))
    emit_copies(i2 & inner, map_to(1, -2))
    emit_copies(i1, map_to(0, -1))

    @pl.when(i3 & inner)
    def _():
        for one in ahead_of_late:
            one.start()

    start_raw(1)

    join = swap("gk", gk.at[c], gk.at[c])
    join.start()
    pm1[...] = d_ref[1]
    join.wait_recv()
    m0[...] = gk[...]
    m1[:, :rows] = g1f[...]
    m1[:, rows:] = -dh1f[:, rows:]

    def turn():
        for j in range(2):
            span = pl.ds(j * wide, wide)
            t0[span, :] = m0[j, :rows].T
            t1[span, :] = m1[j, :rows].T

    turn()

    handoffs = {}

    def arrive(when, name, ref, number, relay=None, relayed=None):
        here, there = recvs(name, 2), recvs(name, 2) + 1
        h = o if relayed is None else jnp.where(relayed, c, o)
        onward = copy(ref(h), ref(h), sends(("on", number)), there, mate)
        handoffs[name] = onward

        @pl.when(when)
        def _():
            copy(ref(h), ref(h), sends(("on", number)), here, mate).wait_recv()
            onward.start()

        if relay is not None:
            step, where = relay
            handed = copy(ref(h), ref(h), place[where](("relay", name)), here, at(step))
            emit_copies(when & (i == where), [handed])

    def collect(when, *names):
        @pl.when(when)
        def _():
            for name in names:
                handoffs[name].wait_recv()

    uses = (i0, inner & (i0 | i1), inner & jnp.logical_not(i3))
    relays = (None, (1, 0), (-2, 2))

    def block_arrives(slot, n, when=True):
        arrive(
            uses[slot] & when, (("raw", slot), n), lambda h: zc.at[slot, h, spans[n]],
            (slot % 2) * 4 + n, relays[slot], (None, i1, i0)[slot],
        )

    def map_arrives(slot, when=True):
        for n in range(2):
            arrive(
                uses[slot] & when, (("map", slot), n), lambda h: gc.at[slot, h, parts[n]],
                (slot % 2) * 4 + 2 + n, relays[slot] if slot == 1 else None, i1 if slot == 1 else None,
            )

    def handed_on(slot):
        for n in range(2):
            handoffs[("raw", slot), n].wait_send()
            handoffs[("map", slot), n].wait_send()

    def swaps(slot):
        return [
            copy(xm0.at[slot, c], xm0.at[slot, c], sends("m0"), recvs(("m0", slot)), mate),
            copy(xm1.at[slot, c], xm1.at[slot, c], sends("m1"), recvs(("m1", slot)), mate),
        ]

    maps = ((m0, xm0, t0, pm0, 1.0), (m1, xm1, t1, pm1, -1.0))

    def compose(slot, n):
        m, x, _, _, sign = maps[n]
        own = m[c, :rows]
        edge = mm(fc[rows:], own)
        x[slot, c, rows:] = (m[c, rows:].astype(F32) + sign * edge).astype(BF16)
        x[slot, c, :rows] = times(gc.at[slot], body, own).astype(BF16)
        swaps(slot)[n].start()

    def extend(n):
        m, _, t, p, _ = maps[n]
        wb = mm(fc[:rows], m[c, :rows]).astype(BF16)
        for j in range(2):
            span = pl.ds(j * wide, wide)
            p[span] += mm(t[span, :], wb)

    def settle(slot, n):
        m, x, t, _, _ = maps[n]
        one = swaps(slot)[n]
        one.wait_recv()
        m[...] = x[slot]
        for j in range(2):
            t[pl.ds(j * wide, wide), :] = x[slot, j, :rows].T
        one.wait_send()

    later = i0 & top
    prompt = jnp.logical_not(later)
    started = jnp.logical_not(i3 & top)

    def y_arrives(n, when):
        arrive(
            started & when, ("y", n), lambda h: zy.at[h, fine[n]], (8, 5, 9)[n], None, (i1 & inner) | i3
        )
        ref = zy.at[o, fine[n]]
        emit_copies(
            i0 & inner & when, [copy(ref, ref, place[0](("relay", n)), recvs(("y", n), 2), at(1))]
        )

    def block_whole(slot):
        for n in range(2):
            unpack_outer(zc.at[slot], fc, n)

    def merge(slot):
        raw, drawn = ("raw", slot), ("map", slot)
        use = uses[slot]
        collect(use, (raw, 0), (drawn, 0), (drawn, 1))

        @pl.when(use)
        def _():
            unpack_first(zc.at[slot], fc)
            compose(slot, 0)

            @pl.when(prompt)
            def _():
                compose(slot, 1)

        if slot == 0:
            block_arrives(1, 1)
            block_arrives(0, 1)
            block_arrives(2, 0, i1)
            map_arrives(2, i1)
            block_arrives(2, 1, i1)
        collect(use, (raw, 1))
        if slot == 0:
            y_arrives(0, later)

        @pl.when(use)
        def _():
            block_whole(slot)
            extend(0)

        if slot == 0:
            y_arrives(1, later)

        @pl.when(use)
        def _():
            settle(slot, 0)

            @pl.when(prompt)
            def _():
                extend(1)
                settle(slot, 1)

            handed_on(slot)

    block_arrives(1, 0)
    block_arrives(0, 0)
    map_arrives(1)
    map_arrives(0)
    merge(0)
    merge(1)
    early = jnp.logical_not(i1)
    block_arrives(2, 0, early)
    block_arrives(2, 1, early)
    collect(uses[2], (("raw", 2), 0), (("raw", 2), 1))

    @pl.when(uses[2])
    def _():
        unpack_first(zc.at[2], fc)
        block_whole(2)
        extend(0)
        extend(1)

    map_arrives(2, early)
    collect(uses[2], (("map", 2), 0), (("map", 2), 1))

    @pl.when(uses[2])
    def _():
        compose(2, 0)
        compose(2, 1)

    y_arrives(0, i0 & inner)

    @pl.when(uses[2])
    def _():
        settle(2, 0)
        settle(2, 1)
        handed_on(2)

    @pl.when(i3 & inner)
    def _():
        for one in ahead_of_late:
            one.wait_send()
        for one in late:
            one.start()

    pending.append((i3 & inner, late))

    cov = a_ref[...].astype(BF16)

    def edges(step, sign, m):
        for j in range(2):
            kb[step, j] = sign * mm(full[rows:], m[j, :rows]) + m[j, rows:].astype(F32)
        cross_ref[step] = mm(cov, kb[step, c].astype(BF16))

    @pl.when(jnp.logical_not(started))
    def _():
        full[...] = jnp.zeros_like(full)

    y_arrives(0, jnp.logical_not(i0))
    y_arrives(1, prompt)
    collect(started, ("y", 0))

    @pl.when(started)
    def _():
        unpack_first(zy, full)

    y_arrives(2, True)
    edges(0, 1.0, m0)

    @pl.when(jnp.logical_not(later))
    def _():
        edges(1, -1.0, m1)

    for n in range(2):
        collect(started, ("y", 1 + n))

        @pl.when(started)
        def _():
            unpack_outer(zy, full, n)

    def state(m):
        return mm(full[:rows], m[c, :rows]).astype(BF16)

    leads = i0 & passes
    heads = i2 & top

    def start_y(n):
        emit_copies(heads, [packed_to(2, n, zy, "y", -2)])
        emit_copies(leads, [packed_to(0, n, zy, "y", -4), packed_to(0, n, zr, "r", 1)])

    w = state(m0)
    pm0[mine] += mm(t0[mine, :], w)

    @pl.when(leads | heads)
    def _():
        pack_first(pm0, kb[0, c])

    start_y(0)
    pm0[other] += mm(t0[other, :], w)

    for n in range(2):

        @pl.when(leads | heads)
        def _():
            pack_outer(pm0, n)

        start_y(1 + n)
    emit_copies(heads, [packed_to(2, n, zy, "y", -1) for n in range(3)])
    emit_copies(leads, [packed_to(0, n, zy, "y", -2) for n in range(3)])

    @pl.when(later)
    def _():
        compose(0, 1)
        extend(1)
        settle(0, 1)
        edges(1, -1.0, m1)

    for n in range(3):
        ref = zr.at[o, fine[n]]
        there = zy.at[o, fine[n]]
        forth = copy(ref, there, place[1](("r", n)), recvs(("y", n), 2), at(-2))

        @pl.when(i1 & passes)
        def _():
            copy(ref, ref, place[1](("r", n)), recvs(("r", n)), at(-2)).wait_recv()

        emit_copies(i1 & passes, [forth])

    @pl.when(started)
    def _():
        for n in range(3):
            handoffs["y", n].wait_send()

    for one in first:
        one.wait_send()
    join.wait_send()
    for when, copies in pending:

        @pl.when(when)
        def _():
            for one in copies:
                one.wait_send()


def finish(full, m1, t1, pm0, pm1, kb, cross_ref, out_hbm, cross_hbm, out, store):
    rows, wide = out.shape[1], out.shape[2]
    c = lax.axis_index("col")
    ends = pltpu.make_async_copy(cross_ref, cross_hbm, store.at[4])
    ends.start()
    stores = []

    def emit(step, j, value):
        span = pl.ds(j * wide, wide)
        out[step, span] = value + mt(kb[step, j].astype(BF16), cross_ref[step].astype(BF16))
        one = pltpu.make_async_copy(out.at[step, span], out_hbm.at[step, span], store.at[2 * step + j])
        one.start()
        stores.append(one)

    for j in range(2):
        emit(0, j, pm0[pl.ds(j * wide, wide)])
    w = mm(full[:rows], m1[c, :rows]).astype(BF16)
    for j in range(2):
        span = pl.ds(j * wide, wide)
        emit(1, j, pm1[span] + mm(t1[span, :], w))
    ends.wait()
    for one in stores:
        one.wait()


def shards(diagonal_block_inverse, step_map, arrow_map, arrow_cov):
    count, nodes, wide = diagonal_block_inverse.shape
    effects = arrow_map.shape[1]
    tall = nodes + effects
    packed = 4 * (wide // 2) + 2 * effects + MARK
    vmem = pl.BlockSpec(memory_space=pltpu.VMEM)
    hbm = pl.BlockSpec(memory_space=pltpu.HBM)
    held = pl.pallas_call(
        kernel,
        out_shape=(
            jax.ShapeDtypeStruct((tall, nodes), BF16),
            jax.ShapeDtypeStruct((2, tall, wide), BF16),
            jax.ShapeDtypeStruct((nodes, nodes), BF16),
            jax.ShapeDtypeStruct((nodes, wide), F32),
            jax.ShapeDtypeStruct((nodes, wide), F32),
            jax.ShapeDtypeStruct((count, 2, effects, wide), F32),
            jax.ShapeDtypeStruct((count, effects, wide), F32),
        ),
        in_specs=[hbm] * 4,
        out_specs=(vmem,) * 7,
        scratch_shapes=[
            pltpu.VMEM((count, nodes, wide), F32),
            pltpu.VMEM((count, effects, wide), BF16),
            pltpu.VMEM((effects, effects), F32),
            pltpu.VMEM((2, nodes, wide), BF16),
            pltpu.VMEM((2, nodes, wide), BF16),
            pltpu.VMEM((2, tall, wide), BF16),
            pltpu.VMEM((2, tall, wide), BF16),
            pltpu.VMEM((nodes, nodes), BF16),
            pltpu.VMEM((2, tall, wide), BF16),
            pltpu.VMEM((3, 2, tall, wide), BF16),
            pltpu.VMEM((3, 2, tall, wide), BF16),
            pltpu.VMEM((packed, wide // 2), BF16),
            pltpu.VMEM((2, packed, wide // 2), BF16),
            pltpu.VMEM((2, packed, wide // 2), BF16),
            pltpu.VMEM((3, 2, packed, wide // 2), BF16),
            pltpu.VMEM((3, 2, nodes, wide), BF16),
            pltpu.VMEM((tall, nodes), BF16),
            pltpu.SemaphoreType.DMA((SENDS,)),
            pltpu.SemaphoreType.DMA((RECVS,)),
            pltpu.SemaphoreType.DMA((6,)),
        ],
        compiler_params=pltpu.CompilerParams(
            collective_id=0, has_side_effects=True, vmem_limit_bytes=28 * 1024 * 1024
        ),
    )(*(
        pltpu.with_memory_space_constraint(array, pltpu.HBM)
        for array in (diagonal_block_inverse, step_map, arrow_map, arrow_cov)
    ))
    return pl.pallas_call(
        finish,
        out_shape=(
            jax.ShapeDtypeStruct((count, nodes, wide), F32),
            jax.ShapeDtypeStruct((count, effects, wide), F32),
        ),
        in_specs=[vmem] * 7,
        out_specs=(hbm, hbm),
        scratch_shapes=[
            pltpu.VMEM((count, nodes, wide), F32),
            pltpu.SemaphoreType.DMA((5,)),
        ],
        compiler_params=pltpu.CompilerParams(vmem_limit_bytes=28 * 1024 * 1024),
    )(*held)


def solution(mesh):
    return jax.shard_map(
        shards,
        mesh=mesh,
        in_specs=(
            P(("rep", "tm"), None, "col"),
            P(("rep", "tm"), None, "col"),
            P(("rep", "tm"), None, "col"),
            P("rep", None),
        ),
        out_specs=(P(("rep", "tm"), None, "col"), P(("rep", "tm"), None, "col")),
        check_vma=False,
    )
```

```python
import jax
import jax.numpy as jnp
from jax import lax
from jax.experimental import pallas as pl
from jax.experimental.pallas import tpu as pltpu
from jax.sharding import PartitionSpec as P

MESH = pl.DeviceIdType.MESH
F32 = jnp.float32
BF16 = jnp.bfloat16
SENDS = 32
RECVS = 43
MARK = 16


def mm(left, right):
    return jnp.dot(left, right, preferred_element_type=F32)


def mt(left, right):
    return lax.dot_general(left, right, (((0,), (0,)), ((), ())), preferred_element_type=F32)


class Slots:
    def __init__(self, start, end):
        self.found = {}
        self.free = start
        self.end = end

    def __call__(self, name, width=1):
        if name not in self.found:
            self.found[name] = self.free
            self.free += width
            assert self.free <= self.end
        return self.found[name]


def kernel(
    d_hbm, g_hbm, h_hbm, a_hbm,
    full, m1, t1, pm0, pm1, kb, cross_ref,
    d_ref, h_ref, a_ref, g0f, g1f, dh1f, gk, t0, m0, xm0, xm1,
    zs, zy, zr, zc, gc, fc,
    send, recv, load,
):
    rows = g0f.shape[1]
    wide = g0f.shape[2]
    tall = gk.shape[1]
    half = wide // 2
    edge_rows = tall - rows
    tm = lax.axis_index("tm")
    c = lax.axis_index("col")
    o = 1 - c
    quads = lax.axis_size("tm") // 4
    q = tm // 4
    i = tm % 4
    top = q == quads - 1
    inner = jnp.logical_not(top)
    passes = q > 0
    i0, i1, i2, i3 = (i == n for n in range(4))
    mate = {"col": o}
    recvs = Slots(0, RECVS)
    sends = Slots(0, 16)
    place = [Slots(16, SENDS) for _ in range(4)]

    def at(step):
        return {"tm": tm + step, "col": o}

    def copy(src, dst, sem, sem_there, device):
        return pltpu.make_async_remote_copy(
            src_ref=src, dst_ref=dst, send_sem=send.at[sem], recv_sem=recv.at[sem_there],
            device_id=device, device_id_type=MESH,
        )

    loads = [
        pltpu.make_async_copy(d_hbm.at[1], d_ref.at[1], load.at[0]),
        pltpu.make_async_copy(h_hbm, h_ref, load.at[1]),
        pltpu.make_async_copy(g_hbm.at[0], g0f.at[c], load.at[2]),
        pltpu.make_async_copy(g_hbm.at[1], g1f.at[c], load.at[3]),
        pltpu.make_async_copy(d_hbm.at[0], d_ref.at[0], load.at[4]),
        pltpu.make_async_copy(a_hbm, a_ref, load.at[5]),
    ]
    for one in loads:
        one.start()

    barrier = pltpu.get_barrier_semaphore()
    pl.semaphore_signal(barrier, inc=1, device_id=mate, device_id_type=MESH)

    def greet(when, steps):
        @pl.when(when)
        def _():
            for step in steps:
                pl.semaphore_signal(barrier, inc=1, device_id=at(step), device_id_type=MESH)

    greet(i0, (1, 2))
    greet(i0 & inner, (3, 4))
    greet(i1, (-1,))
    greet(i1 & inner, (2,))
    greet(i1 & top, (1,))
    greet(i2, (1,))
    greet(i2 & inner, (2,))
    greet(i3 & inner, (2,))

    def one_if(flag):
        return jnp.where(flag, 1, 0)

    targets = (
        1 + 2 * one_if(i3 & inner) + one_if(i2 & top) + one_if(i1 & passes) + 2 * one_if(i0 & passes)
    )

    loads[0].wait()
    loads[1].wait()
    dh1f[c, :rows] = d_ref[1].astype(BF16)
    dh1f[c, rows:] = h_ref[1]
    pl.semaphore_wait(barrier, 1 + targets)

    def swap(name, src, dst):
        return copy(src, dst, sends(name), recvs(name), mate)

    first = [
        swap("dh1", dh1f.at[c], dh1f.at[c]),
        swap("g0", g_hbm.at[0], g0f.at[c]),
        swap("g1", g_hbm.at[1], g1f.at[c]),
    ]
    for one in first:
        one.start()
    for one in loads[2:]:
        one.wait()
    first[0].wait_recv()

    def times(left, span, right):
        return mm(jnp.concatenate([left[0, span], left[1, span]], axis=1), right)

    body = pl.ds(0, rows)
    whole = pl.ds(0, tall)
    mine = pl.ds(pl.multiple_of(c * wide, wide), wide)
    other = pl.ds(pl.multiple_of(o * wide, wide), wide)
    edge_base = 2 * half
    mark_base = edge_base + 2 * edge_rows
    first_rows = mark_base + MARK
    top_span = pl.ds(0, first_rows)
    low_span = pl.ds(first_rows, zs.shape[0] - first_rows)
    spans = (top_span, low_span)
    fine = (top_span, pl.ds(first_rows, half), pl.ds(first_rows + half, half))
    across = lax.broadcasted_iota(jnp.int32, (half, half), 1)
    down = lax.broadcasted_iota(jnp.int32, (half, half), 0)

    def pack_first(p, edge):
        r = pl.multiple_of(c * wide, wide)
        one = p[pl.ds(r, half), :half]
        two = p[pl.ds(r + half, half), half:]
        zs[:half] = jnp.where(down >= across, one, two).astype(BF16)
        zs[half:edge_base] = p[pl.ds(r, half), half:].astype(BF16)
        zs[edge_base : edge_base + edge_rows] = edge[:, :half].astype(BF16)
        zs[edge_base + edge_rows : mark_base] = edge[:, half:].astype(BF16)
        mark = jnp.sum(jnp.where(down == across, two, 0.0), axis=0, keepdims=True)
        zs[mark_base:first_rows] = jnp.broadcast_to(mark, (MARK, half)).astype(BF16)

    def pack_outer(p, n):
        to = fine[1 + n]

        @pl.when(c == 0)
        def _():
            zs[to] = p[pl.ds(wide + n * half, half), :half].astype(BF16)

        @pl.when(c == 1)
        def _():
            zs[to] = p[half:wide, pl.ds(n * half, half)].astype(BF16)

    def unpack_first(z, full):
        for j in range(2):
            base = j * wide
            lo = pl.ds(base, half)
            hi = pl.ds(base + half, half)
            both = z[j, :half].astype(F32)
            turned = both.T
            mark = z[j, mark_base:first_rows].astype(F32)[:1]
            full[lo, lo] = jnp.where(down >= across, both, turned).astype(BF16)
            full[hi, hi] = jnp.where(
                down < across, both, jnp.where(down == across, mark, turned)
            ).astype(BF16)
            side = z[j, half:edge_base]
            full[lo, hi] = side
            full[hi, lo] = side.T
            for n in range(2):
                full[rows:, pl.ds(base + n * half, half)] = z[
                    j, edge_base + n * edge_rows : edge_base + (n + 1) * edge_rows
                ]

    def unpack_outer(z, full, n):
        far = pl.ds(wide + n * half, half)
        for j in range(2):
            close = pl.ds(j * half, half)
            outer = z[j, fine[1 + n]]
            if j == 0:
                full[far, close] = outer
                full[close, far] = outer.T
            else:
                full[close, far] = outer
                full[far, close] = outer.T

    pending = []

    def emit_copies(when, copies):
        @pl.when(when)
        def _():
            for one in copies:
                one.start()

        pending.append((when, copies))

    def packed_to(where, n, buffer, there, step):
        span = (spans if there[0] == "raw" else fine)[n]
        return copy(
            zs.at[span], buffer.at[c, span],
            place[where]((there, step, n)), recvs((there, n), 1 if there == "r" else 2), at(step),
        )

    parts = (pl.ds(0, wide), pl.ds(wide, wide))

    def map_to(slot, step):
        return [
            copy(
                gk.at[c, parts[n]], gc.at[slot, c, parts[n]],
                place[slot + 1](("map", step, n)), recvs((("map", slot), n), 2), at(step),
            )
            for n in range(2)
        ]

    own0 = g0f[c]
    w = times(dh1f, whole, own0)
    wb = w[:rows].astype(BF16)
    kappa = w[rows:] - h_ref[0].astype(F32)
    pm0[mine] = d_ref[0, mine] + mt(g0f[c], wb)

    raw_targets = (
        (i3 & inner, 2, (-1, -2)),
        (i2 & inner, 1, (-2,)),
        (i1, 0, (-1,)),
    )

    def start_raw(n):
        for when, slot, steps in raw_targets:
            emit_copies(
                when, [packed_to(slot + 1, n, zc.at[slot], ("raw", slot), step) for step in steps]
            )

    pack_first(pm0, kappa)
    emit_copies(i3 & top, [packed_to(3, 0, zy, "y", -1)])
    start_raw(0)
    first[1].wait_recv()
    pm0[other] = d_ref[0, other] + mt(g0f[o], wb)
    for n in range(2):
        pack_outer(pm0, n)
        emit_copies(i3 & top, [packed_to(3, 1 + n, zy, "y", -1)])

    first[2].wait_recv()
    gk[c, :rows] = times(g1f, body, own0).astype(BF16)
    gk[c, rows:] = kappa.astype(BF16)
    ahead_of_late = map_to(2, -2)
    late = map_to(2, -3)[:1]
    emit_copies(i3 & inner, map_to(2, -1))
    emit_copies(i2 & inner, map_to(1, -2))
    emit_copies(i1, map_to(0, -1))

    @pl.when(i3 & inner)
    def _():
        for one in ahead_of_late:
            one.start()

    start_raw(1)

    join = swap("gk", gk.at[c], gk.at[c])
    join.start()
    pm1[...] = d_ref[1]
    join.wait_recv()
    m0[...] = gk[...]
    m1[:, :rows] = g1f[...]
    m1[:, rows:] = -dh1f[:, rows:]

    def turn():
        for j in range(2):
            span = pl.ds(j * wide, wide)
            t0[span, :] = m0[j, :rows].T
            t1[span, :] = m1[j, :rows].T

    turn()

    handoffs = {}

    def arrive(when, name, ref, number, relay=None, relayed=None):
        here, there = recvs(name, 2), recvs(name, 2) + 1
        h = o if relayed is None else jnp.where(relayed, c, o)
        onward = copy(ref(h), ref(h), sends(("on", number)), there, mate)
        handoffs[name] = onward

        @pl.when(when)
        def _():
            copy(ref(h), ref(h), sends(("on", number)), here, mate).wait_recv()
            onward.start()

        if relay is not None:
            step, where = relay
            handed = copy(ref(h), ref(h), place[where](("relay", name)), here, at(step))
            emit_copies(when & (i == where), [handed])

    def collect(when, *names):
        @pl.when(when)
        def _():
            for name in names:
                handoffs[name].wait_recv()

    uses = (i0, inner & (i0 | i1), inner & jnp.logical_not(i3))
    relays = (None, (1, 0), (-2, 2))

    def block_arrives(slot, n, when=True):
        arrive(
            uses[slot] & when, (("raw", slot), n), lambda h: zc.at[slot, h, spans[n]],
            (slot % 2) * 4 + n, relays[slot], (None, i1, i0)[slot],
        )

    def map_arrives(slot, when=True):
        for n in range(2):
            arrive(
                uses[slot] & when, (("map", slot), n), lambda h: gc.at[slot, h, parts[n]],
                (slot % 2) * 4 + 2 + n, relays[slot] if slot == 1 or n == 1 else None,
                (None, i1, i0 if n == 1 else None)[slot],
            )

    def handed_on(slot):
        for n in range(2):
            handoffs[("raw", slot), n].wait_send()
            handoffs[("map", slot), n].wait_send()

    def swaps(slot):
        return [
            copy(xm0.at[slot, c], xm0.at[slot, c], sends("m0"), recvs(("m0", slot)), mate),
            copy(xm1.at[slot, c], xm1.at[slot, c], sends("m1"), recvs(("m1", slot)), mate),
        ]

    maps = ((m0, xm0, t0, pm0, 1.0), (m1, xm1, t1, pm1, -1.0))

    def compose(slot, n):
        m, x, _, _, sign = maps[n]
        own = m[c, :rows]
        edge = mm(fc[rows:], own)
        x[slot, c, rows:] = (m[c, rows:].astype(F32) + sign * edge).astype(BF16)
        x[slot, c, :rows] = times(gc.at[slot], body, own).astype(BF16)
        swaps(slot)[n].start()

    def extend(n):
        m, _, t, p, _ = maps[n]
        wb = mm(fc[:rows], m[c, :rows]).astype(BF16)
        for j in range(2):
            span = pl.ds(j * wide, wide)
            p[span] += mm(t[span, :], wb)

    def settle(slot, n):
        m, x, t, _, _ = maps[n]
        one = swaps(slot)[n]
        one.wait_recv()
        m[...] = x[slot]
        for j in range(2):
            t[pl.ds(j * wide, wide), :] = x[slot, j, :rows].T
        one.wait_send()

    later = i0 & top
    prompt = jnp.logical_not(later)
    started = jnp.logical_not(i3 & top)

    def y_arrives(n, when):
        arrive(
            started & when, ("y", n), lambda h: zy.at[h, fine[n]], (8, 5, 9)[n], None, (i1 & inner) | i3
        )
        ref = zy.at[o, fine[n]]
        emit_copies(
            i0 & inner & when, [copy(ref, ref, place[0](("relay", n)), recvs(("y", n), 2), at(1))]
        )

    def block_whole(slot):
        for n in range(2):
            unpack_outer(zc.at[slot], fc, n)

    def merge(slot):
        raw, drawn = ("raw", slot), ("map", slot)
        use = uses[slot]
        collect(use, (raw, 0), (drawn, 0), (drawn, 1))

        @pl.when(use)
        def _():
            unpack_first(zc.at[slot], fc)
            compose(slot, 0)

            @pl.when(prompt)
            def _():
                compose(slot, 1)

        if slot == 0:
            block_arrives(1, 1)
            block_arrives(0, 1)
            block_arrives(2, 0, i1)
            map_arrives(2, i1)
            block_arrives(2, 1, i1)
        collect(use, (raw, 1))
        if slot == 0:
            y_arrives(0, later)

        @pl.when(use)
        def _():
            block_whole(slot)
            extend(0)

        if slot == 0:
            y_arrives(1, later)

        @pl.when(use)
        def _():
            settle(slot, 0)

            @pl.when(prompt)
            def _():
                extend(1)
                settle(slot, 1)

            handed_on(slot)

    block_arrives(1, 0)
    block_arrives(0, 0)
    map_arrives(1)
    map_arrives(0)
    merge(0)
    merge(1)
    early = jnp.logical_not(i1)
    block_arrives(2, 0, early)
    map_arrives(2, i2)
    block_arrives(2, 1, early)
    collect(uses[2], (("raw", 2), 0), (("raw", 2), 1))

    @pl.when(uses[2])
    def _():
        unpack_first(zc.at[2], fc)
        block_whole(2)
        extend(0)
        extend(1)

    map_arrives(2, i0)
    collect(uses[2], (("map", 2), 0), (("map", 2), 1))

    @pl.when(uses[2])
    def _():
        compose(2, 0)
        compose(2, 1)

    for n in range(3):
        y_arrives(n, i0 & inner)

    @pl.when(uses[2])
    def _():
        settle(2, 0)
        settle(2, 1)
        handed_on(2)

    @pl.when(i3 & inner)
    def _():
        for one in ahead_of_late:
            one.wait_send()
        for one in late:
            one.start()

    pending.append((i3 & inner, late))

    cov = a_ref[...].astype(BF16)

    def edges(step, sign, m):
        for j in range(2):
            kb[step, j] = sign * mm(full[rows:], m[j, :rows]) + m[j, rows:].astype(F32)
        cross_ref[step] = mm(cov, kb[step, c].astype(BF16))

    @pl.when(jnp.logical_not(started))
    def _():
        full[...] = jnp.zeros_like(full)

    y_arrives(0, jnp.logical_not(i0))
    y_arrives(1, jnp.logical_not(i0))
    collect(started, ("y", 0))

    @pl.when(started)
    def _():
        unpack_first(zy, full)

    y_arrives(2, later | jnp.logical_not(i0))
    edges(0, 1.0, m0)

    @pl.when(jnp.logical_not(later))
    def _():
        edges(1, -1.0, m1)

    for n in range(2):
        collect(started, ("y", 1 + n))

        @pl.when(started)
        def _():
            unpack_outer(zy, full, n)

    def state(m):
        return mm(full[:rows], m[c, :rows]).astype(BF16)

    leads = i0 & passes
    heads = i2 & top

    def start_y(n):
        emit_copies(heads, [packed_to(2, n, zy, "y", -2)])
        emit_copies(leads, [packed_to(0, n, zy, "y", -4), packed_to(0, n, zr, "r", 1)])

    w = state(m0)
    pm0[mine] += mm(t0[mine, :], w)

    @pl.when(leads | heads)
    def _():
        pack_first(pm0, kb[0, c])

    start_y(0)
    pm0[other] += mm(t0[other, :], w)

    for n in range(2):

        @pl.when(leads | heads)
        def _():
            pack_outer(pm0, n)

        start_y(1 + n)
    emit_copies(heads, [packed_to(2, n, zy, "y", -1) for n in range(3)])
    emit_copies(leads, [packed_to(0, n, zy, "y", -2) for n in range(3)])

    @pl.when(later)
    def _():
        compose(0, 1)
        extend(1)
        settle(0, 1)
        edges(1, -1.0, m1)

    for n in range(3):
        ref = zr.at[o, fine[n]]
        there = zy.at[o, fine[n]]
        forth = copy(ref, there, place[1](("r", n)), recvs(("y", n), 2), at(-2))

        @pl.when(i1 & passes)
        def _():
            copy(ref, ref, place[1](("r", n)), recvs(("r", n)), at(-2)).wait_recv()

        emit_copies(i1 & passes, [forth])

    @pl.when(started)
    def _():
        for n in range(3):
            handoffs["y", n].wait_send()

    for one in first:
        one.wait_send()
    join.wait_send()
    for when, copies in pending:

        @pl.when(when)
        def _():
            for one in copies:
                one.wait_send()


def finish(full, m1, t1, pm0, pm1, kb, cross_ref, out_hbm, cross_hbm, out, store):
    rows, wide = out.shape[1], out.shape[2]
    c = lax.axis_index("col")
    ends = pltpu.make_async_copy(cross_ref, cross_hbm, store.at[4])
    ends.start()
    stores = []

    def emit(step, j, value):
        span = pl.ds(j * wide, wide)
        out[step, span] = value + mt(kb[step, j].astype(BF16), cross_ref[step].astype(BF16))
        one = pltpu.make_async_copy(out.at[step, span], out_hbm.at[step, span], store.at[2 * step + j])
        one.start()
        stores.append(one)

    for j in range(2):
        emit(0, j, pm0[pl.ds(j * wide, wide)])
    w = mm(full[:rows], m1[c, :rows]).astype(BF16)
    for j in range(2):
        span = pl.ds(j * wide, wide)
        emit(1, j, pm1[span] + mm(t1[span, :], w))
    ends.wait()
    for one in stores:
        one.wait()


def shards(diagonal_block_inverse, step_map, arrow_map, arrow_cov):
    count, nodes, wide = diagonal_block_inverse.shape
    effects = arrow_map.shape[1]
    tall = nodes + effects
    packed = 4 * (wide // 2) + 2 * effects + MARK
    vmem = pl.BlockSpec(memory_space=pltpu.VMEM)
    hbm = pl.BlockSpec(memory_space=pltpu.HBM)
    held = pl.pallas_call(
        kernel,
        out_shape=(
            jax.ShapeDtypeStruct((tall, nodes), BF16),
            jax.ShapeDtypeStruct((2, tall, wide), BF16),
            jax.ShapeDtypeStruct((nodes, nodes), BF16),
            jax.ShapeDtypeStruct((nodes, wide), F32),
            jax.ShapeDtypeStruct((nodes, wide), F32),
            jax.ShapeDtypeStruct((count, 2, effects, wide), F32),
            jax.ShapeDtypeStruct((count, effects, wide), F32),
        ),
        in_specs=[hbm] * 4,
        out_specs=(vmem,) * 7,
        scratch_shapes=[
            pltpu.VMEM((count, nodes, wide), F32),
            pltpu.VMEM((count, effects, wide), BF16),
            pltpu.VMEM((effects, effects), F32),
            pltpu.VMEM((2, nodes, wide), BF16),
            pltpu.VMEM((2, nodes, wide), BF16),
            pltpu.VMEM((2, tall, wide), BF16),
            pltpu.VMEM((2, tall, wide), BF16),
            pltpu.VMEM((nodes, nodes), BF16),
            pltpu.VMEM((2, tall, wide), BF16),
            pltpu.VMEM((3, 2, tall, wide), BF16),
            pltpu.VMEM((3, 2, tall, wide), BF16),
            pltpu.VMEM((packed, wide // 2), BF16),
            pltpu.VMEM((2, packed, wide // 2), BF16),
            pltpu.VMEM((2, packed, wide // 2), BF16),
            pltpu.VMEM((3, 2, packed, wide // 2), BF16),
            pltpu.VMEM((3, 2, nodes, wide), BF16),
            pltpu.VMEM((tall, nodes), BF16),
            pltpu.SemaphoreType.DMA((SENDS,)),
            pltpu.SemaphoreType.DMA((RECVS,)),
            pltpu.SemaphoreType.DMA((6,)),
        ],
        compiler_params=pltpu.CompilerParams(
            collective_id=0, has_side_effects=True, vmem_limit_bytes=28 * 1024 * 1024
        ),
    )(*(
        pltpu.with_memory_space_constraint(array, pltpu.HBM)
        for array in (diagonal_block_inverse, step_map, arrow_map, arrow_cov)
    ))
    return pl.pallas_call(
        finish,
        out_shape=(
            jax.ShapeDtypeStruct((count, nodes, wide), F32),
            jax.ShapeDtypeStruct((count, effects, wide), F32),
        ),
        in_specs=[vmem] * 7,
        out_specs=(hbm, hbm),
        scratch_shapes=[
            pltpu.VMEM((count, nodes, wide), F32),
            pltpu.SemaphoreType.DMA((5,)),
        ],
        compiler_params=pltpu.CompilerParams(vmem_limit_bytes=28 * 1024 * 1024),
    )(*held)


def solution(mesh):
    return jax.shard_map(
        shards,
        mesh=mesh,
        in_specs=(
            P(("rep", "tm"), None, "col"),
            P(("rep", "tm"), None, "col"),
            P(("rep", "tm"), None, "col"),
            P("rep", None),
        ),
        out_specs=(P(("rep", "tm"), None, "col"), P(("rep", "tm"), None, "col")),
        check_vma=False,
    )
```

```python
import jax
import jax.numpy as jnp
from jax import lax
from jax.experimental import pallas as pl
from jax.experimental.pallas import tpu as pltpu
from jax.sharding import PartitionSpec as P

MESH = pl.DeviceIdType.MESH
F32 = jnp.float32
BF16 = jnp.bfloat16
SENDS = 37
RECVS = 46
MARK = 16


def mm(left, right):
    return jnp.dot(left, right, preferred_element_type=F32)


def mt(left, right):
    return lax.dot_general(left, right, (((0,), (0,)), ((), ())), preferred_element_type=F32)


class Slots:
    def __init__(self, start, end):
        self.found = {}
        self.free = start
        self.end = end

    def __call__(self, name, width=1):
        if name not in self.found:
            self.found[name] = self.free
            self.free += width
            assert self.free <= self.end
        return self.found[name]


def kernel(
    d_hbm, g_hbm, h_hbm, a_hbm,
    w1, t1, pm0, pm1, kb, cross_ref,
    d_ref, h_ref, a_ref, g0f, g1f, dh1f, gk, t0, m0, m1, xm0, xm1,
    zs, zy, zr, zc, gc, fc, full, half_done,
    send, recv, load,
):
    rows = g0f.shape[1]
    wide = g0f.shape[2]
    tall = gk.shape[1]
    half = wide // 2
    edge_rows = tall - rows
    tm = lax.axis_index("tm")
    c = lax.axis_index("col")
    o = 1 - c
    quads = lax.axis_size("tm") // 4
    q = tm // 4
    i = tm % 4
    top = q == quads - 1
    inner = jnp.logical_not(top)
    passes = q > 0
    i0, i1, i2, i3 = (i == n for n in range(4))
    mate = {"col": o}
    recvs = Slots(0, RECVS)
    sends = Slots(0, 17)
    place = [Slots(17, SENDS) for _ in range(4)]

    def at(step):
        return {"tm": tm + step, "col": o}

    def copy(src, dst, sem, sem_there, device):
        return pltpu.make_async_remote_copy(
            src_ref=src, dst_ref=dst, send_sem=send.at[sem], recv_sem=recv.at[sem_there],
            device_id=device, device_id_type=MESH,
        )

    loads = [
        pltpu.make_async_copy(d_hbm.at[1], d_ref.at[1], load.at[0]),
        pltpu.make_async_copy(h_hbm, h_ref, load.at[1]),
        pltpu.make_async_copy(g_hbm.at[0], g0f.at[c], load.at[2]),
        pltpu.make_async_copy(g_hbm.at[1], g1f.at[c], load.at[3]),
        pltpu.make_async_copy(d_hbm.at[0], d_ref.at[0], load.at[4]),
        pltpu.make_async_copy(a_hbm, a_ref, load.at[5]),
    ]
    for one in loads:
        one.start()

    barrier = pltpu.get_barrier_semaphore()
    pl.semaphore_signal(barrier, inc=1, device_id=mate, device_id_type=MESH)

    def greet(when, steps):
        @pl.when(when)
        def _():
            for step in steps:
                pl.semaphore_signal(barrier, inc=1, device_id=at(step), device_id_type=MESH)

    greet(i0, (1, 2))
    greet(i0 & inner, (3, 4))
    greet(i1, (-1,))
    greet(i1 & inner, (2,))
    greet(i1 & top, (1,))
    greet(i2, (1,))
    greet(i2 & inner, (2,))
    greet(i3 & inner, (2,))

    def one_if(flag):
        return jnp.where(flag, 1, 0)

    targets = (
        1 + 2 * one_if(i3 & inner) + one_if(i2 & top) + one_if(i1 & passes) + 2 * one_if(i0 & passes)
    )

    loads[0].wait()
    loads[1].wait()
    dh1f[c, :rows] = d_ref[1].astype(BF16)
    dh1f[c, rows:] = h_ref[1]
    pl.semaphore_wait(barrier, 1 + targets)

    def swap(name, src, dst):
        return copy(src, dst, sends(name), recvs(name), mate)

    first = [
        swap("dh1", dh1f.at[c], dh1f.at[c]),
        swap("g0", g_hbm.at[0], g0f.at[c]),
        swap("g1", g_hbm.at[1], g1f.at[c]),
    ]
    for one in first:
        one.start()
    for one in loads[2:]:
        one.wait()
    first[0].wait_recv()

    def times(left, span, right):
        return mm(jnp.concatenate([left[0, span], left[1, span]], axis=1), right)

    body = pl.ds(0, rows)
    whole = pl.ds(0, tall)
    mine = pl.ds(pl.multiple_of(c * wide, wide), wide)
    other = pl.ds(pl.multiple_of(o * wide, wide), wide)
    edge_base = 2 * half
    mark_base = edge_base + 2 * edge_rows
    first_rows = mark_base + MARK
    top_span = pl.ds(0, first_rows)
    low_span = pl.ds(first_rows, zs.shape[0] - first_rows)
    spans = (top_span, low_span)
    middle = first_rows // 32 * 16
    fine = (
        pl.ds(0, middle), pl.ds(middle, first_rows - middle),
        pl.ds(first_rows, half), pl.ds(first_rows + half, half),
    )
    across = lax.broadcasted_iota(jnp.int32, (half, half), 1)
    down = lax.broadcasted_iota(jnp.int32, (half, half), 0)

    def pack_first(p, edge):
        r = pl.multiple_of(c * wide, wide)
        one = p[pl.ds(r, half), :half]
        two = p[pl.ds(r + half, half), half:]
        zs[:half] = jnp.where(down >= across, one, two).astype(BF16)
        zs[half:edge_base] = p[pl.ds(r, half), half:].astype(BF16)
        zs[edge_base : edge_base + edge_rows] = edge[:, :half].astype(BF16)
        zs[edge_base + edge_rows : mark_base] = edge[:, half:].astype(BF16)
        mark = jnp.sum(jnp.where(down == across, two, 0.0), axis=0, keepdims=True)
        zs[mark_base:first_rows] = jnp.broadcast_to(mark, (MARK, half)).astype(BF16)

    def pack_outer(p, n):
        to = fine[2 + n]

        @pl.when(c == 0)
        def _():
            zs[to] = p[pl.ds(wide + n * half, half), :half].astype(BF16)

        @pl.when(c == 1)
        def _():
            zs[to] = p[half:wide, pl.ds(n * half, half)].astype(BF16)

    def unpack_first(z, full):
        for j in range(2):
            base = j * wide
            lo = pl.ds(base, half)
            hi = pl.ds(base + half, half)
            both = z[j, :half].astype(F32)
            turned = both.T
            mark = z[j, mark_base:first_rows].astype(F32)[:1]
            full[lo, lo] = jnp.where(down >= across, both, turned).astype(BF16)
            full[hi, hi] = jnp.where(
                down < across, both, jnp.where(down == across, mark, turned)
            ).astype(BF16)
            side = z[j, half:edge_base]
            full[lo, hi] = side
            full[hi, lo] = side.T
            for n in range(2):
                full[rows:, pl.ds(base + n * half, half)] = z[
                    j, edge_base + n * edge_rows : edge_base + (n + 1) * edge_rows
                ]

    def unpack_outer(z, full, n):
        far = pl.ds(wide + n * half, half)
        for j in range(2):
            close = pl.ds(j * half, half)
            outer = z[j, fine[2 + n]]
            if j == 0:
                full[far, close] = outer
                full[close, far] = outer.T
            else:
                full[close, far] = outer
                full[far, close] = outer.T

    pending = []

    def emit_copies(when, copies):
        @pl.when(when)
        def _():
            for one in copies:
                one.start()

        pending.append((when, copies))

    def packed_to(where, n, buffer, there, step):
        span = (spans if there[0] == "raw" else fine)[n]
        return copy(
            zs.at[span], buffer.at[c, span],
            place[where]((there, step, n)), recvs((there, n), 1 if there == "r" else 2), at(step),
        )

    parts = (pl.ds(0, wide), pl.ds(wide, wide))

    def map_to(slot, step):
        return [
            copy(
                gk.at[c, parts[n]], gc.at[slot, c, parts[n]],
                place[slot + 1](("map", step, n)), recvs((("map", slot), n), 2), at(step),
            )
            for n in range(2)
        ]

    own0 = g0f[c]
    w = times(dh1f, whole, own0)
    wb = w[:rows].astype(BF16)
    kappa = w[rows:] - h_ref[0].astype(F32)
    pm0[mine] = d_ref[0, mine] + mt(g0f[c], wb)

    raw_targets = (
        (i3 & inner, 2, (-1, -2)),
        (i2 & inner, 1, (-2,)),
        (i1, 0, (-1,)),
    )

    def start_raw(n):
        for when, slot, steps in raw_targets:
            emit_copies(
                when, [packed_to(slot + 1, n, zc.at[slot], ("raw", slot), step) for step in steps]
            )

    pack_first(pm0, kappa)
    emit_copies(i3 & top, [packed_to(3, n, zy, "y", -1) for n in range(2)])
    start_raw(0)
    first[1].wait_recv()
    pm0[other] = d_ref[0, other] + mt(g0f[o], wb)
    for n in range(2):
        pack_outer(pm0, n)
        emit_copies(i3 & top, [packed_to(3, 2 + n, zy, "y", -1)])

    first[2].wait_recv()
    gk[c, :rows] = times(g1f, body, own0).astype(BF16)
    gk[c, rows:] = kappa.astype(BF16)
    ahead_of_late = map_to(2, -2)
    late = map_to(2, -3)[:1]
    emit_copies(i3 & inner, map_to(2, -1))
    emit_copies(i2 & inner, map_to(1, -2))
    emit_copies(i1, map_to(0, -1))

    @pl.when(i3 & inner)
    def _():
        for one in ahead_of_late:
            one.start()

    start_raw(1)

    join = swap("gk", gk.at[c], gk.at[c])
    join.start()
    pm1[...] = d_ref[1]
    join.wait_recv()
    m0[...] = gk[...]
    m1[:, :rows] = g1f[...]
    m1[:, rows:] = -dh1f[:, rows:]

    def turn():
        for j in range(2):
            span = pl.ds(j * wide, wide)
            t0[span, :] = m0[j, :rows].T
            t1[span, :] = m1[j, :rows].T

    turn()

    handoffs = {}

    def arrive(when, name, ref, number, relay=None, relayed=None):
        here, there = recvs(name, 2), recvs(name, 2) + 1
        h = o if relayed is None else jnp.where(relayed, c, o)
        onward = copy(ref(h), ref(h), sends(("on", number)), there, mate)
        handoffs[name] = onward

        @pl.when(when)
        def _():
            copy(ref(h), ref(h), sends(("on", number)), here, mate).wait_recv()
            onward.start()

        if relay is not None:
            step, where = relay
            handed = copy(ref(h), ref(h), place[where](("relay", name)), here, at(step))
            emit_copies(when & (i == where), [handed])

    def collect(when, *names):
        @pl.when(when)
        def _():
            for name in names:
                handoffs[name].wait_recv()

    uses = (i0, inner & (i0 | i1), inner & jnp.logical_not(i3))
    relays = (None, (1, 0), (-2, 2))

    def block_arrives(slot, n, when=True):
        arrive(
            uses[slot] & when, (("raw", slot), n), lambda h: zc.at[slot, h, spans[n]],
            (slot % 2) * 4 + n, relays[slot], (None, i1, i0)[slot],
        )

    def map_arrives(slot, when=True):
        for n in range(2):
            arrive(
                uses[slot] & when, (("map", slot), n), lambda h: gc.at[slot, h, parts[n]],
                (slot % 2) * 4 + 2 + n, relays[slot] if slot == 1 or n == 1 else None,
                (None, i1, i0 if n == 1 else None)[slot],
            )

    def handed_on(slot):
        for n in range(2):
            handoffs[("raw", slot), n].wait_send()
            handoffs[("map", slot), n].wait_send()

    def swaps(slot):
        return [
            copy(xm0.at[slot, c], xm0.at[slot, c], sends("m0"), recvs(("m0", slot)), mate),
            copy(xm1.at[slot, c], xm1.at[slot, c], sends("m1"), recvs(("m1", slot)), mate),
        ]

    maps = ((m0, xm0, t0, pm0, 1.0), (m1, xm1, t1, pm1, -1.0))

    def compose(slot, n):
        m, x, _, _, sign = maps[n]
        own = m[c, :rows]
        edge = mm(fc[rows:], own)
        x[slot, c, rows:] = (m[c, rows:].astype(F32) + sign * edge).astype(BF16)
        x[slot, c, :rows] = times(gc.at[slot], body, own).astype(BF16)
        swaps(slot)[n].start()

    def extend(n):
        m, _, t, p, _ = maps[n]
        wb = mm(fc[:rows], m[c, :rows]).astype(BF16)
        for j in range(2):
            span = pl.ds(j * wide, wide)
            p[span] += mm(t[span, :], wb)

    def settle(slot, n):
        m, x, t, _, _ = maps[n]
        one = swaps(slot)[n]
        one.wait_recv()
        m[...] = x[slot]
        for j in range(2):
            t[pl.ds(j * wide, wide), :] = x[slot, j, :rows].T
        one.wait_send()

    later = i0 & top
    prompt = jnp.logical_not(later)
    started = jnp.logical_not(i3 & top)

    def y_arrives(n, when):
        arrive(
            started & when, ("y", n), lambda h: zy.at[h, fine[n]], (8, 9, 5, 10)[n], None, (i1 & inner) | i3
        )
        ref = zy.at[o, fine[n]]
        emit_copies(
            i0 & inner & when, [copy(ref, ref, place[0](("relay", n)), recvs(("y", n), 2), at(1))]
        )

    def block_whole(slot):
        for n in range(2):
            unpack_outer(zc.at[slot], fc, n)

    def merge(slot):
        raw, drawn = ("raw", slot), ("map", slot)
        use = uses[slot]
        collect(use, (raw, 0), (drawn, 0), (drawn, 1))

        @pl.when(use)
        def _():
            unpack_first(zc.at[slot], fc)
            compose(slot, 0)

            @pl.when(prompt)
            def _():
                compose(slot, 1)

        if slot == 0:
            block_arrives(1, 1)
            block_arrives(0, 1)
            block_arrives(2, 0, i1)
            map_arrives(2, i1)
            block_arrives(2, 1, i1)
        collect(use, (raw, 1))
        if slot == 0:
            y_arrives(0, later)
            y_arrives(1, later)

        @pl.when(use)
        def _():
            block_whole(slot)
            extend(0)

        if slot == 0:
            y_arrives(2, later)

        @pl.when(use)
        def _():
            settle(slot, 0)

            @pl.when(prompt)
            def _():
                extend(1)
                settle(slot, 1)

            handed_on(slot)

    block_arrives(1, 0)
    block_arrives(0, 0)
    map_arrives(1)
    map_arrives(0)
    merge(0)
    merge(1)
    early = jnp.logical_not(i1)
    block_arrives(2, 0, early)
    map_arrives(2, i2)
    block_arrives(2, 1, early)
    collect(uses[2], (("raw", 2), 0), (("raw", 2), 1))

    @pl.when(uses[2])
    def _():
        unpack_first(zc.at[2], fc)
        block_whole(2)
        extend(0)
        extend(1)

    map_arrives(2, i0)
    collect(uses[2], (("map", 2), 0), (("map", 2), 1))

    @pl.when(uses[2])
    def _():
        compose(2, 0)
        compose(2, 1)

    for n in range(4):
        y_arrives(n, i0 & inner)

    @pl.when(uses[2])
    def _():
        settle(2, 0)
        settle(2, 1)
        handed_on(2)

    @pl.when(i3 & inner)
    def _():
        for one in ahead_of_late:
            one.wait_send()
        for one in late:
            one.start()

    pending.append((i3 & inner, late))

    cov = a_ref[...].astype(BF16)

    def edges(step, sign, m):
        for j in range(2):
            kb[step, j] = sign * mm(full[rows:], m[j, :rows]) + m[j, rows:].astype(F32)
        cross_ref[step] = mm(cov, kb[step, c].astype(BF16))

    @pl.when(jnp.logical_not(started))
    def _():
        full[...] = jnp.zeros_like(full)

    for n in range(3):
        y_arrives(n, jnp.logical_not(i0))
    collect(started, ("y", 0), ("y", 1))

    @pl.when(started)
    def _():
        unpack_first(zy, full)

    def close(m, n):
        return mm(full[parts[n], parts[n]], m[c, parts[n]])

    def far(m, n):
        return mm(full[parts[n], parts[1 - n]], m[c, parts[1 - n]])

    y_arrives(3, later | jnp.logical_not(i0))
    edges(0, 1.0, m0)
    begun = [close(m0, n) for n in range(2)]

    @pl.when(prompt)
    def _():
        edges(1, -1.0, m1)
        for n in range(2):
            half_done[parts[n]] = close(m1, n)

    for n in range(2):
        collect(started, ("y", 2 + n))

        @pl.when(started)
        def _():
            unpack_outer(zy, full, n)

    leads = i0 & passes
    heads = i2 & top

    def start_y(n):
        emit_copies(heads, [packed_to(2, n, zy, "y", -2)])
        emit_copies(leads, [packed_to(0, n, zy, "y", -4), packed_to(0, n, zr, "r", 1)])

    w = jnp.concatenate([begun[n] + far(m0, n) for n in range(2)], axis=0).astype(BF16)
    pm0[mine] += mm(t0[mine, :], w)

    @pl.when(leads | heads)
    def _():
        pack_first(pm0, kb[0, c])

    start_y(0)
    start_y(1)
    pm0[other] += mm(t0[other, :], w)

    for n in range(2):

        @pl.when(leads | heads)
        def _():
            pack_outer(pm0, n)

        start_y(2 + n)
    emit_copies(heads, [packed_to(2, n, zy, "y", -1) for n in range(4)])
    emit_copies(leads, [packed_to(0, n, zy, "y", -2) for n in range(4)])

    @pl.when(later)
    def _():
        compose(0, 1)
        extend(1)
        settle(0, 1)
        edges(1, -1.0, m1)
        for n in range(2):
            half_done[parts[n]] = close(m1, n)

    for n in range(2):
        w1[parts[n]] = (half_done[parts[n]] + far(m1, n)).astype(BF16)

    for n in range(4):
        ref = zr.at[o, fine[n]]
        there = zy.at[o, fine[n]]
        forth = copy(ref, there, place[1](("r", n)), recvs(("y", n), 2), at(-2))

        @pl.when(i1 & passes)
        def _():
            copy(ref, ref, place[1](("r", n)), recvs(("r", n)), at(-2)).wait_recv()

        emit_copies(i1 & passes, [forth])

    @pl.when(started)
    def _():
        for n in range(4):
            handoffs["y", n].wait_send()

    for one in first:
        one.wait_send()
    join.wait_send()
    for when, copies in pending:

        @pl.when(when)
        def _():
            for one in copies:
                one.wait_send()


def finish(w1, t1, pm0, pm1, kb, cross_ref, out_hbm, cross_hbm, out, store):
    wide = out.shape[2]
    ends = pltpu.make_async_copy(cross_ref, cross_hbm, store.at[4])
    ends.start()
    stores = []

    def emit(step, j, value):
        span = pl.ds(j * wide, wide)
        out[step, span] = value + mt(kb[step, j].astype(BF16), cross_ref[step].astype(BF16))
        one = pltpu.make_async_copy(out.at[step, span], out_hbm.at[step, span], store.at[2 * step + j])
        one.start()
        stores.append(one)

    for j in range(2):
        emit(0, j, pm0[pl.ds(j * wide, wide)])
    for j in range(2):
        span = pl.ds(j * wide, wide)
        emit(1, j, pm1[span] + mm(t1[span, :], w1[...]))
    ends.wait()
    for one in stores:
        one.wait()


def shards(diagonal_block_inverse, step_map, arrow_map, arrow_cov):
    count, nodes, wide = diagonal_block_inverse.shape
    effects = arrow_map.shape[1]
    tall = nodes + effects
    packed = 4 * (wide // 2) + 2 * effects + MARK
    vmem = pl.BlockSpec(memory_space=pltpu.VMEM)
    hbm = pl.BlockSpec(memory_space=pltpu.HBM)
    held = pl.pallas_call(
        kernel,
        out_shape=(
            jax.ShapeDtypeStruct((nodes, wide), BF16),
            jax.ShapeDtypeStruct((nodes, nodes), BF16),
            jax.ShapeDtypeStruct((nodes, wide), F32),
            jax.ShapeDtypeStruct((nodes, wide), F32),
            jax.ShapeDtypeStruct((count, 2, effects, wide), F32),
            jax.ShapeDtypeStruct((count, effects, wide), F32),
        ),
        in_specs=[hbm] * 4,
        out_specs=(vmem,) * 6,
        scratch_shapes=[
            pltpu.VMEM((count, nodes, wide), F32),
            pltpu.VMEM((count, effects, wide), BF16),
            pltpu.VMEM((effects, effects), F32),
            pltpu.VMEM((2, nodes, wide), BF16),
            pltpu.VMEM((2, nodes, wide), BF16),
            pltpu.VMEM((2, tall, wide), BF16),
            pltpu.VMEM((2, tall, wide), BF16),
            pltpu.VMEM((nodes, nodes), BF16),
            pltpu.VMEM((2, tall, wide), BF16),
            pltpu.VMEM((2, tall, wide), BF16),
            pltpu.VMEM((3, 2, tall, wide), BF16),
            pltpu.VMEM((3, 2, tall, wide), BF16),
            pltpu.VMEM((packed, wide // 2), BF16),
            pltpu.VMEM((2, packed, wide // 2), BF16),
            pltpu.VMEM((2, packed, wide // 2), BF16),
            pltpu.VMEM((3, 2, packed, wide // 2), BF16),
            pltpu.VMEM((3, 2, nodes, wide), BF16),
            pltpu.VMEM((tall, nodes), BF16),
            pltpu.VMEM((tall, nodes), BF16),
            pltpu.VMEM((nodes, wide), F32),
            pltpu.SemaphoreType.DMA((SENDS,)),
            pltpu.SemaphoreType.DMA((RECVS,)),
            pltpu.SemaphoreType.DMA((6,)),
        ],
        compiler_params=pltpu.CompilerParams(
            collective_id=0, has_side_effects=True, vmem_limit_bytes=28 * 1024 * 1024
        ),
    )(*(
        pltpu.with_memory_space_constraint(array, pltpu.HBM)
        for array in (diagonal_block_inverse, step_map, arrow_map, arrow_cov)
    ))
    return pl.pallas_call(
        finish,
        out_shape=(
            jax.ShapeDtypeStruct((count, nodes, wide), F32),
            jax.ShapeDtypeStruct((count, effects, wide), F32),
        ),
        in_specs=[vmem] * 6,
        out_specs=(hbm, hbm),
        scratch_shapes=[
            pltpu.VMEM((count, nodes, wide), F32),
            pltpu.SemaphoreType.DMA((5,)),
        ],
        compiler_params=pltpu.CompilerParams(vmem_limit_bytes=28 * 1024 * 1024),
    )(*held)


def solution(mesh):
    return jax.shard_map(
        shards,
        mesh=mesh,
        in_specs=(
            P(("rep", "tm"), None, "col"),
            P(("rep", "tm"), None, "col"),
            P(("rep", "tm"), None, "col"),
            P("rep", None),
        ),
        out_specs=(P(("rep", "tm"), None, "col"), P(("rep", "tm"), None, "col")),
        check_vma=False,
    )
```

```python
import jax
import jax.numpy as jnp
from jax import lax
from jax.experimental import pallas as pl
from jax.experimental.pallas import tpu as pltpu
from jax.sharding import PartitionSpec as P

MESH = pl.DeviceIdType.MESH
F32 = jnp.float32
BF16 = jnp.bfloat16
SENDS = 37
RECVS = 46
MARK = 16


def mm(left, right):
    return jnp.dot(left, right, preferred_element_type=F32)


def mt(left, right):
    return lax.dot_general(left, right, (((0,), (0,)), ((), ())), preferred_element_type=F32)


class Slots:
    def __init__(self, start, end):
        self.found = {}
        self.free = start
        self.end = end

    def __call__(self, name, width=1):
        if name not in self.found:
            self.found[name] = self.free
            self.free += width
            assert self.free <= self.end
        return self.found[name]


def kernel(
    d_hbm, g_hbm, h_hbm, a_hbm,
    w1, t1, pm0, pm1, kb, cross_ref,
    d_ref, h_ref, a_ref, g0f, g1f, dh1f, gk, t0, m0, m1, xm0, xm1,
    zs, zy, zr, zc, gc, fc, full, half_done,
    send, recv, load,
):
    rows = g0f.shape[1]
    wide = g0f.shape[2]
    tall = gk.shape[1]
    half = wide // 2
    edge_rows = tall - rows
    tm = lax.axis_index("tm")
    c = lax.axis_index("col")
    o = 1 - c
    quads = lax.axis_size("tm") // 4
    q = tm // 4
    i = tm % 4
    top = q == quads - 1
    inner = jnp.logical_not(top)
    passes = q > 0
    i0, i1, i2, i3 = (i == n for n in range(4))
    mate = {"col": o}
    recvs = Slots(0, RECVS)
    sends = Slots(0, 17)
    place = [Slots(17, SENDS) for _ in range(4)]

    def at(step):
        return {"tm": tm + step, "col": o}

    def copy(src, dst, sem, sem_there, device):
        return pltpu.make_async_remote_copy(
            src_ref=src, dst_ref=dst, send_sem=send.at[sem], recv_sem=recv.at[sem_there],
            device_id=device, device_id_type=MESH,
        )

    loads = [
        pltpu.make_async_copy(d_hbm.at[1], d_ref.at[1], load.at[0]),
        pltpu.make_async_copy(h_hbm, h_ref, load.at[1]),
        pltpu.make_async_copy(g_hbm.at[0], g0f.at[c], load.at[2]),
        pltpu.make_async_copy(g_hbm.at[1], g1f.at[c], load.at[3]),
        pltpu.make_async_copy(d_hbm.at[0], d_ref.at[0], load.at[4]),
        pltpu.make_async_copy(a_hbm, a_ref, load.at[5]),
    ]
    for one in loads:
        one.start()

    barrier = pltpu.get_barrier_semaphore()
    pl.semaphore_signal(barrier, inc=1, device_id=mate, device_id_type=MESH)

    def greet(when, steps):
        @pl.when(when)
        def _():
            for step in steps:
                pl.semaphore_signal(barrier, inc=1, device_id=at(step), device_id_type=MESH)

    greet(i0, (1, 2))
    greet(i0 & inner, (3, 4))
    greet(i1, (-1,))
    greet(i1 & inner, (2,))
    greet(i1 & top, (1,))
    greet(i2, (1,))
    greet(i2 & inner, (2,))
    greet(i3 & inner, (2,))

    def one_if(flag):
        return jnp.where(flag, 1, 0)

    targets = (
        1 + 2 * one_if(i3 & inner) + one_if(i2 & top) + one_if(i1 & passes) + 2 * one_if(i0 & passes)
    )

    loads[0].wait()
    loads[1].wait()
    dh1f[c, :rows] = d_ref[1].astype(BF16)
    dh1f[c, rows:] = h_ref[1]
    pl.semaphore_wait(barrier, 1 + targets)

    def swap(name, src, dst):
        return copy(src, dst, sends(name), recvs(name), mate)

    first = [
        swap("dh1", dh1f.at[c], dh1f.at[c]),
        swap("g0", g_hbm.at[0], g0f.at[c]),
        swap("g1", g_hbm.at[1], g1f.at[c]),
    ]
    for one in first:
        one.start()
    for one in loads[2:]:
        one.wait()

    def times(left, span, right):
        return mm(jnp.concatenate([left[0, span], left[1, span]], axis=1), right)

    body = pl.ds(0, rows)
    mine = pl.ds(pl.multiple_of(c * wide, wide), wide)
    other = pl.ds(pl.multiple_of(o * wide, wide), wide)
    edge_base = 2 * half
    mark_base = edge_base + 2 * edge_rows
    first_rows = mark_base + MARK
    top_span = pl.ds(0, first_rows)
    low_span = pl.ds(first_rows, zs.shape[0] - first_rows)
    spans = (top_span, low_span)
    middle = first_rows // 32 * 16
    fine = (
        pl.ds(0, middle), pl.ds(middle, first_rows - middle),
        pl.ds(first_rows, half), pl.ds(first_rows + half, half),
    )
    across = lax.broadcasted_iota(jnp.int32, (half, half), 1)
    down = lax.broadcasted_iota(jnp.int32, (half, half), 0)

    def pack_first(p, edge):
        r = pl.multiple_of(c * wide, wide)
        one = p[pl.ds(r, half), :half]
        two = p[pl.ds(r + half, half), half:]
        zs[:half] = jnp.where(down >= across, one, two).astype(BF16)
        zs[half:edge_base] = p[pl.ds(r, half), half:].astype(BF16)
        zs[edge_base : edge_base + edge_rows] = edge[:, :half].astype(BF16)
        zs[edge_base + edge_rows : mark_base] = edge[:, half:].astype(BF16)
        mark = jnp.sum(jnp.where(down == across, two, 0.0), axis=0, keepdims=True)
        zs[mark_base:first_rows] = jnp.broadcast_to(mark, (MARK, half)).astype(BF16)

    def pack_outer(p, n):
        to = fine[2 + n]

        @pl.when(c == 0)
        def _():
            zs[to] = p[pl.ds(wide + n * half, half), :half].astype(BF16)

        @pl.when(c == 1)
        def _():
            zs[to] = p[half:wide, pl.ds(n * half, half)].astype(BF16)

    def unpack_first(z, full):
        for j in range(2):
            base = j * wide
            lo = pl.ds(base, half)
            hi = pl.ds(base + half, half)
            both = z[j, :half].astype(F32)
            turned = both.T
            mark = z[j, mark_base:first_rows].astype(F32)[:1]
            full[lo, lo] = jnp.where(down >= across, both, turned).astype(BF16)
            full[hi, hi] = jnp.where(
                down < across, both, jnp.where(down == across, mark, turned)
            ).astype(BF16)
            side = z[j, half:edge_base]
            full[lo, hi] = side
            full[hi, lo] = side.T
            for n in range(2):
                full[rows:, pl.ds(base + n * half, half)] = z[
                    j, edge_base + n * edge_rows : edge_base + (n + 1) * edge_rows
                ]

    def unpack_outer(z, full, n):
        far = pl.ds(wide + n * half, half)
        for j in range(2):
            close = pl.ds(j * half, half)
            outer = z[j, fine[2 + n]]
            if j == 0:
                full[far, close] = outer
                full[close, far] = outer.T
            else:
                full[close, far] = outer
                full[far, close] = outer.T

    pending = []

    def emit_copies(when, copies):
        @pl.when(when)
        def _():
            for one in copies:
                one.start()

        pending.append((when, copies))

    def packed_to(where, n, buffer, there, step):
        span = (spans if there[0] == "raw" else fine)[n]
        return copy(
            zs.at[span], buffer.at[c, span],
            place[where]((there, step, n)), recvs((there, n), 1 if there == "r" else 2), at(step),
        )

    parts = (pl.ds(0, wide), pl.ds(wide, wide))

    def map_to(slot, step):
        return [
            copy(
                gk.at[c, parts[n]], gc.at[slot, c, parts[n]],
                place[slot + 1](("map", step, n)), recvs((("map", slot), n), 2), at(step),
            )
            for n in range(2)
        ]

    own0 = g0f[c]
    w = mm(dh1f[c], g0f[c, mine])
    first[0].wait_recv()
    w += mm(dh1f[o], g0f[c, other])
    wb = w[:rows].astype(BF16)
    kappa = w[rows:] - h_ref[0].astype(F32)
    pm0[mine] = d_ref[0, mine] + mt(g0f[c], wb)

    raw_targets = (
        (i3 & inner, 2, (-1, -2)),
        (i2 & inner, 1, (-2,)),
        (i1, 0, (-1,)),
    )

    def start_raw(n):
        for when, slot, steps in raw_targets:
            emit_copies(
                when, [packed_to(slot + 1, n, zc.at[slot], ("raw", slot), step) for step in steps]
            )

    pack_first(pm0, kappa)
    emit_copies(i3 & top, [packed_to(3, n, zy, "y", -1) for n in range(2)])
    start_raw(0)
    first[1].wait_recv()
    pm0[other] = d_ref[0, other] + mt(g0f[o], wb)
    for n in range(2):
        pack_outer(pm0, n)
        emit_copies(i3 & top, [packed_to(3, 2 + n, zy, "y", -1)])

    first[2].wait_recv()
    gk[c, :rows] = times(g1f, body, own0).astype(BF16)
    gk[c, rows:] = kappa.astype(BF16)
    ahead_of_late = map_to(2, -2)
    late = map_to(2, -3)[:1]
    emit_copies(i3 & inner, map_to(2, -1))
    emit_copies(i2 & inner, map_to(1, -2))
    emit_copies(i1, map_to(0, -1))

    @pl.when(i3 & inner)
    def _():
        for one in ahead_of_late:
            one.start()

    start_raw(1)

    join = swap("gk", gk.at[c], gk.at[c])
    join.start()
    pm1[...] = d_ref[1]
    join.wait_recv()
    m0[...] = gk[...]
    m1[:, :rows] = g1f[...]
    m1[:, rows:] = -dh1f[:, rows:]

    def turn():
        for j in range(2):
            span = pl.ds(j * wide, wide)
            t0[span, :] = m0[j, :rows].T
            t1[span, :] = m1[j, :rows].T

    turn()

    handoffs = {}

    def arrive(when, name, ref, number, relay=None, relayed=None):
        here, there = recvs(name, 2), recvs(name, 2) + 1
        h = o if relayed is None else jnp.where(relayed, c, o)
        onward = copy(ref(h), ref(h), sends(("on", number)), there, mate)
        handoffs[name] = onward

        @pl.when(when)
        def _():
            copy(ref(h), ref(h), sends(("on", number)), here, mate).wait_recv()
            onward.start()

        if relay is not None:
            step, where = relay
            handed = copy(ref(h), ref(h), place[where](("relay", name)), here, at(step))
            emit_copies(when & (i == where), [handed])

    def collect(when, *names):
        @pl.when(when)
        def _():
            for name in names:
                handoffs[name].wait_recv()

    uses = (i0, inner & (i0 | i1), inner & jnp.logical_not(i3))
    relays = (None, (1, 0), (-2, 2))

    def block_arrives(slot, n, when=True):
        arrive(
            uses[slot] & when, (("raw", slot), n), lambda h: zc.at[slot, h, spans[n]],
            (slot % 2) * 4 + n, relays[slot], (None, i1, i0)[slot],
        )

    def map_arrives(slot, when=True):
        for n in range(2):
            arrive(
                uses[slot] & when, (("map", slot), n), lambda h: gc.at[slot, h, parts[n]],
                (slot % 2) * 4 + 2 + n, relays[slot] if slot == 1 or n == 1 else None,
                (None, i1, i0 if n == 1 else None)[slot],
            )

    def handed_on(slot):
        for n in range(2):
            handoffs[("raw", slot), n].wait_send()
            handoffs[("map", slot), n].wait_send()

    def swaps(slot):
        return [
            copy(xm0.at[slot, c], xm0.at[slot, c], sends("m0"), recvs(("m0", slot)), mate),
            copy(xm1.at[slot, c], xm1.at[slot, c], sends("m1"), recvs(("m1", slot)), mate),
        ]

    maps = ((m0, xm0, t0, pm0, 1.0), (m1, xm1, t1, pm1, -1.0))

    def compose(slot, n):
        m, x, _, _, sign = maps[n]
        own = m[c, :rows]
        edge = mm(fc[rows:], own)
        x[slot, c, rows:] = (m[c, rows:].astype(F32) + sign * edge).astype(BF16)
        x[slot, c, :rows] = times(gc.at[slot], body, own).astype(BF16)
        swaps(slot)[n].start()

    def extend(n):
        m, _, t, p, _ = maps[n]
        wb = mm(fc[:rows], m[c, :rows]).astype(BF16)
        for j in range(2):
            span = pl.ds(j * wide, wide)
            p[span] += mm(t[span, :], wb)

    def settle(slot, n):
        m, x, t, _, _ = maps[n]
        one = swaps(slot)[n]
        one.wait_recv()
        m[...] = x[slot]
        for j in range(2):
            t[pl.ds(j * wide, wide), :] = x[slot, j, :rows].T
        one.wait_send()

    later = i0 & top
    prompt = jnp.logical_not(later)
    started = jnp.logical_not(i3 & top)

    def y_arrives(n, when):
        arrive(
            started & when, ("y", n), lambda h: zy.at[h, fine[n]], (8, 9, 5, 10)[n], None, (i1 & inner) | i3
        )
        ref = zy.at[o, fine[n]]
        emit_copies(
            i0 & inner & when, [copy(ref, ref, place[0](("relay", n)), recvs(("y", n), 2), at(1))]
        )

    def block_whole(slot):
        for n in range(2):
            unpack_outer(zc.at[slot], fc, n)

    def merge(slot):
        raw, drawn = ("raw", slot), ("map", slot)
        use = uses[slot]
        collect(use, (raw, 0), (drawn, 0), (drawn, 1))

        @pl.when(use)
        def _():
            unpack_first(zc.at[slot], fc)
            compose(slot, 0)

            @pl.when(prompt)
            def _():
                compose(slot, 1)

        if slot == 0:
            block_arrives(1, 1)
            block_arrives(0, 1)
            block_arrives(2, 0, i1)
            map_arrives(2, i1)
            block_arrives(2, 1, i1)
        collect(use, (raw, 1))
        if slot == 0:
            y_arrives(0, later)
            y_arrives(1, later)

        @pl.when(use)
        def _():
            block_whole(slot)
            extend(0)

        if slot == 0:
            y_arrives(2, later)

        @pl.when(use)
        def _():
            settle(slot, 0)

            @pl.when(prompt)
            def _():
                extend(1)
                settle(slot, 1)

            handed_on(slot)

    block_arrives(1, 0)
    block_arrives(0, 0)
    map_arrives(1)
    map_arrives(0)
    merge(0)
    merge(1)
    early = jnp.logical_not(i1)
    block_arrives(2, 0, early)
    map_arrives(2, i2)
    block_arrives(2, 1, early)
    collect(uses[2], (("raw", 2), 0), (("raw", 2), 1))

    @pl.when(uses[2])
    def _():
        unpack_first(zc.at[2], fc)
        block_whole(2)
        extend(0)
        extend(1)

    for n in range(2):
        y_arrives(n, i0 & inner)
    map_arrives(2, i0)
    collect(uses[2], (("map", 2), 0), (("map", 2), 1))

    @pl.when(uses[2])
    def _():
        compose(2, 0)
        compose(2, 1)

    for n in range(2, 4):
        y_arrives(n, i0 & inner)

    @pl.when(uses[2])
    def _():
        settle(2, 0)
        settle(2, 1)
        handed_on(2)

    @pl.when(i3 & inner)
    def _():
        for one in ahead_of_late:
            one.wait_send()
        for one in late:
            one.start()

    pending.append((i3 & inner, late))

    cov = a_ref[...].astype(BF16)

    def edges(step, sign, m):
        for j in range(2):
            kb[step, j] = sign * mm(full[rows:], m[j, :rows]) + m[j, rows:].astype(F32)
        cross_ref[step] = mm(cov, kb[step, c].astype(BF16))

    @pl.when(jnp.logical_not(started))
    def _():
        full[...] = jnp.zeros_like(full)

    for n in range(3):
        y_arrives(n, jnp.logical_not(i0))
    collect(started, ("y", 0), ("y", 1))

    @pl.when(started)
    def _():
        unpack_first(zy, full)

    def close(m, n):
        return mm(full[parts[n], parts[n]], m[c, parts[n]])

    def far(m, n):
        return mm(full[parts[n], parts[1 - n]], m[c, parts[1 - n]])

    y_arrives(3, later | jnp.logical_not(i0))
    edges(0, 1.0, m0)
    begun = [close(m0, n) for n in range(2)]

    @pl.when(prompt)
    def _():
        edges(1, -1.0, m1)
        for n in range(2):
            half_done[parts[n]] = close(m1, n)

    for n in range(2):
        collect(started, ("y", 2 + n))

        @pl.when(started)
        def _():
            unpack_outer(zy, full, n)

    leads = i0 & passes
    heads = i2 & top

    def start_y(n):
        emit_copies(heads, [packed_to(2, n, zy, "y", -2)])
        emit_copies(leads, [packed_to(0, n, zy, "y", -4), packed_to(0, n, zr, "r", 1)])

    w = jnp.concatenate([begun[n] + far(m0, n) for n in range(2)], axis=0).astype(BF16)
    pm0[mine] += mm(t0[mine, :], w)

    @pl.when(leads | heads)
    def _():
        pack_first(pm0, kb[0, c])

    start_y(0)
    start_y(1)
    pm0[other] += mm(t0[other, :], w)

    for n in range(2):

        @pl.when(leads | heads)
        def _():
            pack_outer(pm0, n)

        start_y(2 + n)
    emit_copies(heads, [packed_to(2, n, zy, "y", -1) for n in range(4)])
    emit_copies(leads, [packed_to(0, n, zy, "y", -2) for n in range(4)])

    @pl.when(later)
    def _():
        compose(0, 1)
        extend(1)
        settle(0, 1)
        edges(1, -1.0, m1)
        for n in range(2):
            half_done[parts[n]] = close(m1, n)

    for n in range(2):
        w1[parts[n]] = (half_done[parts[n]] + far(m1, n)).astype(BF16)

    for n in range(4):
        ref = zr.at[o, fine[n]]
        there = zy.at[o, fine[n]]
        forth = copy(ref, there, place[1](("r", n)), recvs(("y", n), 2), at(-2))

        @pl.when(i1 & passes)
        def _():
            copy(ref, ref, place[1](("r", n)), recvs(("r", n)), at(-2)).wait_recv()

        emit_copies(i1 & passes, [forth])

    @pl.when(started)
    def _():
        for n in range(4):
            handoffs["y", n].wait_send()

    for one in first:
        one.wait_send()
    join.wait_send()
    for when, copies in pending:

        @pl.when(when)
        def _():
            for one in copies:
                one.wait_send()


def finish(w1, t1, pm0, pm1, kb, cross_ref, out_hbm, cross_hbm, out, store):
    wide = out.shape[2]
    ends = pltpu.make_async_copy(cross_ref, cross_hbm, store.at[4])
    ends.start()
    stores = []

    def emit(step, j, value):
        span = pl.ds(j * wide, wide)
        out[step, span] = value + mt(kb[step, j].astype(BF16), cross_ref[step].astype(BF16))
        one = pltpu.make_async_copy(out.at[step, span], out_hbm.at[step, span], store.at[2 * step + j])
        one.start()
        stores.append(one)

    for j in range(2):
        emit(0, j, pm0[pl.ds(j * wide, wide)])
    for j in range(2):
        span = pl.ds(j * wide, wide)
        emit(1, j, pm1[span] + mm(t1[span, :], w1[...]))
    ends.wait()
    for one in stores:
        one.wait()


def shards(diagonal_block_inverse, step_map, arrow_map, arrow_cov):
    count, nodes, wide = diagonal_block_inverse.shape
    effects = arrow_map.shape[1]
    tall = nodes + effects
    packed = 4 * (wide // 2) + 2 * effects + MARK
    vmem = pl.BlockSpec(memory_space=pltpu.VMEM)
    hbm = pl.BlockSpec(memory_space=pltpu.HBM)
    held = pl.pallas_call(
        kernel,
        out_shape=(
            jax.ShapeDtypeStruct((nodes, wide), BF16),
            jax.ShapeDtypeStruct((nodes, nodes), BF16),
            jax.ShapeDtypeStruct((nodes, wide), F32),
            jax.ShapeDtypeStruct((nodes, wide), F32),
            jax.ShapeDtypeStruct((count, 2, effects, wide), F32),
            jax.ShapeDtypeStruct((count, effects, wide), F32),
        ),
        in_specs=[hbm] * 4,
        out_specs=(vmem,) * 6,
        scratch_shapes=[
            pltpu.VMEM((count, nodes, wide), F32),
            pltpu.VMEM((count, effects, wide), BF16),
            pltpu.VMEM((effects, effects), F32),
            pltpu.VMEM((2, nodes, wide), BF16),
            pltpu.VMEM((2, nodes, wide), BF16),
            pltpu.VMEM((2, tall, wide), BF16),
            pltpu.VMEM((2, tall, wide), BF16),
            pltpu.VMEM((nodes, nodes), BF16),
            pltpu.VMEM((2, tall, wide), BF16),
            pltpu.VMEM((2, tall, wide), BF16),
            pltpu.VMEM((3, 2, tall, wide), BF16),
            pltpu.VMEM((3, 2, tall, wide), BF16),
            pltpu.VMEM((packed, wide // 2), BF16),
            pltpu.VMEM((2, packed, wide // 2), BF16),
            pltpu.VMEM((2, packed, wide // 2), BF16),
            pltpu.VMEM((3, 2, packed, wide // 2), BF16),
            pltpu.VMEM((3, 2, nodes, wide), BF16),
            pltpu.VMEM((tall, nodes), BF16),
            pltpu.VMEM((tall, nodes), BF16),
            pltpu.VMEM((nodes, wide), F32),
            pltpu.SemaphoreType.DMA((SENDS,)),
            pltpu.SemaphoreType.DMA((RECVS,)),
            pltpu.SemaphoreType.DMA((6,)),
        ],
        compiler_params=pltpu.CompilerParams(
            collective_id=0, has_side_effects=True, vmem_limit_bytes=28 * 1024 * 1024
        ),
    )(*(
        pltpu.with_memory_space_constraint(array, pltpu.HBM)
        for array in (diagonal_block_inverse, step_map, arrow_map, arrow_cov)
    ))
    return pl.pallas_call(
        finish,
        out_shape=(
            jax.ShapeDtypeStruct((count, nodes, wide), F32),
            jax.ShapeDtypeStruct((count, effects, wide), F32),
        ),
        in_specs=[vmem] * 6,
        out_specs=(hbm, hbm),
        scratch_shapes=[
            pltpu.VMEM((count, nodes, wide), F32),
            pltpu.SemaphoreType.DMA((5,)),
        ],
        compiler_params=pltpu.CompilerParams(vmem_limit_bytes=28 * 1024 * 1024),
    )(*held)


def solution(mesh):
    return jax.shard_map(
        shards,
        mesh=mesh,
        in_specs=(
            P(("rep", "tm"), None, "col"),
            P(("rep", "tm"), None, "col"),
            P(("rep", "tm"), None, "col"),
            P("rep", None),
        ),
        out_specs=(P(("rep", "tm"), None, "col"), P(("rep", "tm"), None, "col")),
        check_vma=False,
    )
```

```python
import jax
import jax.numpy as jnp
from jax import lax
from jax.experimental import pallas as pl
from jax.experimental.pallas import tpu as pltpu
from jax.sharding import PartitionSpec as P

MESH = pl.DeviceIdType.MESH
F32 = jnp.float32
BF16 = jnp.bfloat16
SENDS = 38
RECVS = 47
MARK = 16


def mm(left, right):
    return jnp.dot(left, right, preferred_element_type=F32)


def mt(left, right):
    return lax.dot_general(left, right, (((0,), (0,)), ((), ())), preferred_element_type=F32)


class Slots:
    def __init__(self, start, end):
        self.found = {}
        self.free = start
        self.end = end

    def __call__(self, name, width=1):
        if name not in self.found:
            self.found[name] = self.free
            self.free += width
            assert self.free <= self.end
        return self.found[name]


def kernel(
    d_hbm, g_hbm, h_hbm, a_hbm,
    w1, t1, pm0, pm1, kb, cross_ref,
    d_ref, h_ref, a_ref, g0f, g1f, dh1f, gk, t0, m0, m1, xm0, xm1,
    zs, zy, zr, zc, gc, fc, full, half_done, held,
    send, recv, load,
):
    rows = g0f.shape[1]
    wide = g0f.shape[2]
    tall = gk.shape[1]
    half = wide // 2
    edge_rows = tall - rows
    tm = lax.axis_index("tm")
    c = lax.axis_index("col")
    o = 1 - c
    quads = lax.axis_size("tm") // 4
    q = tm // 4
    i = tm % 4
    top = q == quads - 1
    inner = jnp.logical_not(top)
    passes = q > 0
    i0, i1, i2, i3 = (i == n for n in range(4))
    mate = {"col": o}
    recvs = Slots(0, RECVS)
    sends = Slots(0, 18)
    place = [Slots(18, SENDS) for _ in range(4)]

    def at(step):
        return {"tm": tm + step, "col": o}

    def copy(src, dst, sem, sem_there, device):
        return pltpu.make_async_remote_copy(
            src_ref=src, dst_ref=dst, send_sem=send.at[sem], recv_sem=recv.at[sem_there],
            device_id=device, device_id_type=MESH,
        )

    loads = [
        pltpu.make_async_copy(d_hbm.at[1], d_ref.at[1], load.at[0]),
        pltpu.make_async_copy(h_hbm, h_ref, load.at[1]),
        pltpu.make_async_copy(g_hbm.at[0], g0f.at[c], load.at[2]),
        pltpu.make_async_copy(g_hbm.at[1], g1f.at[c], load.at[3]),
        pltpu.make_async_copy(d_hbm.at[0], d_ref.at[0], load.at[4]),
        pltpu.make_async_copy(a_hbm, a_ref, load.at[5]),
    ]
    for one in loads:
        one.start()

    barrier = pltpu.get_barrier_semaphore()
    pl.semaphore_signal(barrier, inc=1, device_id=mate, device_id_type=MESH)

    def greet(when, steps):
        @pl.when(when)
        def _():
            for step in steps:
                pl.semaphore_signal(barrier, inc=1, device_id=at(step), device_id_type=MESH)

    greet(i0, (1, 2))
    greet(i0 & inner, (3, 4))
    greet(i1, (-1,))
    greet(i1 & inner, (2,))
    greet(i1 & top, (1,))
    greet(i2, (1,))
    greet(i2 & inner, (2,))
    greet(i3 & inner, (2,))

    def one_if(flag):
        return jnp.where(flag, 1, 0)

    targets = (
        1 + 2 * one_if(i3 & inner) + one_if(i2 & top) + one_if(i1 & passes) + 2 * one_if(i0 & passes)
    )

    loads[0].wait()
    loads[1].wait()
    dh1f[c, :rows] = d_ref[1].astype(BF16)
    dh1f[c, rows:] = h_ref[1]
    pl.semaphore_wait(barrier, 1 + targets)

    def swap(name, src, dst):
        return copy(src, dst, sends(name), recvs(name), mate)

    first = [
        swap("dh1", dh1f.at[c], dh1f.at[c]),
        swap("g0", g_hbm.at[0], g0f.at[c]),
        swap("g1", g_hbm.at[1], g1f.at[c]),
    ]
    for one in first:
        one.start()
    for one in loads[2:]:
        one.wait()

    def times(left, span, right):
        return mm(jnp.concatenate([left[0, span], left[1, span]], axis=1), right)

    body = pl.ds(0, rows)
    mine = pl.ds(pl.multiple_of(c * wide, wide), wide)
    other = pl.ds(pl.multiple_of(o * wide, wide), wide)
    edge_base = 2 * half
    mark_base = edge_base + 2 * edge_rows
    first_rows = mark_base + MARK
    top_span = pl.ds(0, first_rows)
    low_span = pl.ds(first_rows, zs.shape[0] - first_rows)
    spans = (top_span, low_span)
    middle = first_rows // 32 * 16
    fine = (
        pl.ds(0, middle), pl.ds(middle, first_rows - middle),
        pl.ds(first_rows, half), pl.ds(first_rows + half, half),
    )
    across = lax.broadcasted_iota(jnp.int32, (half, half), 1)
    down = lax.broadcasted_iota(jnp.int32, (half, half), 0)

    def pack_first(p, edge):
        r = pl.multiple_of(c * wide, wide)
        one = p[pl.ds(r, half), :half]
        two = p[pl.ds(r + half, half), half:]
        zs[:half] = jnp.where(down >= across, one, two).astype(BF16)
        zs[half:edge_base] = p[pl.ds(r, half), half:].astype(BF16)
        zs[edge_base : edge_base + edge_rows] = edge[:, :half].astype(BF16)
        zs[edge_base + edge_rows : mark_base] = edge[:, half:].astype(BF16)
        mark = jnp.sum(jnp.where(down == across, two, 0.0), axis=0, keepdims=True)
        zs[mark_base:first_rows] = jnp.broadcast_to(mark, (MARK, half)).astype(BF16)

    def pack_outer(p, n):
        to = fine[2 + n]

        @pl.when(c == 0)
        def _():
            zs[to] = p[pl.ds(wide + n * half, half), :half].astype(BF16)

        @pl.when(c == 1)
        def _():
            zs[to] = p[half:wide, pl.ds(n * half, half)].astype(BF16)

    def unpack_first(z, full):
        for j in range(2):
            base = j * wide
            lo = pl.ds(base, half)
            hi = pl.ds(base + half, half)
            both = z[j, :half].astype(F32)
            turned = both.T
            mark = z[j, mark_base:first_rows].astype(F32)[:1]
            full[lo, lo] = jnp.where(down >= across, both, turned).astype(BF16)
            full[hi, hi] = jnp.where(
                down < across, both, jnp.where(down == across, mark, turned)
            ).astype(BF16)
            side = z[j, half:edge_base]
            full[lo, hi] = side
            full[hi, lo] = side.T
            for n in range(2):
                full[rows:, pl.ds(base + n * half, half)] = z[
                    j, edge_base + n * edge_rows : edge_base + (n + 1) * edge_rows
                ]

    def unpack_outer(z, full, n):
        far = pl.ds(wide + n * half, half)
        for j in range(2):
            close = pl.ds(j * half, half)
            outer = z[j, fine[2 + n]]
            if j == 0:
                full[far, close] = outer
                full[close, far] = outer.T
            else:
                full[close, far] = outer
                full[far, close] = outer.T

    pending = []

    def emit_copies(when, copies):
        @pl.when(when)
        def _():
            for one in copies:
                one.start()

        pending.append((when, copies))

    def packed_to(where, n, buffer, there, step):
        span = (spans if there[0] == "raw" else fine)[n]
        return copy(
            zs.at[span], buffer.at[c, span],
            place[where]((there, step, n)), recvs((there, n), 1 if there == "r" else 2), at(step),
        )

    parts = (pl.ds(0, wide), pl.ds(wide, wide))

    def map_to(slot, step):
        return [
            copy(
                gk.at[c, parts[n]], gc.at[slot, c, parts[n]],
                place[slot + 1](("map", step, n)), recvs((("map", slot), n), 2), at(step),
            )
            for n in range(2)
        ]

    own0 = g0f[c]
    w = mm(dh1f[c], g0f[c, mine])
    first[0].wait_recv()
    w += mm(dh1f[o], g0f[c, other])
    wb = w[:rows].astype(BF16)
    kappa = w[rows:] - h_ref[0].astype(F32)
    pm0[mine] = d_ref[0, mine] + mt(g0f[c], wb)

    raw_targets = (
        (i3 & inner, 2, (-1, -2)),
        (i2 & inner, 1, (-2,)),
        (i1, 0, (-1,)),
    )

    def start_raw(n):
        for when, slot, steps in raw_targets:
            emit_copies(
                when, [packed_to(slot + 1, n, zc.at[slot], ("raw", slot), step) for step in steps]
            )

    pack_first(pm0, kappa)
    emit_copies(i3 & top, [packed_to(3, n, zy, "y", -1) for n in range(2)])
    start_raw(0)
    first[1].wait_recv()
    pm0[other] = d_ref[0, other] + mt(g0f[o], wb)
    for n in range(2):
        pack_outer(pm0, n)
        emit_copies(i3 & top, [packed_to(3, 2 + n, zy, "y", -1)])

    first[2].wait_recv()
    gk[c, :rows] = times(g1f, body, own0).astype(BF16)
    gk[c, rows:] = kappa.astype(BF16)
    ahead_of_late = map_to(2, -2)
    late = map_to(2, -3)[:1]
    emit_copies(i3 & inner, map_to(2, -1))
    emit_copies(i2 & inner, map_to(1, -2))
    emit_copies(i1, map_to(0, -1))

    @pl.when(i3 & inner)
    def _():
        for one in ahead_of_late:
            one.start()

    start_raw(1)

    join = swap("gk", gk.at[c], gk.at[c])
    join.start()
    pm1[...] = d_ref[1]
    join.wait_recv()
    m0[...] = gk[...]
    m1[:, :rows] = g1f[...]
    m1[:, rows:] = -dh1f[:, rows:]

    def turn():
        for j in range(2):
            span = pl.ds(j * wide, wide)
            t0[span, :] = m0[j, :rows].T
            t1[span, :] = m1[j, :rows].T

    turn()

    handoffs = {}

    def arrive(when, name, ref, number, relay=None, relayed=None):
        here, there = recvs(name, 2), recvs(name, 2) + 1
        h = o if relayed is None else jnp.where(relayed, c, o)
        onward = copy(ref(h), ref(h), sends(("on", number)), there, mate)
        handoffs[name] = onward

        @pl.when(when)
        def _():
            copy(ref(h), ref(h), sends(("on", number)), here, mate).wait_recv()
            onward.start()

        if relay is not None:
            step, where = relay
            handed = copy(ref(h), ref(h), place[where](("relay", name)), here, at(step))
            emit_copies(when & (i == where), [handed])

    def collect(when, *names):
        @pl.when(when)
        def _():
            for name in names:
                handoffs[name].wait_recv()

    uses = (i0, inner & (i0 | i1), inner & jnp.logical_not(i3))
    relays = (None, (1, 0), (-2, 2))

    def block_arrives(slot, n, when=True):
        arrive(
            uses[slot] & when, (("raw", slot), n), lambda h: zc.at[slot, h, spans[n]],
            (slot % 2) * 4 + n, relays[slot], (None, i1, i0)[slot],
        )

    def map_arrives(slot, when=True):
        for n in range(2):
            arrive(
                uses[slot] & when, (("map", slot), n), lambda h: gc.at[slot, h, parts[n]],
                (slot % 2) * 4 + 2 + n, relays[slot] if slot == 1 or n == 1 else None,
                (None, i1, i0 if n == 1 else None)[slot],
            )

    def handed_on(slot):
        for n in range(2):
            handoffs[("raw", slot), n].wait_send()
            handoffs[("map", slot), n].wait_send()

    def swaps(slot):
        return [
            copy(xm0.at[slot, c], xm0.at[slot, c], sends("m0"), recvs(("m0", slot)), mate),
            copy(xm1.at[slot, c], xm1.at[slot, c], sends("m1"), recvs(("m1", slot)), mate),
        ]

    maps = ((m0, xm0, t0, pm0, 1.0), (m1, xm1, t1, pm1, -1.0))

    def compose(slot, n):
        m, x, _, _, sign = maps[n]
        own = m[c, :rows]
        edge = mm(fc[rows:], own)
        x[slot, c, rows:] = (m[c, rows:].astype(F32) + sign * edge).astype(BF16)
        x[slot, c, :rows] = times(gc.at[slot], body, own).astype(BF16)
        swaps(slot)[n].start()

    def extend(n):
        m, _, t, p, _ = maps[n]
        wb = mm(fc[:rows], m[c, :rows]).astype(BF16)
        for j in range(2):
            span = pl.ds(j * wide, wide)
            p[span] += mm(t[span, :], wb)

    def settle(slot, n):
        m, x, t, _, _ = maps[n]
        one = swaps(slot)[n]
        one.wait_recv()
        m[...] = x[slot]
        for j in range(2):
            t[pl.ds(j * wide, wide), :] = x[slot, j, :rows].T
        one.wait_send()

    later = i0 & top
    prompt = jnp.logical_not(later)
    lazy = i0 & inner
    across_mate = swap("pm1", held.at[c], held.at[c])
    started = jnp.logical_not(i3 & top)

    def y_arrives(n, when):
        arrive(
            started & when, ("y", n), lambda h: zy.at[h, fine[n]], (8, 9, 5, 10)[n], None, (i1 & inner) | i3
        )
        ref = zy.at[o, fine[n]]
        emit_copies(
            i0 & inner & when, [copy(ref, ref, place[0](("relay", n)), recvs(("y", n), 2), at(1))]
        )

    def block_whole(slot):
        for n in range(2):
            unpack_outer(zc.at[slot], fc, n)

    def merge(slot):
        raw, drawn = ("raw", slot), ("map", slot)
        use = uses[slot]
        collect(use, (raw, 0), (drawn, 0), (drawn, 1))

        @pl.when(use)
        def _():
            unpack_first(zc.at[slot], fc)
            compose(slot, 0)

            @pl.when(prompt)
            def _():
                compose(slot, 1)

        if slot == 0:
            block_arrives(1, 1)
            block_arrives(0, 1)
            block_arrives(2, 0, i1)
            map_arrives(2, i1)
            block_arrives(2, 1, i1)
        collect(use, (raw, 1))
        if slot == 0:
            y_arrives(0, later)
            y_arrives(1, later)

        @pl.when(use)
        def _():
            block_whole(slot)

            @pl.when(jnp.logical_not(lazy))
            def _():
                extend(0)

        if slot == 0:
            y_arrives(2, later)

        @pl.when(use)
        def _():
            settle(slot, 0)

            @pl.when(prompt)
            def _():
                extend(1)
                settle(slot, 1)

            handed_on(slot)

    block_arrives(1, 0)
    block_arrives(0, 0)
    map_arrives(1)
    map_arrives(0)
    merge(0)
    merge(1)
    early = jnp.logical_not(i1)
    block_arrives(2, 0, early)
    map_arrives(2, i2)
    block_arrives(2, 1, early)
    collect(uses[2], (("raw", 2), 0), (("raw", 2), 1))

    @pl.when(uses[2])
    def _():
        unpack_first(zc.at[2], fc)
        block_whole(2)
        extend(1)

        @pl.when(jnp.logical_not(lazy))
        def _():
            extend(0)

        @pl.when(lazy)
        def _():
            held[c] = pm1[...].astype(BF16)
            across_mate.start()

    map_arrives(2, i0)
    collect(uses[2], (("map", 2), 0), (("map", 2), 1))

    @pl.when(uses[2])
    def _():
        compose(2, 0)
        compose(2, 1)

    @pl.when(lazy)
    def _():
        across_mate.wait_recv()
        wb = times(held, body, g0f[c]).astype(BF16)
        pm0[mine] = d_ref[0, mine] + mt(g0f[c], wb)
        pm0[other] = d_ref[0, other] + mt(g0f[o], wb)
        across_mate.wait_send()

    y_arrives(0, lazy)
    y_arrives(1, lazy)

    @pl.when(uses[2])
    def _():
        settle(2, 0)

    y_arrives(2, lazy)

    @pl.when(uses[2])
    def _():
        settle(2, 1)
        handed_on(2)

    y_arrives(3, lazy)

    @pl.when(i3 & inner)
    def _():
        for one in ahead_of_late:
            one.wait_send()
        for one in late:
            one.start()

    pending.append((i3 & inner, late))

    cov = a_ref[...].astype(BF16)

    def edges(step, sign, m):
        for j in range(2):
            kb[step, j] = sign * mm(full[rows:], m[j, :rows]) + m[j, rows:].astype(F32)
        cross_ref[step] = mm(cov, kb[step, c].astype(BF16))

    @pl.when(jnp.logical_not(started))
    def _():
        full[...] = jnp.zeros_like(full)

    for n in range(3):
        y_arrives(n, jnp.logical_not(i0))
    collect(started, ("y", 0), ("y", 1))

    @pl.when(started)
    def _():
        unpack_first(zy, full)

    def close(m, n):
        return mm(full[parts[n], parts[n]], m[c, parts[n]])

    def far(m, n):
        return mm(full[parts[n], parts[1 - n]], m[c, parts[1 - n]])

    y_arrives(3, later | jnp.logical_not(i0))
    edges(0, 1.0, m0)
    begun = [close(m0, n) for n in range(2)]

    @pl.when(prompt)
    def _():
        edges(1, -1.0, m1)
        for n in range(2):
            half_done[parts[n]] = close(m1, n)

    for n in range(2):
        collect(started, ("y", 2 + n))

        @pl.when(started)
        def _():
            unpack_outer(zy, full, n)

    leads = i0 & passes
    heads = i2 & top

    def start_y(n):
        emit_copies(heads, [packed_to(2, n, zy, "y", -2)])
        emit_copies(leads, [packed_to(0, n, zy, "y", -4), packed_to(0, n, zr, "r", 1)])

    w = jnp.concatenate([begun[n] + far(m0, n) for n in range(2)], axis=0).astype(BF16)
    pm0[mine] += mm(t0[mine, :], w)

    @pl.when(leads | heads)
    def _():
        pack_first(pm0, kb[0, c])

    start_y(0)
    start_y(1)
    pm0[other] += mm(t0[other, :], w)

    for n in range(2):

        @pl.when(leads | heads)
        def _():
            pack_outer(pm0, n)

        start_y(2 + n)
    emit_copies(heads, [packed_to(2, n, zy, "y", -1) for n in range(4)])
    emit_copies(leads, [packed_to(0, n, zy, "y", -2) for n in range(4)])

    @pl.when(later)
    def _():
        compose(0, 1)
        extend(1)
        settle(0, 1)
        edges(1, -1.0, m1)
        for n in range(2):
            half_done[parts[n]] = close(m1, n)

    for n in range(2):
        w1[parts[n]] = (half_done[parts[n]] + far(m1, n)).astype(BF16)

    for n in range(4):
        ref = zr.at[o, fine[n]]
        there = zy.at[o, fine[n]]
        forth = copy(ref, there, place[1](("r", n)), recvs(("y", n), 2), at(-2))

        @pl.when(i1 & passes)
        def _():
            copy(ref, ref, place[1](("r", n)), recvs(("r", n)), at(-2)).wait_recv()

        emit_copies(i1 & passes, [forth])

    @pl.when(started)
    def _():
        for n in range(4):
            handoffs["y", n].wait_send()

    for one in first:
        one.wait_send()
    join.wait_send()
    for when, copies in pending:

        @pl.when(when)
        def _():
            for one in copies:
                one.wait_send()


def finish(w1, t1, pm0, pm1, kb, cross_ref, out_hbm, cross_hbm, out, store):
    wide = out.shape[2]
    ends = pltpu.make_async_copy(cross_ref, cross_hbm, store.at[4])
    ends.start()
    stores = []

    def emit(step, j, value):
        span = pl.ds(j * wide, wide)
        out[step, span] = value + mt(kb[step, j].astype(BF16), cross_ref[step].astype(BF16))
        one = pltpu.make_async_copy(out.at[step, span], out_hbm.at[step, span], store.at[2 * step + j])
        one.start()
        stores.append(one)

    for j in range(2):
        emit(0, j, pm0[pl.ds(j * wide, wide)])
    for j in range(2):
        span = pl.ds(j * wide, wide)
        emit(1, j, pm1[span] + mm(t1[span, :], w1[...]))
    ends.wait()
    for one in stores:
        one.wait()


def shards(diagonal_block_inverse, step_map, arrow_map, arrow_cov):
    count, nodes, wide = diagonal_block_inverse.shape
    effects = arrow_map.shape[1]
    tall = nodes + effects
    packed = 4 * (wide // 2) + 2 * effects + MARK
    vmem = pl.BlockSpec(memory_space=pltpu.VMEM)
    hbm = pl.BlockSpec(memory_space=pltpu.HBM)
    held = pl.pallas_call(
        kernel,
        out_shape=(
            jax.ShapeDtypeStruct((nodes, wide), BF16),
            jax.ShapeDtypeStruct((nodes, nodes), BF16),
            jax.ShapeDtypeStruct((nodes, wide), F32),
            jax.ShapeDtypeStruct((nodes, wide), F32),
            jax.ShapeDtypeStruct((count, 2, effects, wide), F32),
            jax.ShapeDtypeStruct((count, effects, wide), F32),
        ),
        in_specs=[hbm] * 4,
        out_specs=(vmem,) * 6,
        scratch_shapes=[
            pltpu.VMEM((count, nodes, wide), F32),
            pltpu.VMEM((count, effects, wide), BF16),
            pltpu.VMEM((effects, effects), F32),
            pltpu.VMEM((2, nodes, wide), BF16),
            pltpu.VMEM((2, nodes, wide), BF16),
            pltpu.VMEM((2, tall, wide), BF16),
            pltpu.VMEM((2, tall, wide), BF16),
            pltpu.VMEM((nodes, nodes), BF16),
            pltpu.VMEM((2, tall, wide), BF16),
            pltpu.VMEM((2, tall, wide), BF16),
            pltpu.VMEM((3, 2, tall, wide), BF16),
            pltpu.VMEM((3, 2, tall, wide), BF16),
            pltpu.VMEM((packed, wide // 2), BF16),
            pltpu.VMEM((2, packed, wide // 2), BF16),
            pltpu.VMEM((2, packed, wide // 2), BF16),
            pltpu.VMEM((3, 2, packed, wide // 2), BF16),
            pltpu.VMEM((3, 2, nodes, wide), BF16),
            pltpu.VMEM((tall, nodes), BF16),
            pltpu.VMEM((tall, nodes), BF16),
            pltpu.VMEM((nodes, wide), F32),
            pltpu.VMEM((2, nodes, wide), BF16),
            pltpu.SemaphoreType.DMA((SENDS,)),
            pltpu.SemaphoreType.DMA((RECVS,)),
            pltpu.SemaphoreType.DMA((6,)),
        ],
        compiler_params=pltpu.CompilerParams(
            collective_id=0, has_side_effects=True, vmem_limit_bytes=28 * 1024 * 1024
        ),
    )(*(
        pltpu.with_memory_space_constraint(array, pltpu.HBM)
        for array in (diagonal_block_inverse, step_map, arrow_map, arrow_cov)
    ))
    return pl.pallas_call(
        finish,
        out_shape=(
            jax.ShapeDtypeStruct((count, nodes, wide), F32),
            jax.ShapeDtypeStruct((count, effects, wide), F32),
        ),
        in_specs=[vmem] * 6,
        out_specs=(hbm, hbm),
        scratch_shapes=[
            pltpu.VMEM((count, nodes, wide), F32),
            pltpu.SemaphoreType.DMA((5,)),
        ],
        compiler_params=pltpu.CompilerParams(vmem_limit_bytes=28 * 1024 * 1024),
    )(*held)


def solution(mesh):
    return jax.shard_map(
        shards,
        mesh=mesh,
        in_specs=(
            P(("rep", "tm"), None, "col"),
            P(("rep", "tm"), None, "col"),
            P(("rep", "tm"), None, "col"),
            P("rep", None),
        ),
        out_specs=(P(("rep", "tm"), None, "col"), P(("rep", "tm"), None, "col")),
        check_vma=False,
    )
```

```python
import jax
import jax.numpy as jnp
from jax import lax
from jax.experimental import pallas as pl
from jax.experimental.pallas import tpu as pltpu
from jax.sharding import PartitionSpec as P

MESH = pl.DeviceIdType.MESH
F32 = jnp.float32
BF16 = jnp.bfloat16
SENDS = 38
RECVS = 47
MARK = 16


def mm(left, right):
    return jnp.dot(left, right, preferred_element_type=F32)


def mt(left, right):
    return lax.dot_general(left, right, (((0,), (0,)), ((), ())), preferred_element_type=F32)


class Slots:
    def __init__(self, start, end):
        self.found = {}
        self.free = start
        self.end = end

    def __call__(self, name, width=1):
        if name not in self.found:
            self.found[name] = self.free
            self.free += width
            assert self.free <= self.end
        return self.found[name]


def kernel(
    d_hbm, g_hbm, h_hbm, a_hbm,
    w1, t1, pm0, pm1, kb, cross_ref,
    d_ref, h_ref, a_ref, g0f, g1f, dh1f, gk, t0, m0, m1, xm0, xm1,
    zs, zy, zr, zc, gc, fc, full, half_done, held,
    send, recv, load,
):
    rows = g0f.shape[1]
    wide = g0f.shape[2]
    tall = gk.shape[1]
    half = wide // 2
    edge_rows = tall - rows
    tm = lax.axis_index("tm")
    c = lax.axis_index("col")
    o = 1 - c
    quads = lax.axis_size("tm") // 4
    q = tm // 4
    i = tm % 4
    top = q == quads - 1
    inner = jnp.logical_not(top)
    passes = q > 0
    i0, i1, i2, i3 = (i == n for n in range(4))
    mate = {"col": o}
    recvs = Slots(0, RECVS)
    sends = Slots(0, 18)
    place = [Slots(18, SENDS) for _ in range(4)]

    def at(step):
        return {"tm": tm + step, "col": o}

    def copy(src, dst, sem, sem_there, device):
        return pltpu.make_async_remote_copy(
            src_ref=src, dst_ref=dst, send_sem=send.at[sem], recv_sem=recv.at[sem_there],
            device_id=device, device_id_type=MESH,
        )

    loads = [
        pltpu.make_async_copy(d_hbm.at[1], d_ref.at[1], load.at[0]),
        pltpu.make_async_copy(h_hbm, h_ref, load.at[1]),
        pltpu.make_async_copy(g_hbm.at[0], g0f.at[c], load.at[2]),
        pltpu.make_async_copy(g_hbm.at[1], g1f.at[c], load.at[3]),
        pltpu.make_async_copy(d_hbm.at[0], d_ref.at[0], load.at[4]),
        pltpu.make_async_copy(a_hbm, a_ref, load.at[5]),
    ]
    for one in loads:
        one.start()

    barrier = pltpu.get_barrier_semaphore()
    pl.semaphore_signal(barrier, inc=1, device_id=mate, device_id_type=MESH)

    def greet(when, steps):
        @pl.when(when)
        def _():
            for step in steps:
                pl.semaphore_signal(barrier, inc=1, device_id=at(step), device_id_type=MESH)

    greet(i0, (1, 2))
    greet(i0 & inner, (3, 4))
    greet(i1, (-1,))
    greet(i1 & inner, (2,))
    greet(i1 & top, (1,))
    greet(i2, (1,))
    greet(i2 & inner, (2,))
    greet(i3 & inner, (2,))

    def one_if(flag):
        return jnp.where(flag, 1, 0)

    targets = (
        1 + 2 * one_if(i3 & inner) + one_if(i2 & top) + one_if(i1 & passes) + 2 * one_if(i0 & passes)
    )

    loads[0].wait()
    loads[1].wait()
    dh1f[c, :rows] = d_ref[1].astype(BF16)
    dh1f[c, rows:] = h_ref[1]
    pl.semaphore_wait(barrier, 1 + targets)

    def swap(name, src, dst):
        return copy(src, dst, sends(name), recvs(name), mate)

    first = [
        swap("dh1", dh1f.at[c], dh1f.at[c]),
        swap("g0", g_hbm.at[0], g0f.at[c]),
        swap("g1", g_hbm.at[1], g1f.at[c]),
    ]
    for one in first:
        one.start()
    for one in loads[2:]:
        one.wait()

    def times(left, span, right):
        return mm(jnp.concatenate([left[0, span], left[1, span]], axis=1), right)

    body = pl.ds(0, rows)
    mine = pl.ds(pl.multiple_of(c * wide, wide), wide)
    other = pl.ds(pl.multiple_of(o * wide, wide), wide)
    edge_base = 2 * half
    mark_base = edge_base + 2 * edge_rows
    first_rows = mark_base + MARK
    top_span = pl.ds(0, first_rows)
    low_span = pl.ds(first_rows, zs.shape[0] - first_rows)
    spans = (top_span, low_span)
    middle = first_rows // 32 * 16
    fine = (
        pl.ds(0, middle), pl.ds(middle, first_rows - middle),
        pl.ds(first_rows, half), pl.ds(first_rows + half, half),
    )
    across = lax.broadcasted_iota(jnp.int32, (half, half), 1)
    down = lax.broadcasted_iota(jnp.int32, (half, half), 0)

    def pack_first(p, edge):
        r = pl.multiple_of(c * wide, wide)
        one = p[pl.ds(r, half), :half]
        two = p[pl.ds(r + half, half), half:]
        zs[:half] = jnp.where(down >= across, one, two).astype(BF16)
        zs[half:edge_base] = p[pl.ds(r, half), half:].astype(BF16)
        zs[edge_base : edge_base + edge_rows] = edge[:, :half].astype(BF16)
        zs[edge_base + edge_rows : mark_base] = edge[:, half:].astype(BF16)
        mark = jnp.sum(jnp.where(down == across, two, 0.0), axis=0, keepdims=True)
        zs[mark_base:first_rows] = jnp.broadcast_to(mark, (MARK, half)).astype(BF16)

    def pack_outer(p, n):
        to = fine[2 + n]

        @pl.when(c == 0)
        def _():
            zs[to] = p[pl.ds(wide + n * half, half), :half].astype(BF16)

        @pl.when(c == 1)
        def _():
            zs[to] = p[half:wide, pl.ds(n * half, half)].astype(BF16)

    def unpack_first(z, full):
        for j in range(2):
            base = j * wide
            lo = pl.ds(base, half)
            hi = pl.ds(base + half, half)
            both = z[j, :half].astype(F32)
            turned = both.T
            mark = z[j, mark_base:first_rows].astype(F32)[:1]
            full[lo, lo] = jnp.where(down >= across, both, turned).astype(BF16)
            full[hi, hi] = jnp.where(
                down < across, both, jnp.where(down == across, mark, turned)
            ).astype(BF16)
            side = z[j, half:edge_base]
            full[lo, hi] = side
            full[hi, lo] = side.T
            for n in range(2):
                full[rows:, pl.ds(base + n * half, half)] = z[
                    j, edge_base + n * edge_rows : edge_base + (n + 1) * edge_rows
                ]

    def unpack_outer(z, full, n):
        far = pl.ds(wide + n * half, half)
        for j in range(2):
            close = pl.ds(j * half, half)
            outer = z[j, fine[2 + n]]
            if j == 0:
                full[far, close] = outer
                full[close, far] = outer.T
            else:
                full[close, far] = outer
                full[far, close] = outer.T

    pending = []

    def emit_copies(when, copies):
        @pl.when(when)
        def _():
            for one in copies:
                one.start()

        pending.append((when, copies))

    def packed_to(where, n, buffer, there, step):
        span = (spans if there[0] == "raw" else fine)[n]
        return copy(
            zs.at[span], buffer.at[c, span],
            place[where]((there, step, n)), recvs((there, n), 1 if there == "r" else 2), at(step),
        )

    parts = (pl.ds(0, wide), pl.ds(wide, wide))

    def map_to(slot, step):
        return [
            copy(
                gk.at[c, parts[n]], gc.at[slot, c, parts[n]],
                place[slot + 1](("map", step, n)), recvs((("map", slot), n), 2), at(step),
            )
            for n in range(2)
        ]

    own0 = g0f[c]
    w = mm(dh1f[c], g0f[c, mine])
    first[0].wait_recv()
    w += mm(dh1f[o], g0f[c, other])
    wb = w[:rows].astype(BF16)
    kappa = w[rows:] - h_ref[0].astype(F32)
    pm0[mine] = d_ref[0, mine] + mt(g0f[c], wb)

    raw_targets = (
        (i3 & inner, 2, (-1, -2)),
        (i2 & inner, 1, (-2,)),
        (i1, 0, (-1,)),
    )

    def start_raw(n):
        for when, slot, steps in raw_targets:
            emit_copies(
                when, [packed_to(slot + 1, n, zc.at[slot], ("raw", slot), step) for step in steps]
            )

    pack_first(pm0, kappa)
    emit_copies(i3 & top, [packed_to(3, n, zy, "y", -1) for n in range(2)])
    start_raw(0)
    first[1].wait_recv()
    pm0[other] = d_ref[0, other] + mt(g0f[o], wb)
    for n in range(2):
        pack_outer(pm0, n)
        emit_copies(i3 & top, [packed_to(3, 2 + n, zy, "y", -1)])

    first[2].wait_recv()
    gk[c, :rows] = times(g1f, body, own0).astype(BF16)
    gk[c, rows:] = kappa.astype(BF16)
    ahead_of_late = map_to(2, -2)
    late = map_to(2, -3)[:1]
    emit_copies(i3 & inner, map_to(2, -1))
    emit_copies(i2 & inner, map_to(1, -2))
    emit_copies(i1, map_to(0, -1))

    @pl.when(i3 & inner)
    def _():
        for one in ahead_of_late:
            one.start()

    start_raw(1)

    join = swap("gk", gk.at[c], gk.at[c])
    join.start()
    pm1[...] = d_ref[1]
    join.wait_recv()
    m0[...] = gk[...]
    m1[:, :rows] = g1f[...]
    m1[:, rows:] = -dh1f[:, rows:]

    def turn():
        for j in range(2):
            span = pl.ds(j * wide, wide)
            t0[span, :] = m0[j, :rows].T
            t1[span, :] = m1[j, :rows].T

    turn()

    handoffs = {}

    def arrive(when, name, ref, number, relay=None, relayed=None):
        here, there = recvs(name, 2), recvs(name, 2) + 1
        h = o if relayed is None else jnp.where(relayed, c, o)
        onward = copy(ref(h), ref(h), sends(("on", number)), there, mate)
        handoffs[name] = onward

        @pl.when(when)
        def _():
            copy(ref(h), ref(h), sends(("on", number)), here, mate).wait_recv()
            onward.start()

        if relay is not None:
            step, where = relay
            handed = copy(ref(h), ref(h), place[where](("relay", name)), here, at(step))
            emit_copies(when & (i == where), [handed])

    def collect(when, *names):
        @pl.when(when)
        def _():
            for name in names:
                handoffs[name].wait_recv()

    uses = (i0, inner & (i0 | i1), inner & jnp.logical_not(i3))
    relays = (None, (1, 0), (-2, 2))

    def block_arrives(slot, n, when=True):
        arrive(
            uses[slot] & when, (("raw", slot), n), lambda h: zc.at[slot, h, spans[n]],
            (slot % 2) * 4 + n, relays[slot], (None, i1, i0)[slot],
        )

    def map_arrives(slot, when=True):
        for n in range(2):
            arrive(
                uses[slot] & when, (("map", slot), n), lambda h: gc.at[slot, h, parts[n]],
                (slot % 2) * 4 + 2 + n, relays[slot] if slot == 1 or n == 1 else None,
                (None, i1, i0 if n == 1 else None)[slot],
            )

    def handed_on(slot):
        for n in range(2):
            handoffs[("raw", slot), n].wait_send()
            handoffs[("map", slot), n].wait_send()

    def swaps(slot):
        return [
            copy(xm0.at[slot, c], xm0.at[slot, c], sends("m0"), recvs(("m0", slot)), mate),
            copy(xm1.at[slot, c], xm1.at[slot, c], sends("m1"), recvs(("m1", slot)), mate),
        ]

    maps = ((m0, xm0, t0, pm0, 1.0), (m1, xm1, t1, pm1, -1.0))

    def compose(slot, n):
        m, x, _, _, sign = maps[n]
        own = m[c, :rows]
        edge = mm(fc[rows:], own)
        x[slot, c, rows:] = (m[c, rows:].astype(F32) + sign * edge).astype(BF16)
        x[slot, c, :rows] = times(gc.at[slot], body, own).astype(BF16)
        swaps(slot)[n].start()

    def extend(n):
        m, _, t, p, _ = maps[n]
        wb = mm(fc[:rows], m[c, :rows]).astype(BF16)
        for j in range(2):
            span = pl.ds(j * wide, wide)
            p[span] += mm(t[span, :], wb)

    def settle(slot, n):
        m, x, t, _, _ = maps[n]
        one = swaps(slot)[n]
        one.wait_recv()
        m[...] = x[slot]
        for j in range(2):
            t[pl.ds(j * wide, wide), :] = x[slot, j, :rows].T
        one.wait_send()

    later = i0 & top
    prompt = jnp.logical_not(later)
    lazy = i0 & inner
    across_mate = swap("pm1", held.at[c], held.at[c])
    started = jnp.logical_not(i3 & top)

    def y_arrives(n, when):
        arrive(
            started & when, ("y", n), lambda h: zy.at[h, fine[n]], (8, 9, 5, 10)[n], None, (i1 & inner) | i3
        )
        ref = zy.at[o, fine[n]]
        emit_copies(
            i0 & inner & when, [copy(ref, ref, place[0](("relay", n)), recvs(("y", n), 2), at(1))]
        )

    def block_whole(slot):
        for n in range(2):
            unpack_outer(zc.at[slot], fc, n)

    def merge(slot):
        raw, drawn = ("raw", slot), ("map", slot)
        use = uses[slot]
        collect(use, (raw, 0), (drawn, 0), (drawn, 1))

        @pl.when(use)
        def _():
            unpack_first(zc.at[slot], fc)
            compose(slot, 0)

            @pl.when(prompt)
            def _():
                compose(slot, 1)

        if slot == 0:
            block_arrives(1, 1)
            block_arrives(0, 1)
            block_arrives(2, 0, i1)
            map_arrives(2, i1)
            block_arrives(2, 1, i1)
        collect(use, (raw, 1))
        if slot == 0:
            y_arrives(0, later)
            y_arrives(1, later)

        @pl.when(use)
        def _():
            block_whole(slot)

            @pl.when(jnp.logical_not(lazy))
            def _():
                extend(0)

        if slot == 0:
            y_arrives(2, later)

        @pl.when(use)
        def _():
            settle(slot, 0)

            @pl.when(prompt)
            def _():
                extend(1)
                settle(slot, 1)

            handed_on(slot)

    block_arrives(1, 0)
    block_arrives(0, 0)
    map_arrives(1)
    map_arrives(0)
    merge(0)
    merge(1)
    early = jnp.logical_not(i1)
    block_arrives(2, 0, early)
    map_arrives(2, i2)
    block_arrives(2, 1, early)
    collect(uses[2], (("raw", 2), 0), (("raw", 2), 1))

    @pl.when(uses[2])
    def _():
        unpack_first(zc.at[2], fc)
        block_whole(2)
        extend(1)

        @pl.when(jnp.logical_not(lazy))
        def _():
            extend(0)

        @pl.when(lazy)
        def _():
            held[c] = pm1[...].astype(BF16)
            across_mate.start()

    y_arrives(0, lazy)
    y_arrives(1, lazy)
    map_arrives(2, i0)
    collect(uses[2], (("map", 2), 0), (("map", 2), 1))

    @pl.when(uses[2])
    def _():
        compose(2, 0)
        compose(2, 1)

    y_arrives(2, lazy)
    y_arrives(3, lazy)

    @pl.when(lazy)
    def _():
        across_mate.wait_recv()
        wb = times(held, body, g0f[c]).astype(BF16)
        pm0[mine] = d_ref[0, mine] + mt(g0f[c], wb)
        pm0[other] = d_ref[0, other] + mt(g0f[o], wb)
        across_mate.wait_send()

    @pl.when(uses[2])
    def _():
        settle(2, 0)
        settle(2, 1)
        handed_on(2)

    @pl.when(i3 & inner)
    def _():
        for one in ahead_of_late:
            one.wait_send()
        for one in late:
            one.start()

    pending.append((i3 & inner, late))

    cov = a_ref[...].astype(BF16)

    def edges(step, sign, m):
        for j in range(2):
            kb[step, j] = sign * mm(full[rows:], m[j, :rows]) + m[j, rows:].astype(F32)
        cross_ref[step] = mm(cov, kb[step, c].astype(BF16))

    @pl.when(jnp.logical_not(started))
    def _():
        full[...] = jnp.zeros_like(full)

    for n in range(3):
        y_arrives(n, jnp.logical_not(i0))
    collect(started, ("y", 0), ("y", 1))

    @pl.when(started)
    def _():
        unpack_first(zy, full)

    def close(m, n):
        return mm(full[parts[n], parts[n]], m[c, parts[n]])

    def far(m, n):
        return mm(full[parts[n], parts[1 - n]], m[c, parts[1 - n]])

    y_arrives(3, later | jnp.logical_not(i0))
    edges(0, 1.0, m0)
    begun = [close(m0, n) for n in range(2)]

    @pl.when(prompt)
    def _():
        edges(1, -1.0, m1)
        for n in range(2):
            half_done[parts[n]] = close(m1, n)

    for n in range(2):
        collect(started, ("y", 2 + n))

        @pl.when(started)
        def _():
            unpack_outer(zy, full, n)

    leads = i0 & passes
    heads = i2 & top

    def start_y(n):
        emit_copies(heads, [packed_to(2, n, zy, "y", -2)])
        emit_copies(leads, [packed_to(0, n, zy, "y", -4), packed_to(0, n, zr, "r", 1)])

    w = jnp.concatenate([begun[n] + far(m0, n) for n in range(2)], axis=0).astype(BF16)
    pm0[mine] += mm(t0[mine, :], w)

    @pl.when(leads | heads)
    def _():
        pack_first(pm0, kb[0, c])

    start_y(0)
    start_y(1)
    pm0[other] += mm(t0[other, :], w)

    for n in range(2):

        @pl.when(leads | heads)
        def _():
            pack_outer(pm0, n)

        start_y(2 + n)
    emit_copies(heads, [packed_to(2, n, zy, "y", -1) for n in range(4)])
    emit_copies(leads, [packed_to(0, n, zy, "y", -2) for n in range(4)])

    @pl.when(later)
    def _():
        compose(0, 1)
        extend(1)
        settle(0, 1)
        edges(1, -1.0, m1)
        for n in range(2):
            half_done[parts[n]] = close(m1, n)

    for n in range(2):
        w1[parts[n]] = (half_done[parts[n]] + far(m1, n)).astype(BF16)

    for n in range(4):
        ref = zr.at[o, fine[n]]
        there = zy.at[o, fine[n]]
        forth = copy(ref, there, place[1](("r", n)), recvs(("y", n), 2), at(-2))

        @pl.when(i1 & passes)
        def _():
            copy(ref, ref, place[1](("r", n)), recvs(("r", n)), at(-2)).wait_recv()

        emit_copies(i1 & passes, [forth])

    @pl.when(started)
    def _():
        for n in range(4):
            handoffs["y", n].wait_send()

    for one in first:
        one.wait_send()
    join.wait_send()
    for when, copies in pending:

        @pl.when(when)
        def _():
            for one in copies:
                one.wait_send()


def finish(w1, t1, pm0, pm1, kb, cross_ref, out_hbm, cross_hbm, out, store):
    wide = out.shape[2]
    ends = pltpu.make_async_copy(cross_ref, cross_hbm, store.at[4])
    ends.start()
    stores = []

    def emit(step, j, value):
        span = pl.ds(j * wide, wide)
        out[step, span] = value + mt(kb[step, j].astype(BF16), cross_ref[step].astype(BF16))
        one = pltpu.make_async_copy(out.at[step, span], out_hbm.at[step, span], store.at[2 * step + j])
        one.start()
        stores.append(one)

    for j in range(2):
        emit(0, j, pm0[pl.ds(j * wide, wide)])
    for j in range(2):
        span = pl.ds(j * wide, wide)
        emit(1, j, pm1[span] + mm(t1[span, :], w1[...]))
    ends.wait()
    for one in stores:
        one.wait()


def shards(diagonal_block_inverse, step_map, arrow_map, arrow_cov):
    count, nodes, wide = diagonal_block_inverse.shape
    effects = arrow_map.shape[1]
    tall = nodes + effects
    packed = 4 * (wide // 2) + 2 * effects + MARK
    vmem = pl.BlockSpec(memory_space=pltpu.VMEM)
    hbm = pl.BlockSpec(memory_space=pltpu.HBM)
    held = pl.pallas_call(
        kernel,
        out_shape=(
            jax.ShapeDtypeStruct((nodes, wide), BF16),
            jax.ShapeDtypeStruct((nodes, nodes), BF16),
            jax.ShapeDtypeStruct((nodes, wide), F32),
            jax.ShapeDtypeStruct((nodes, wide), F32),
            jax.ShapeDtypeStruct((count, 2, effects, wide), F32),
            jax.ShapeDtypeStruct((count, effects, wide), F32),
        ),
        in_specs=[hbm] * 4,
        out_specs=(vmem,) * 6,
        scratch_shapes=[
            pltpu.VMEM((count, nodes, wide), F32),
            pltpu.VMEM((count, effects, wide), BF16),
            pltpu.VMEM((effects, effects), F32),
            pltpu.VMEM((2, nodes, wide), BF16),
            pltpu.VMEM((2, nodes, wide), BF16),
            pltpu.VMEM((2, tall, wide), BF16),
            pltpu.VMEM((2, tall, wide), BF16),
            pltpu.VMEM((nodes, nodes), BF16),
            pltpu.VMEM((2, tall, wide), BF16),
            pltpu.VMEM((2, tall, wide), BF16),
            pltpu.VMEM((3, 2, tall, wide), BF16),
            pltpu.VMEM((3, 2, tall, wide), BF16),
            pltpu.VMEM((packed, wide // 2), BF16),
            pltpu.VMEM((2, packed, wide // 2), BF16),
            pltpu.VMEM((2, packed, wide // 2), BF16),
            pltpu.VMEM((3, 2, packed, wide // 2), BF16),
            pltpu.VMEM((3, 2, nodes, wide), BF16),
            pltpu.VMEM((tall, nodes), BF16),
            pltpu.VMEM((tall, nodes), BF16),
            pltpu.VMEM((nodes, wide), F32),
            pltpu.VMEM((2, nodes, wide), BF16),
            pltpu.SemaphoreType.DMA((SENDS,)),
            pltpu.SemaphoreType.DMA((RECVS,)),
            pltpu.SemaphoreType.DMA((6,)),
        ],
        compiler_params=pltpu.CompilerParams(
            collective_id=0, has_side_effects=True, vmem_limit_bytes=28 * 1024 * 1024
        ),
    )(*(
        pltpu.with_memory_space_constraint(array, pltpu.HBM)
        for array in (diagonal_block_inverse, step_map, arrow_map, arrow_cov)
    ))
    return pl.pallas_call(
        finish,
        out_shape=(
            jax.ShapeDtypeStruct((count, nodes, wide), F32),
            jax.ShapeDtypeStruct((count, effects, wide), F32),
        ),
        in_specs=[vmem] * 6,
        out_specs=(hbm, hbm),
        scratch_shapes=[
            pltpu.VMEM((count, nodes, wide), F32),
            pltpu.SemaphoreType.DMA((5,)),
        ],
        compiler_params=pltpu.CompilerParams(vmem_limit_bytes=28 * 1024 * 1024),
    )(*held)


def solution(mesh):
    return jax.shard_map(
        shards,
        mesh=mesh,
        in_specs=(
            P(("rep", "tm"), None, "col"),
            P(("rep", "tm"), None, "col"),
            P(("rep", "tm"), None, "col"),
            P("rep", None),
        ),
        out_specs=(P(("rep", "tm"), None, "col"), P(("rep", "tm"), None, "col")),
        check_vma=False,
    )
```

```python
import jax
import jax.numpy as jnp
from jax import lax
from jax.experimental import pallas as pl
from jax.experimental.pallas import tpu as pltpu
from jax.sharding import PartitionSpec as P

MESH = pl.DeviceIdType.MESH
F32 = jnp.float32
BF16 = jnp.bfloat16
SENDS = 38
RECVS = 47
MARK = 16


def mm(left, right):
    return jnp.dot(left, right, preferred_element_type=F32)


def mt(left, right):
    return lax.dot_general(left, right, (((0,), (0,)), ((), ())), preferred_element_type=F32)


class Slots:
    def __init__(self, start, end):
        self.found = {}
        self.free = start
        self.end = end

    def __call__(self, name, width=1):
        if name not in self.found:
            self.found[name] = self.free
            self.free += width
            assert self.free <= self.end
        return self.found[name]


def kernel(
    d_hbm, g_hbm, h_hbm, a_hbm,
    w1, t1, pm0, pm1, kb, cross_ref,
    d_ref, h_ref, a_ref, g0f, g1f, dh1f, gk, t0, m0, m1, xm0, xm1,
    zs, zy, zr, zc, gc, fc, full, half_done, held,
    send, recv, load,
):
    rows = g0f.shape[1]
    wide = g0f.shape[2]
    tall = gk.shape[1]
    half = wide // 2
    edge_rows = tall - rows
    tm = lax.axis_index("tm")
    c = lax.axis_index("col")
    o = 1 - c
    quads = lax.axis_size("tm") // 4
    q = tm // 4
    i = tm % 4
    top = q == quads - 1
    inner = jnp.logical_not(top)
    passes = q > 0
    i0, i1, i2, i3 = (i == n for n in range(4))
    mate = {"col": o}
    recvs = Slots(0, RECVS)
    sends = Slots(0, 18)
    place = [Slots(18, SENDS) for _ in range(4)]

    def at(step):
        return {"tm": tm + step, "col": o}

    def copy(src, dst, sem, sem_there, device):
        return pltpu.make_async_remote_copy(
            src_ref=src, dst_ref=dst, send_sem=send.at[sem], recv_sem=recv.at[sem_there],
            device_id=device, device_id_type=MESH,
        )

    loads = [
        pltpu.make_async_copy(d_hbm.at[1], d_ref.at[1], load.at[0]),
        pltpu.make_async_copy(h_hbm, h_ref, load.at[1]),
        pltpu.make_async_copy(g_hbm.at[0], g0f.at[c], load.at[2]),
        pltpu.make_async_copy(g_hbm.at[1], g1f.at[c], load.at[3]),
        pltpu.make_async_copy(d_hbm.at[0], d_ref.at[0], load.at[4]),
        pltpu.make_async_copy(a_hbm, a_ref, load.at[5]),
    ]
    for one in loads:
        one.start()

    barrier = pltpu.get_barrier_semaphore()
    pl.semaphore_signal(barrier, inc=1, device_id=mate, device_id_type=MESH)

    def greet(when, steps):
        @pl.when(when)
        def _():
            for step in steps:
                pl.semaphore_signal(barrier, inc=1, device_id=at(step), device_id_type=MESH)

    greet(i0, (1, 2))
    greet(i0 & inner, (3, 4))
    greet(i1, (-1,))
    greet(i1 & inner, (2,))
    greet(i1 & top, (1,))
    greet(i2, (1,))
    greet(i2 & inner, (2,))
    greet(i3 & inner, (2,))

    def one_if(flag):
        return jnp.where(flag, 1, 0)

    targets = (
        1 + 2 * one_if(i3 & inner) + one_if(i2 & top) + one_if(i1 & passes) + 2 * one_if(i0 & passes)
    )

    loads[0].wait()
    loads[1].wait()
    dh1f[c, :rows] = d_ref[1].astype(BF16)
    dh1f[c, rows:] = h_ref[1]
    pl.semaphore_wait(barrier, 1 + targets)

    def swap(name, src, dst):
        return copy(src, dst, sends(name), recvs(name), mate)

    first = [
        swap("dh1", dh1f.at[c], dh1f.at[c]),
        swap("g0", g_hbm.at[0], g0f.at[c]),
        swap("g1", g_hbm.at[1], g1f.at[c]),
    ]
    for one in first:
        one.start()
    for one in loads[2:]:
        one.wait()

    def times(left, span, right):
        return mm(jnp.concatenate([left[0, span], left[1, span]], axis=1), right)

    body = pl.ds(0, rows)
    mine = pl.ds(pl.multiple_of(c * wide, wide), wide)
    other = pl.ds(pl.multiple_of(o * wide, wide), wide)
    edge_base = 2 * half
    mark_base = edge_base + 2 * edge_rows
    first_rows = mark_base + MARK
    top_span = pl.ds(0, first_rows)
    low_span = pl.ds(first_rows, zs.shape[0] - first_rows)
    spans = (top_span, low_span)
    middle = first_rows // 32 * 16
    fine = (
        pl.ds(0, middle), pl.ds(middle, first_rows - middle),
        pl.ds(first_rows, half), pl.ds(first_rows + half, half),
    )
    across = lax.broadcasted_iota(jnp.int32, (half, half), 1)
    down = lax.broadcasted_iota(jnp.int32, (half, half), 0)

    def pack_first(p, edge):
        r = pl.multiple_of(c * wide, wide)
        one = p[pl.ds(r, half), :half]
        two = p[pl.ds(r + half, half), half:]
        zs[:half] = jnp.where(down >= across, one, two).astype(BF16)
        zs[half:edge_base] = p[pl.ds(r, half), half:].astype(BF16)
        zs[edge_base : edge_base + edge_rows] = edge[:, :half].astype(BF16)
        zs[edge_base + edge_rows : mark_base] = edge[:, half:].astype(BF16)
        mark = jnp.sum(jnp.where(down == across, two, 0.0), axis=0, keepdims=True)
        zs[mark_base:first_rows] = jnp.broadcast_to(mark, (MARK, half)).astype(BF16)

    def pack_outer(p, n):
        to = fine[2 + n]

        @pl.when(c == 0)
        def _():
            zs[to] = p[pl.ds(wide + n * half, half), :half].astype(BF16)

        @pl.when(c == 1)
        def _():
            zs[to] = p[half:wide, pl.ds(n * half, half)].astype(BF16)

    def unpack_first(z, full):
        for j in range(2):
            base = j * wide
            lo = pl.ds(base, half)
            hi = pl.ds(base + half, half)
            both = z[j, :half].astype(F32)
            turned = both.T
            mark = z[j, mark_base:first_rows].astype(F32)[:1]
            full[lo, lo] = jnp.where(down >= across, both, turned).astype(BF16)
            full[hi, hi] = jnp.where(
                down < across, both, jnp.where(down == across, mark, turned)
            ).astype(BF16)
            side = z[j, half:edge_base]
            full[lo, hi] = side
            full[hi, lo] = side.T
            for n in range(2):
                full[rows:, pl.ds(base + n * half, half)] = z[
                    j, edge_base + n * edge_rows : edge_base + (n + 1) * edge_rows
                ]

    def unpack_outer(z, full, n):
        far = pl.ds(wide + n * half, half)
        for j in range(2):
            close = pl.ds(j * half, half)
            outer = z[j, fine[2 + n]]
            if j == 0:
                full[far, close] = outer
                full[close, far] = outer.T
            else:
                full[close, far] = outer
                full[far, close] = outer.T

    pending = []

    def emit_copies(when, copies):
        @pl.when(when)
        def _():
            for one in copies:
                one.start()

        pending.append((when, copies))

    def packed_to(where, n, buffer, there, step):
        span = (spans if there[0] == "raw" else fine)[n]
        return copy(
            zs.at[span], buffer.at[c, span],
            place[where]((there, step, n)), recvs((there, n), 1 if there == "r" else 2), at(step),
        )

    parts = (pl.ds(0, wide), pl.ds(wide, wide))

    def map_to(slot, step):
        return [
            copy(
                gk.at[c, parts[n]], gc.at[slot, c, parts[n]],
                place[slot + 1](("map", step, n)), recvs((("map", slot), n), 2), at(step),
            )
            for n in range(2)
        ]

    own0 = g0f[c]
    w = mm(dh1f[c], g0f[c, mine])
    first[0].wait_recv()
    w += mm(dh1f[o], g0f[c, other])
    wb = w[:rows].astype(BF16)
    kappa = w[rows:] - h_ref[0].astype(F32)
    pm0[mine] = d_ref[0, mine] + mt(g0f[c], wb)

    raw_targets = (
        (i3 & inner, 2, (-1, -2)),
        (i2 & inner, 1, (-2,)),
        (i1, 0, (-1,)),
    )

    def start_raw(n):
        for when, slot, steps in raw_targets:
            emit_copies(
                when, [packed_to(slot + 1, n, zc.at[slot], ("raw", slot), step) for step in steps]
            )

    pack_first(pm0, kappa)
    emit_copies(i3 & top, [packed_to(3, n, zy, "y", -1) for n in range(2)])
    start_raw(0)
    first[1].wait_recv()
    pm0[other] = d_ref[0, other] + mt(g0f[o], wb)
    for n in range(2):
        pack_outer(pm0, n)
        emit_copies(i3 & top, [packed_to(3, 2 + n, zy, "y", -1)])

    first[2].wait_recv()
    gk[c, :rows] = times(g1f, body, own0).astype(BF16)
    gk[c, rows:] = kappa.astype(BF16)
    ahead_of_late = map_to(2, -2)
    late = map_to(2, -3)[:1]
    emit_copies(i3 & inner, map_to(2, -1))
    emit_copies(i2 & inner, map_to(1, -2))
    emit_copies(i1, map_to(0, -1))

    @pl.when(i3 & inner)
    def _():
        for one in ahead_of_late:
            one.start()

    start_raw(1)

    join = swap("gk", gk.at[c], gk.at[c])
    join.start()
    pm1[...] = d_ref[1]
    join.wait_recv()
    m0[...] = gk[...]
    m1[:, :rows] = g1f[...]
    m1[:, rows:] = -dh1f[:, rows:]

    def turn():
        for j in range(2):
            span = pl.ds(j * wide, wide)
            t0[span, :] = m0[j, :rows].T
            t1[span, :] = m1[j, :rows].T

    turn()

    handoffs = {}

    def arrive(when, name, ref, number, relay=None, relayed=None):
        here, there = recvs(name, 2), recvs(name, 2) + 1
        h = o if relayed is None else jnp.where(relayed, c, o)
        onward = copy(ref(h), ref(h), sends(("on", number)), there, mate)
        handoffs[name] = onward

        @pl.when(when)
        def _():
            copy(ref(h), ref(h), sends(("on", number)), here, mate).wait_recv()
            onward.start()

        if relay is not None:
            step, where = relay
            handed = copy(ref(h), ref(h), place[where](("relay", name)), here, at(step))
            emit_copies(when & (i == where), [handed])

    def collect(when, *names):
        @pl.when(when)
        def _():
            for name in names:
                handoffs[name].wait_recv()

    uses = (i0, inner & (i0 | i1), inner & jnp.logical_not(i3))
    relays = (None, (1, 0), (-2, 2))

    def block_arrives(slot, n, when=True):
        arrive(
            uses[slot] & when, (("raw", slot), n), lambda h: zc.at[slot, h, spans[n]],
            (slot % 2) * 4 + n, relays[slot], (None, i1, i0)[slot],
        )

    def map_arrives(slot, when=True):
        for n in range(2):
            arrive(
                uses[slot] & when, (("map", slot), n), lambda h: gc.at[slot, h, parts[n]],
                (slot % 2) * 4 + 2 + n, relays[slot] if slot == 1 or n == 1 else None,
                (None, i1, i0 if n == 1 else None)[slot],
            )

    def handed_on(slot):
        for n in range(2):
            handoffs[("raw", slot), n].wait_send()
            handoffs[("map", slot), n].wait_send()

    def swaps(slot):
        return [
            copy(xm0.at[slot, c], xm0.at[slot, c], sends("m0"), recvs(("m0", slot)), mate),
            copy(xm1.at[slot, c], xm1.at[slot, c], sends("m1"), recvs(("m1", slot)), mate),
        ]

    maps = ((m0, xm0, t0, pm0, 1.0), (m1, xm1, t1, pm1, -1.0))

    def compose(slot, n):
        m, x, _, _, sign = maps[n]
        own = m[c, :rows]
        edge = mm(fc[rows:], own)
        x[slot, c, rows:] = (m[c, rows:].astype(F32) + sign * edge).astype(BF16)
        x[slot, c, :rows] = times(gc.at[slot], body, own).astype(BF16)
        swaps(slot)[n].start()

    def extend(n):
        m, _, t, p, _ = maps[n]
        wb = mm(fc[:rows], m[c, :rows]).astype(BF16)
        for j in range(2):
            span = pl.ds(j * wide, wide)
            p[span] += mm(t[span, :], wb)

    def settle(slot, n):
        m, x, t, _, _ = maps[n]
        one = swaps(slot)[n]
        one.wait_recv()
        m[...] = x[slot]
        for j in range(2):
            t[pl.ds(j * wide, wide), :] = x[slot, j, :rows].T
        one.wait_send()

    later = i0 & top
    prompt = jnp.logical_not(later)
    lazy = i0 & inner
    across_mate = swap("pm1", held.at[c], held.at[c])
    started = jnp.logical_not(i3 & top)

    def y_arrives(n, when):
        arrive(
            started & when, ("y", n), lambda h: zy.at[h, fine[n]], (8, 9, 5, 10)[n], None, (i1 & inner) | i3
        )
        ref = zy.at[o, fine[n]]
        emit_copies(
            i0 & inner & when, [copy(ref, ref, place[0](("relay", n)), recvs(("y", n), 2), at(1))]
        )

    def block_whole(slot):
        for n in range(2):
            unpack_outer(zc.at[slot], fc, n)

    def merge(slot):
        raw, drawn = ("raw", slot), ("map", slot)
        use = uses[slot]
        collect(use, (raw, 0), (drawn, 0), (drawn, 1))

        @pl.when(use)
        def _():
            unpack_first(zc.at[slot], fc)
            compose(slot, 0)

            @pl.when(prompt)
            def _():
                compose(slot, 1)

        if slot == 0:
            block_arrives(1, 1)
            block_arrives(0, 1)
            block_arrives(2, 0, i1)
            map_arrives(2, i1)
            block_arrives(2, 1, i1)
        collect(use, (raw, 1))
        if slot == 0:
            y_arrives(0, later)
            y_arrives(1, later)

        @pl.when(use)
        def _():
            block_whole(slot)

            @pl.when(jnp.logical_not(lazy))
            def _():
                extend(0)

        if slot == 0:
            y_arrives(2, later)

        @pl.when(use)
        def _():
            settle(slot, 0)

            @pl.when(prompt)
            def _():
                extend(1)
                settle(slot, 1)

            handed_on(slot)

    block_arrives(1, 0)
    block_arrives(0, 0)
    map_arrives(1)
    map_arrives(0)
    merge(0)
    merge(1)
    early = jnp.logical_not(i1)
    block_arrives(2, 0, early)
    map_arrives(2, i2)
    block_arrives(2, 1, early)
    collect(uses[2], (("raw", 2), 0), (("raw", 2), 1))

    @pl.when(uses[2])
    def _():
        unpack_first(zc.at[2], fc)
        block_whole(2)
        extend(1)

        @pl.when(jnp.logical_not(lazy))
        def _():
            extend(0)

        @pl.when(lazy)
        def _():
            held[c] = pm1[...].astype(BF16)
            across_mate.start()

    y_arrives(0, lazy)
    y_arrives(1, lazy)
    map_arrives(2, i0)
    collect(uses[2], (("map", 2), 0), (("map", 2), 1))

    @pl.when(uses[2])
    def _():
        compose(2, 0)
        compose(2, 1)

    y_arrives(2, lazy)
    y_arrives(3, lazy)

    @pl.when(lazy)
    def _():
        across_mate.wait_recv()
        wb = times(held, body, g0f[c]).astype(BF16)
        pm0[mine] = d_ref[0, mine] + mt(g0f[c], wb)
        pm0[other] = d_ref[0, other] + mt(g0f[o], wb)
        across_mate.wait_send()

    @pl.when(uses[2])
    def _():
        settle(2, 0)
        settle(2, 1)
        handed_on(2)

    @pl.when(i3 & inner)
    def _():
        for one in ahead_of_late:
            one.wait_send()
        for one in late:
            one.start()

    pending.append((i3 & inner, late))

    cov = a_ref[...].astype(BF16)

    def edges(step, sign, m):
        for j in range(2):
            kb[step, j] = sign * mm(full[rows:], m[j, :rows]) + m[j, rows:].astype(F32)
        cross_ref[step] = mm(cov, kb[step, c].astype(BF16))

    @pl.when(jnp.logical_not(started))
    def _():
        full[...] = jnp.zeros_like(full)

    for n in range(3):
        y_arrives(n, jnp.logical_not(i0))
    collect(started, ("y", 0), ("y", 1))

    @pl.when(started)
    def _():
        unpack_first(zy, full)

    def close(m, n):
        return mm(full[parts[n], parts[n]], m[c, parts[n]])

    def far(m, n):
        return mm(full[parts[n], parts[1 - n]], m[c, parts[1 - n]])

    y_arrives(3, later | jnp.logical_not(i0))
    edges(0, 1.0, m0)
    begun = [close(m0, n) for n in range(2)]

    @pl.when(prompt)
    def _():
        edges(1, -1.0, m1)
        for n in range(2):
            half_done[parts[n]] = close(m1, n)

    for n in range(2):
        collect(started, ("y", 2 + n))

        @pl.when(started)
        def _():
            unpack_outer(zy, full, n)

    leads = i0 & passes
    heads = i2 & top

    gates = []

    def start_y(n):
        to_heir, to_next = packed_to(2, n, zy, "y", -2), packed_to(0, n, zy, "y", -4)
        emit_copies(leads, [packed_to(0, n, zr, "r", 1)])
        for when, one in ((heads, to_heir), (leads, to_next)):
            if n != 2:
                emit_copies(when, [one])
                continue
            gates.append((when, one))

            @pl.when(when)
            def _():
                one.start()

    w = jnp.concatenate([begun[n] + far(m0, n) for n in range(2)], axis=0).astype(BF16)
    pm0[mine] += mm(t0[mine, :], w)

    @pl.when(leads | heads)
    def _():
        pack_first(pm0, kb[0, c])

    start_y(0)
    start_y(1)
    pm0[other] += mm(t0[other, :], w)

    for n in range(2):

        @pl.when(leads | heads)
        def _():
            pack_outer(pm0, n)

        start_y(2 + n)
    for when, one in gates:

        @pl.when(when)
        def _():
            one.wait_send()

    emit_copies(heads, [packed_to(2, n, zy, "y", -1) for n in range(4)])
    emit_copies(leads, [packed_to(0, n, zy, "y", -2) for n in range(4)])

    @pl.when(later)
    def _():
        compose(0, 1)
        extend(1)
        settle(0, 1)
        edges(1, -1.0, m1)
        for n in range(2):
            half_done[parts[n]] = close(m1, n)

    for n in range(2):
        w1[parts[n]] = (half_done[parts[n]] + far(m1, n)).astype(BF16)

    for n in range(4):
        ref = zr.at[o, fine[n]]
        there = zy.at[o, fine[n]]
        forth = copy(ref, there, place[1](("r", n)), recvs(("y", n), 2), at(-2))

        @pl.when(i1 & passes)
        def _():
            copy(ref, ref, place[1](("r", n)), recvs(("r", n)), at(-2)).wait_recv()

        emit_copies(i1 & passes, [forth])

    @pl.when(started)
    def _():
        for n in range(4):
            handoffs["y", n].wait_send()

    for one in first:
        one.wait_send()
    join.wait_send()
    for when, copies in pending:

        @pl.when(when)
        def _():
            for one in copies:
                one.wait_send()


def finish(w1, t1, pm0, pm1, kb, cross_ref, out_hbm, cross_hbm, out, store):
    wide = out.shape[2]
    ends = pltpu.make_async_copy(cross_ref, cross_hbm, store.at[4])
    ends.start()
    stores = []

    def emit(step, j, value):
        span = pl.ds(j * wide, wide)
        out[step, span] = value + mt(kb[step, j].astype(BF16), cross_ref[step].astype(BF16))
        one = pltpu.make_async_copy(out.at[step, span], out_hbm.at[step, span], store.at[2 * step + j])
        one.start()
        stores.append(one)

    for j in range(2):
        emit(0, j, pm0[pl.ds(j * wide, wide)])
    for j in range(2):
        span = pl.ds(j * wide, wide)
        emit(1, j, pm1[span] + mm(t1[span, :], w1[...]))
    ends.wait()
    for one in stores:
        one.wait()


def shards(diagonal_block_inverse, step_map, arrow_map, arrow_cov):
    count, nodes, wide = diagonal_block_inverse.shape
    effects = arrow_map.shape[1]
    tall = nodes + effects
    packed = 4 * (wide // 2) + 2 * effects + MARK
    vmem = pl.BlockSpec(memory_space=pltpu.VMEM)
    hbm = pl.BlockSpec(memory_space=pltpu.HBM)
    held = pl.pallas_call(
        kernel,
        out_shape=(
            jax.ShapeDtypeStruct((nodes, wide), BF16),
            jax.ShapeDtypeStruct((nodes, nodes), BF16),
            jax.ShapeDtypeStruct((nodes, wide), F32),
            jax.ShapeDtypeStruct((nodes, wide), F32),
            jax.ShapeDtypeStruct((count, 2, effects, wide), F32),
            jax.ShapeDtypeStruct((count, effects, wide), F32),
        ),
        in_specs=[hbm] * 4,
        out_specs=(vmem,) * 6,
        scratch_shapes=[
            pltpu.VMEM((count, nodes, wide), F32),
            pltpu.VMEM((count, effects, wide), BF16),
            pltpu.VMEM((effects, effects), F32),
            pltpu.VMEM((2, nodes, wide), BF16),
            pltpu.VMEM((2, nodes, wide), BF16),
            pltpu.VMEM((2, tall, wide), BF16),
            pltpu.VMEM((2, tall, wide), BF16),
            pltpu.VMEM((nodes, nodes), BF16),
            pltpu.VMEM((2, tall, wide), BF16),
            pltpu.VMEM((2, tall, wide), BF16),
            pltpu.VMEM((3, 2, tall, wide), BF16),
            pltpu.VMEM((3, 2, tall, wide), BF16),
            pltpu.VMEM((packed, wide // 2), BF16),
            pltpu.VMEM((2, packed, wide // 2), BF16),
            pltpu.VMEM((2, packed, wide // 2), BF16),
            pltpu.VMEM((3, 2, packed, wide // 2), BF16),
            pltpu.VMEM((3, 2, nodes, wide), BF16),
            pltpu.VMEM((tall, nodes), BF16),
            pltpu.VMEM((tall, nodes), BF16),
            pltpu.VMEM((nodes, wide), F32),
            pltpu.VMEM((2, nodes, wide), BF16),
            pltpu.SemaphoreType.DMA((SENDS,)),
            pltpu.SemaphoreType.DMA((RECVS,)),
            pltpu.SemaphoreType.DMA((6,)),
        ],
        compiler_params=pltpu.CompilerParams(
            collective_id=0, has_side_effects=True, vmem_limit_bytes=28 * 1024 * 1024
        ),
    )(*(
        pltpu.with_memory_space_constraint(array, pltpu.HBM)
        for array in (diagonal_block_inverse, step_map, arrow_map, arrow_cov)
    ))
    return pl.pallas_call(
        finish,
        out_shape=(
            jax.ShapeDtypeStruct((count, nodes, wide), F32),
            jax.ShapeDtypeStruct((count, effects, wide), F32),
        ),
        in_specs=[vmem] * 6,
        out_specs=(hbm, hbm),
        scratch_shapes=[
            pltpu.VMEM((count, nodes, wide), F32),
            pltpu.SemaphoreType.DMA((5,)),
        ],
        compiler_params=pltpu.CompilerParams(vmem_limit_bytes=28 * 1024 * 1024),
    )(*held)


def solution(mesh):
    return jax.shard_map(
        shards,
        mesh=mesh,
        in_specs=(
            P(("rep", "tm"), None, "col"),
            P(("rep", "tm"), None, "col"),
            P(("rep", "tm"), None, "col"),
            P("rep", None),
        ),
        out_specs=(P(("rep", "tm"), None, "col"), P(("rep", "tm"), None, "col")),
        check_vma=False,
    )
```

```python
import jax
import jax.numpy as jnp
from jax import lax
from jax.experimental import pallas as pl
from jax.experimental.pallas import tpu as pltpu
from jax.sharding import PartitionSpec as P

MESH = pl.DeviceIdType.MESH
F32 = jnp.float32
BF16 = jnp.bfloat16
SENDS = 38
RECVS = 47
MARK = 16


def mm(left, right):
    return jnp.dot(left, right, preferred_element_type=F32)


def mt(left, right):
    return lax.dot_general(left, right, (((0,), (0,)), ((), ())), preferred_element_type=F32)


class Slots:
    def __init__(self, start, end):
        self.found = {}
        self.free = start
        self.end = end

    def __call__(self, name, width=1):
        if name not in self.found:
            self.found[name] = self.free
            self.free += width
            assert self.free <= self.end
        return self.found[name]


def kernel(
    d_hbm, g_hbm, h_hbm, a_hbm,
    w1, t1, pm0, pm1, kb, cross_ref,
    d_ref, h_ref, a_ref, g0f, g1f, dh1f, gk, t0, m0, m1, xm0, xm1,
    zs, zy, zr, zc, gc, fc, full, half_done, held,
    send, recv, load,
):
    rows = g0f.shape[1]
    wide = g0f.shape[2]
    tall = gk.shape[1]
    half = wide // 2
    edge_rows = tall - rows
    tm = lax.axis_index("tm")
    c = lax.axis_index("col")
    o = 1 - c
    quads = lax.axis_size("tm") // 4
    q = tm // 4
    i = tm % 4
    top = q == quads - 1
    inner = jnp.logical_not(top)
    passes = q > 0
    i0, i1, i2, i3 = (i == n for n in range(4))
    mate = {"col": o}
    recvs = Slots(0, RECVS)
    sends = Slots(0, 18)
    place = [Slots(18, SENDS) for _ in range(4)]

    def at(step):
        return {"tm": tm + step, "col": o}

    def copy(src, dst, sem, sem_there, device):
        return pltpu.make_async_remote_copy(
            src_ref=src, dst_ref=dst, send_sem=send.at[sem], recv_sem=recv.at[sem_there],
            device_id=device, device_id_type=MESH,
        )

    loads = [
        pltpu.make_async_copy(d_hbm.at[1], d_ref.at[1], load.at[0]),
        pltpu.make_async_copy(h_hbm, h_ref, load.at[1]),
        pltpu.make_async_copy(g_hbm.at[0], g0f.at[c], load.at[2]),
        pltpu.make_async_copy(g_hbm.at[1], g1f.at[c], load.at[3]),
        pltpu.make_async_copy(d_hbm.at[0], d_ref.at[0], load.at[4]),
        pltpu.make_async_copy(a_hbm, a_ref, load.at[5]),
    ]
    for one in loads:
        one.start()

    barrier = pltpu.get_barrier_semaphore()
    pl.semaphore_signal(barrier, inc=1, device_id=mate, device_id_type=MESH)

    def greet(when, steps):
        @pl.when(when)
        def _():
            for step in steps:
                pl.semaphore_signal(barrier, inc=1, device_id=at(step), device_id_type=MESH)

    greet(i0, (1, 2))
    greet(i0 & inner, (3, 4))
    greet(i1, (-1,))
    greet(i1 & inner, (2,))
    greet(i1 & top, (1,))
    greet(i2, (1,))
    greet(i2 & inner, (2,))
    greet(i3 & inner, (2,))

    def one_if(flag):
        return jnp.where(flag, 1, 0)

    targets = (
        1 + 2 * one_if(i3 & inner) + one_if(i2 & top) + one_if(i1 & passes) + 2 * one_if(i0 & passes)
    )

    loads[0].wait()
    loads[1].wait()
    dh1f[c, :rows] = d_ref[1].astype(BF16)
    dh1f[c, rows:] = h_ref[1]
    pl.semaphore_wait(barrier, 1 + targets)

    def swap(name, src, dst):
        return copy(src, dst, sends(name), recvs(name), mate)

    first = [
        swap("dh1", dh1f.at[c], dh1f.at[c]),
        swap("g0", g_hbm.at[0], g0f.at[c]),
        swap("g1", g_hbm.at[1], g1f.at[c]),
    ]
    for one in first:
        one.start()
    for one in loads[2:]:
        one.wait()

    def times(left, span, right):
        return mm(jnp.concatenate([left[0, span], left[1, span]], axis=1), right)

    body = pl.ds(0, rows)
    mine = pl.ds(pl.multiple_of(c * wide, wide), wide)
    other = pl.ds(pl.multiple_of(o * wide, wide), wide)
    edge_base = 2 * half
    mark_base = edge_base + 2 * edge_rows
    first_rows = mark_base + MARK
    top_span = pl.ds(0, first_rows)
    low_span = pl.ds(first_rows, zs.shape[0] - first_rows)
    spans = (top_span, low_span)
    middle = first_rows // 32 * 16
    fine = (
        pl.ds(0, middle), pl.ds(middle, first_rows - middle),
        pl.ds(first_rows, half), pl.ds(first_rows + half, half),
    )
    across = lax.broadcasted_iota(jnp.int32, (half, half), 1)
    down = lax.broadcasted_iota(jnp.int32, (half, half), 0)

    def pack_first(p, edge):
        r = pl.multiple_of(c * wide, wide)
        one = p[pl.ds(r, half), :half]
        two = p[pl.ds(r + half, half), half:]
        zs[:half] = jnp.where(down >= across, one, two).astype(BF16)
        zs[half:edge_base] = p[pl.ds(r, half), half:].astype(BF16)
        zs[edge_base : edge_base + edge_rows] = edge[:, :half].astype(BF16)
        zs[edge_base + edge_rows : mark_base] = edge[:, half:].astype(BF16)
        mark = jnp.sum(jnp.where(down == across, two, 0.0), axis=0, keepdims=True)
        zs[mark_base:first_rows] = jnp.broadcast_to(mark, (MARK, half)).astype(BF16)

    def pack_outer(p, n):
        to = fine[2 + n]

        @pl.when(c == 0)
        def _():
            zs[to] = p[pl.ds(wide + n * half, half), :half].astype(BF16)

        @pl.when(c == 1)
        def _():
            zs[to] = p[half:wide, pl.ds(n * half, half)].astype(BF16)

    def unpack_first(z, full):
        for j in range(2):
            base = j * wide
            lo = pl.ds(base, half)
            hi = pl.ds(base + half, half)
            both = z[j, :half].astype(F32)
            turned = both.T
            mark = z[j, mark_base:first_rows].astype(F32)[:1]
            full[lo, lo] = jnp.where(down >= across, both, turned).astype(BF16)
            full[hi, hi] = jnp.where(
                down < across, both, jnp.where(down == across, mark, turned)
            ).astype(BF16)
            side = z[j, half:edge_base]
            full[lo, hi] = side
            full[hi, lo] = side.T
            for n in range(2):
                full[rows:, pl.ds(base + n * half, half)] = z[
                    j, edge_base + n * edge_rows : edge_base + (n + 1) * edge_rows
                ]

    def unpack_outer(z, full, n):
        far = pl.ds(wide + n * half, half)
        for j in range(2):
            close = pl.ds(j * half, half)
            outer = z[j, fine[2 + n]]
            if j == 0:
                full[far, close] = outer
                full[close, far] = outer.T
            else:
                full[close, far] = outer
                full[far, close] = outer.T

    pending = []

    def emit_copies(when, copies):
        @pl.when(when)
        def _():
            for one in copies:
                one.start()

        pending.append((when, copies))

    def packed_to(where, n, buffer, there, step):
        span = (spans if there[0] == "raw" else fine)[n]
        return copy(
            zs.at[span], buffer.at[c, span],
            place[where]((there, step, n)), recvs((there, n), 1 if there == "r" else 2), at(step),
        )

    parts = (pl.ds(0, wide), pl.ds(wide, wide))

    def map_to(slot, step):
        return [
            copy(
                gk.at[c, parts[n]], gc.at[slot, c, parts[n]],
                place[slot + 1](("map", step, n)), recvs((("map", slot), n), 2), at(step),
            )
            for n in range(2)
        ]

    own0 = g0f[c]
    w = mm(dh1f[c], g0f[c, mine])
    first[0].wait_recv()
    w += mm(dh1f[o], g0f[c, other])
    wb = w[:rows].astype(BF16)
    kappa = w[rows:] - h_ref[0].astype(F32)
    pm0[mine] = d_ref[0, mine] + mt(g0f[c], wb)

    raw_targets = (
        (i3 & inner, 2, (-1, -2)),
        (i2 & inner, 1, (-2,)),
        (i1, 0, (-1,)),
    )

    def start_raw(n):
        for when, slot, steps in raw_targets:
            emit_copies(
                when, [packed_to(slot + 1, n, zc.at[slot], ("raw", slot), step) for step in steps]
            )

    pack_first(pm0, kappa)
    emit_copies(i3 & top, [packed_to(3, n, zy, "y", -1) for n in range(2)])
    start_raw(0)
    first[1].wait_recv()
    pm0[other] = d_ref[0, other] + mt(g0f[o], wb)
    for n in range(2):
        pack_outer(pm0, n)
        emit_copies(i3 & top, [packed_to(3, 2 + n, zy, "y", -1)])

    first[2].wait_recv()
    gk[c, :rows] = times(g1f, body, own0).astype(BF16)
    gk[c, rows:] = kappa.astype(BF16)
    ahead_of_late = map_to(2, -2)
    late = map_to(2, -3)[:1]
    emit_copies(i3 & inner, map_to(2, -1))
    emit_copies(i2 & inner, map_to(1, -2))
    emit_copies(i1, map_to(0, -1))

    @pl.when(i3 & inner)
    def _():
        for one in ahead_of_late:
            one.start()

    start_raw(1)

    join = swap("gk", gk.at[c], gk.at[c])
    join.start()
    pm1[...] = d_ref[1]
    join.wait_recv()
    m0[...] = gk[...]
    m1[:, :rows] = g1f[...]
    m1[:, rows:] = -dh1f[:, rows:]

    def turn():
        for j in range(2):
            span = pl.ds(j * wide, wide)
            t0[span, :] = m0[j, :rows].T
            t1[span, :] = m1[j, :rows].T

    turn()

    handoffs = {}

    def arrive(when, name, ref, number, relay=None, relayed=None):
        here, there = recvs(name, 2), recvs(name, 2) + 1
        h = o if relayed is None else jnp.where(relayed, c, o)
        onward = copy(ref(h), ref(h), sends(("on", number)), there, mate)
        handoffs[name] = onward

        @pl.when(when)
        def _():
            copy(ref(h), ref(h), sends(("on", number)), here, mate).wait_recv()
            onward.start()

        if relay is not None:
            step, where = relay
            handed = copy(ref(h), ref(h), place[where](("relay", name)), here, at(step))
            emit_copies(when & (i == where), [handed])

    def collect(when, *names):
        @pl.when(when)
        def _():
            for name in names:
                handoffs[name].wait_recv()

    uses = (i0, inner & (i0 | i1), inner & jnp.logical_not(i3))
    relays = (None, (1, 0), (-2, 2))

    def block_arrives(slot, n, when=True):
        arrive(
            uses[slot] & when, (("raw", slot), n), lambda h: zc.at[slot, h, spans[n]],
            (slot % 2) * 4 + n, relays[slot], (None, i1, i0)[slot],
        )

    def map_arrives(slot, when=True):
        for n in range(2):
            arrive(
                uses[slot] & when, (("map", slot), n), lambda h: gc.at[slot, h, parts[n]],
                (slot % 2) * 4 + 2 + n, relays[slot] if slot == 1 or n == 1 else None,
                (None, i1, i0 if n == 1 else None)[slot],
            )

    def handed_on(slot):
        for n in range(2):
            handoffs[("raw", slot), n].wait_send()
            handoffs[("map", slot), n].wait_send()

    def swaps(slot):
        return [
            copy(xm0.at[slot, c], xm0.at[slot, c], sends("m0"), recvs(("m0", slot)), mate),
            copy(xm1.at[slot, c], xm1.at[slot, c], sends("m1"), recvs(("m1", slot)), mate),
        ]

    maps = ((m0, xm0, t0, pm0, 1.0), (m1, xm1, t1, pm1, -1.0))

    def compose(slot, n):
        m, x, _, _, sign = maps[n]
        own = m[c, :rows]
        edge = mm(fc[rows:], own)
        x[slot, c, rows:] = (m[c, rows:].astype(F32) + sign * edge).astype(BF16)
        x[slot, c, :rows] = times(gc.at[slot], body, own).astype(BF16)
        swaps(slot)[n].start()

    def extend(n):
        m, _, t, p, _ = maps[n]
        wb = mm(fc[:rows], m[c, :rows]).astype(BF16)
        for j in range(2):
            span = pl.ds(j * wide, wide)
            p[span] += mm(t[span, :], wb)

    def settle(slot, n):
        m, x, t, _, _ = maps[n]
        one = swaps(slot)[n]
        one.wait_recv()
        m[...] = x[slot]
        for j in range(2):
            t[pl.ds(j * wide, wide), :] = x[slot, j, :rows].T
        one.wait_send()

    later = i0 & top
    prompt = jnp.logical_not(later)
    lazy = i0 & inner
    across_mate = swap("pm1", held.at[c], held.at[c])
    started = jnp.logical_not(i3 & top)

    def y_arrives(n, when):
        arrive(
            started & when, ("y", n), lambda h: zy.at[h, fine[n]], (8, 9, 5, 10)[n], None, (i1 & inner) | i3
        )
        ref = zy.at[o, fine[n]]
        emit_copies(
            i0 & inner & when, [copy(ref, ref, place[0](("relay", n)), recvs(("y", n), 2), at(1))]
        )

    def block_whole(slot):
        for n in range(2):
            unpack_outer(zc.at[slot], fc, n)

    def merge(slot):
        raw, drawn = ("raw", slot), ("map", slot)
        use = uses[slot]
        collect(use, (raw, 0), (drawn, 0), (drawn, 1))

        @pl.when(use)
        def _():
            unpack_first(zc.at[slot], fc)
            compose(slot, 0)

            @pl.when(prompt)
            def _():
                compose(slot, 1)

        if slot == 0:
            block_arrives(1, 1)
            block_arrives(0, 1)
            block_arrives(2, 0, i1)
            map_arrives(2, i1)
            block_arrives(2, 1, i1)
        collect(use, (raw, 1))
        if slot == 0:
            y_arrives(0, later)
            y_arrives(1, later)

        @pl.when(use)
        def _():
            block_whole(slot)

            @pl.when(jnp.logical_not(lazy))
            def _():
                extend(0)

        if slot == 0:
            y_arrives(2, later)
        else:
            block_arrives(2, 0, lazy)
            map_arrives(2, lazy)
            block_arrives(2, 1, lazy)

        @pl.when(use)
        def _():
            settle(slot, 0)

            @pl.when(prompt)
            def _():
                extend(1)
                settle(slot, 1)

            handed_on(slot)

    block_arrives(1, 0)
    block_arrives(0, 0)
    map_arrives(1)
    map_arrives(0)
    merge(0)
    merge(1)
    block_arrives(2, 0, i2)
    map_arrives(2, i2)
    block_arrives(2, 1, i2)
    collect(uses[2], (("raw", 2), 0), (("raw", 2), 1))

    @pl.when(uses[2])
    def _():
        unpack_first(zc.at[2], fc)
        block_whole(2)
        extend(1)

        @pl.when(jnp.logical_not(lazy))
        def _():
            extend(0)

        @pl.when(lazy)
        def _():
            held[c] = pm1[...].astype(BF16)
            across_mate.start()

    y_arrives(0, lazy)
    y_arrives(1, lazy)
    collect(uses[2], (("map", 2), 0), (("map", 2), 1))

    @pl.when(uses[2])
    def _():
        compose(2, 0)
        compose(2, 1)

    y_arrives(2, lazy)
    y_arrives(3, lazy)

    @pl.when(lazy)
    def _():
        across_mate.wait_recv()
        wb = times(held, body, g0f[c]).astype(BF16)
        pm0[mine] = d_ref[0, mine] + mt(g0f[c], wb)
        pm0[other] = d_ref[0, other] + mt(g0f[o], wb)
        across_mate.wait_send()

    @pl.when(uses[2])
    def _():
        settle(2, 0)
        settle(2, 1)
        handed_on(2)

    @pl.when(i3 & inner)
    def _():
        for one in ahead_of_late:
            one.wait_send()
        for one in late:
            one.start()

    pending.append((i3 & inner, late))

    cov = a_ref[...].astype(BF16)

    def edges(step, sign, m):
        for j in range(2):
            kb[step, j] = sign * mm(full[rows:], m[j, :rows]) + m[j, rows:].astype(F32)
        cross_ref[step] = mm(cov, kb[step, c].astype(BF16))

    @pl.when(jnp.logical_not(started))
    def _():
        full[...] = jnp.zeros_like(full)

    for n in range(3):
        y_arrives(n, jnp.logical_not(i0))
    collect(started, ("y", 0), ("y", 1))

    @pl.when(started)
    def _():
        unpack_first(zy, full)

    def close(m, n):
        return mm(full[parts[n], parts[n]], m[c, parts[n]])

    def far(m, n):
        return mm(full[parts[n], parts[1 - n]], m[c, parts[1 - n]])

    y_arrives(3, later | jnp.logical_not(i0))
    edges(0, 1.0, m0)
    begun = [close(m0, n) for n in range(2)]

    @pl.when(prompt)
    def _():
        edges(1, -1.0, m1)
        for n in range(2):
            half_done[parts[n]] = close(m1, n)

    for n in range(2):
        collect(started, ("y", 2 + n))

        @pl.when(started)
        def _():
            unpack_outer(zy, full, n)

    leads = i0 & passes
    heads = i2 & top

    def start_y(n):
        emit_copies(heads, [packed_to(2, n, zy, "y", -2)])
        emit_copies(leads, [packed_to(0, n, zy, "y", -4), packed_to(0, n, zr, "r", 1)])

    w = jnp.concatenate([begun[n] + far(m0, n) for n in range(2)], axis=0).astype(BF16)
    pm0[mine] += mm(t0[mine, :], w)

    @pl.when(leads | heads)
    def _():
        pack_first(pm0, kb[0, c])

    start_y(0)
    start_y(1)
    pm0[other] += mm(t0[other, :], w)

    for n in range(2):

        @pl.when(leads | heads)
        def _():
            pack_outer(pm0, n)

        start_y(2 + n)
    emit_copies(heads, [packed_to(2, n, zy, "y", -1) for n in range(4)])
    emit_copies(leads, [packed_to(0, n, zy, "y", -2) for n in range(4)])

    @pl.when(later)
    def _():
        compose(0, 1)
        extend(1)
        settle(0, 1)
        edges(1, -1.0, m1)
        for n in range(2):
            half_done[parts[n]] = close(m1, n)

    for n in range(2):
        w1[parts[n]] = (half_done[parts[n]] + far(m1, n)).astype(BF16)

    for n in range(4):
        ref = zr.at[o, fine[n]]
        there = zy.at[o, fine[n]]
        forth = copy(ref, there, place[1](("r", n)), recvs(("y", n), 2), at(-2))

        @pl.when(i1 & passes)
        def _():
            copy(ref, ref, place[1](("r", n)), recvs(("r", n)), at(-2)).wait_recv()

        emit_copies(i1 & passes, [forth])

    @pl.when(started)
    def _():
        for n in range(4):
            handoffs["y", n].wait_send()

    for one in first:
        one.wait_send()
    join.wait_send()
    for when, copies in pending:

        @pl.when(when)
        def _():
            for one in copies:
                one.wait_send()


def finish(w1, t1, pm0, pm1, kb, cross_ref, out_hbm, cross_hbm, out, store):
    wide = out.shape[2]
    ends = pltpu.make_async_copy(cross_ref, cross_hbm, store.at[4])
    ends.start()
    stores = []

    def emit(step, j, value):
        span = pl.ds(j * wide, wide)
        out[step, span] = value + mt(kb[step, j].astype(BF16), cross_ref[step].astype(BF16))
        one = pltpu.make_async_copy(out.at[step, span], out_hbm.at[step, span], store.at[2 * step + j])
        one.start()
        stores.append(one)

    for j in range(2):
        emit(0, j, pm0[pl.ds(j * wide, wide)])
    for j in range(2):
        span = pl.ds(j * wide, wide)
        emit(1, j, pm1[span] + mm(t1[span, :], w1[...]))
    ends.wait()
    for one in stores:
        one.wait()


def shards(diagonal_block_inverse, step_map, arrow_map, arrow_cov):
    count, nodes, wide = diagonal_block_inverse.shape
    effects = arrow_map.shape[1]
    tall = nodes + effects
    packed = 4 * (wide // 2) + 2 * effects + MARK
    vmem = pl.BlockSpec(memory_space=pltpu.VMEM)
    hbm = pl.BlockSpec(memory_space=pltpu.HBM)
    held = pl.pallas_call(
        kernel,
        out_shape=(
            jax.ShapeDtypeStruct((nodes, wide), BF16),
            jax.ShapeDtypeStruct((nodes, nodes), BF16),
            jax.ShapeDtypeStruct((nodes, wide), F32),
            jax.ShapeDtypeStruct((nodes, wide), F32),
            jax.ShapeDtypeStruct((count, 2, effects, wide), F32),
            jax.ShapeDtypeStruct((count, effects, wide), F32),
        ),
        in_specs=[hbm] * 4,
        out_specs=(vmem,) * 6,
        scratch_shapes=[
            pltpu.VMEM((count, nodes, wide), F32),
            pltpu.VMEM((count, effects, wide), BF16),
            pltpu.VMEM((effects, effects), F32),
            pltpu.VMEM((2, nodes, wide), BF16),
            pltpu.VMEM((2, nodes, wide), BF16),
            pltpu.VMEM((2, tall, wide), BF16),
            pltpu.VMEM((2, tall, wide), BF16),
            pltpu.VMEM((nodes, nodes), BF16),
            pltpu.VMEM((2, tall, wide), BF16),
            pltpu.VMEM((2, tall, wide), BF16),
            pltpu.VMEM((3, 2, tall, wide), BF16),
            pltpu.VMEM((3, 2, tall, wide), BF16),
            pltpu.VMEM((packed, wide // 2), BF16),
            pltpu.VMEM((2, packed, wide // 2), BF16),
            pltpu.VMEM((2, packed, wide // 2), BF16),
            pltpu.VMEM((3, 2, packed, wide // 2), BF16),
            pltpu.VMEM((3, 2, nodes, wide), BF16),
            pltpu.VMEM((tall, nodes), BF16),
            pltpu.VMEM((tall, nodes), BF16),
            pltpu.VMEM((nodes, wide), F32),
            pltpu.VMEM((2, nodes, wide), BF16),
            pltpu.SemaphoreType.DMA((SENDS,)),
            pltpu.SemaphoreType.DMA((RECVS,)),
            pltpu.SemaphoreType.DMA((6,)),
        ],
        compiler_params=pltpu.CompilerParams(
            collective_id=0, has_side_effects=True, vmem_limit_bytes=28 * 1024 * 1024
        ),
    )(*(
        pltpu.with_memory_space_constraint(array, pltpu.HBM)
        for array in (diagonal_block_inverse, step_map, arrow_map, arrow_cov)
    ))
    return pl.pallas_call(
        finish,
        out_shape=(
            jax.ShapeDtypeStruct((count, nodes, wide), F32),
            jax.ShapeDtypeStruct((count, effects, wide), F32),
        ),
        in_specs=[vmem] * 6,
        out_specs=(hbm, hbm),
        scratch_shapes=[
            pltpu.VMEM((count, nodes, wide), F32),
            pltpu.SemaphoreType.DMA((5,)),
        ],
        compiler_params=pltpu.CompilerParams(vmem_limit_bytes=28 * 1024 * 1024),
    )(*held)


def solution(mesh):
    return jax.shard_map(
        shards,
        mesh=mesh,
        in_specs=(
            P(("rep", "tm"), None, "col"),
            P(("rep", "tm"), None, "col"),
            P(("rep", "tm"), None, "col"),
            P("rep", None),
        ),
        out_specs=(P(("rep", "tm"), None, "col"), P(("rep", "tm"), None, "col")),
        check_vma=False,
    )
```

```python
import jax
import jax.numpy as jnp
from jax import lax
from jax.experimental import pallas as pl
from jax.experimental.pallas import tpu as pltpu
from jax.sharding import PartitionSpec as P

MESH = pl.DeviceIdType.MESH
F32 = jnp.float32
BF16 = jnp.bfloat16
SENDS = 38
RECVS = 47
MARK = 16


def mm(left, right):
    return jnp.dot(left, right, preferred_element_type=F32)


def mt(left, right):
    return lax.dot_general(left, right, (((0,), (0,)), ((), ())), preferred_element_type=F32)


class Slots:
    def __init__(self, start, end):
        self.found = {}
        self.free = start
        self.end = end

    def __call__(self, name, width=1):
        if name not in self.found:
            self.found[name] = self.free
            self.free += width
            assert self.free <= self.end
        return self.found[name]


def kernel(
    d_hbm, g_hbm, h_hbm, a_hbm,
    w1, t1, pm0, pm1, kb, cross_ref,
    d_ref, h_ref, a_ref, g0f, g1f, dh1f, gk, t0, m0, m1, xm0, xm1,
    zs, zy, zr, zc, gc, fc, full, half_done, held,
    send, recv, load,
):
    rows = g0f.shape[1]
    wide = g0f.shape[2]
    tall = gk.shape[1]
    half = wide // 2
    edge_rows = tall - rows
    tm = lax.axis_index("tm")
    c = lax.axis_index("col")
    o = 1 - c
    quads = lax.axis_size("tm") // 4
    q = tm // 4
    i = tm % 4
    top = q == quads - 1
    inner = jnp.logical_not(top)
    passes = q > 0
    i0, i1, i2, i3 = (i == n for n in range(4))
    mate = {"col": o}
    recvs = Slots(0, RECVS)
    sends = Slots(0, 18)
    place = [Slots(18, SENDS) for _ in range(4)]

    def at(step):
        return {"tm": tm + step, "col": o}

    def copy(src, dst, sem, sem_there, device):
        return pltpu.make_async_remote_copy(
            src_ref=src, dst_ref=dst, send_sem=send.at[sem], recv_sem=recv.at[sem_there],
            device_id=device, device_id_type=MESH,
        )

    loads = [
        pltpu.make_async_copy(d_hbm.at[1], d_ref.at[1], load.at[0]),
        pltpu.make_async_copy(h_hbm, h_ref, load.at[1]),
        pltpu.make_async_copy(g_hbm.at[0], g0f.at[c], load.at[2]),
        pltpu.make_async_copy(g_hbm.at[1], g1f.at[c], load.at[3]),
        pltpu.make_async_copy(d_hbm.at[0], d_ref.at[0], load.at[4]),
        pltpu.make_async_copy(a_hbm, a_ref, load.at[5]),
    ]
    for one in loads:
        one.start()

    barrier = pltpu.get_barrier_semaphore()
    pl.semaphore_signal(barrier, inc=1, device_id=mate, device_id_type=MESH)

    def greet(when, steps):
        @pl.when(when)
        def _():
            for step in steps:
                pl.semaphore_signal(barrier, inc=1, device_id=at(step), device_id_type=MESH)

    greet(i0, (1, 2))
    greet(i0 & inner, (3, 4))
    greet(i1, (-1,))
    greet(i1 & inner, (2,))
    greet(i1 & top, (1,))
    greet(i2, (1,))
    greet(i2 & inner, (2,))
    greet(i3 & inner, (2,))

    def one_if(flag):
        return jnp.where(flag, 1, 0)

    targets = (
        1 + 2 * one_if(i3 & inner) + one_if(i2 & top) + one_if(i1 & passes) + 2 * one_if(i0 & passes)
    )

    loads[0].wait()
    loads[1].wait()
    dh1f[c, :rows] = d_ref[1].astype(BF16)
    dh1f[c, rows:] = h_ref[1]
    pl.semaphore_wait(barrier, 1 + targets)

    def swap(name, src, dst):
        return copy(src, dst, sends(name), recvs(name), mate)

    first = [
        swap("dh1", dh1f.at[c], dh1f.at[c]),
        swap("g0", g_hbm.at[0], g0f.at[c]),
        swap("g1", g_hbm.at[1], g1f.at[c]),
    ]
    for one in first:
        one.start()
    for one in loads[2:]:
        one.wait()

    def times(left, span, right):
        return mm(jnp.concatenate([left[0, span], left[1, span]], axis=1), right)

    body = pl.ds(0, rows)
    mine = pl.ds(pl.multiple_of(c * wide, wide), wide)
    other = pl.ds(pl.multiple_of(o * wide, wide), wide)
    edge_base = 2 * half
    mark_base = edge_base + 2 * edge_rows
    first_rows = mark_base + MARK
    top_span = pl.ds(0, first_rows)
    low_span = pl.ds(first_rows, zs.shape[0] - first_rows)
    spans = (top_span, low_span)
    middle = first_rows // 32 * 16
    fine = (
        pl.ds(0, middle), pl.ds(middle, first_rows - middle),
        pl.ds(first_rows, half), pl.ds(first_rows + half, half),
    )
    across = lax.broadcasted_iota(jnp.int32, (half, half), 1)
    down = lax.broadcasted_iota(jnp.int32, (half, half), 0)

    def pack_first(p, edge):
        r = pl.multiple_of(c * wide, wide)
        one = p[pl.ds(r, half), :half]
        two = p[pl.ds(r + half, half), half:]
        zs[:half] = jnp.where(down >= across, one, two).astype(BF16)
        zs[half:edge_base] = p[pl.ds(r, half), half:].astype(BF16)
        zs[edge_base : edge_base + edge_rows] = edge[:, :half].astype(BF16)
        zs[edge_base + edge_rows : mark_base] = edge[:, half:].astype(BF16)
        mark = jnp.sum(jnp.where(down == across, two, 0.0), axis=0, keepdims=True)
        zs[mark_base:first_rows] = jnp.broadcast_to(mark, (MARK, half)).astype(BF16)

    def pack_outer(p, n):
        to = fine[2 + n]

        @pl.when(c == 0)
        def _():
            zs[to] = p[pl.ds(wide + n * half, half), :half].astype(BF16)

        @pl.when(c == 1)
        def _():
            zs[to] = p[half:wide, pl.ds(n * half, half)].astype(BF16)

    def unpack_first(z, full):
        for j in range(2):
            base = j * wide
            lo = pl.ds(base, half)
            hi = pl.ds(base + half, half)
            both = z[j, :half].astype(F32)
            turned = both.T
            mark = z[j, mark_base:first_rows].astype(F32)[:1]
            full[lo, lo] = jnp.where(down >= across, both, turned).astype(BF16)
            full[hi, hi] = jnp.where(
                down < across, both, jnp.where(down == across, mark, turned)
            ).astype(BF16)
            side = z[j, half:edge_base]
            full[lo, hi] = side
            full[hi, lo] = side.T
            for n in range(2):
                full[rows:, pl.ds(base + n * half, half)] = z[
                    j, edge_base + n * edge_rows : edge_base + (n + 1) * edge_rows
                ]

    def unpack_outer(z, full, n):
        far = pl.ds(wide + n * half, half)
        for j in range(2):
            close = pl.ds(j * half, half)
            outer = z[j, fine[2 + n]]
            if j == 0:
                full[far, close] = outer
                full[close, far] = outer.T
            else:
                full[close, far] = outer
                full[far, close] = outer.T

    pending = []

    def emit_copies(when, copies):
        @pl.when(when)
        def _():
            for one in copies:
                one.start()

        pending.append((when, copies))

    def packed_to(where, n, buffer, there, step):
        span = (spans if there[0] == "raw" else fine)[n]
        return copy(
            zs.at[span], buffer.at[c, span],
            place[where]((there, step, n)), recvs((there, n), 1 if there == "r" else 2), at(step),
        )

    parts = (pl.ds(0, wide), pl.ds(wide, wide))

    def map_to(slot, step):
        return [
            copy(
                gk.at[c, parts[n]], gc.at[slot, c, parts[n]],
                place[slot + 1](("map", step, n)), recvs((("map", slot), n), 2), at(step),
            )
            for n in range(2)
        ]

    own0 = g0f[c]
    w = mm(dh1f[c], g0f[c, mine])
    first[0].wait_recv()
    w += mm(dh1f[o], g0f[c, other])
    wb = w[:rows].astype(BF16)
    kappa = w[rows:] - h_ref[0].astype(F32)
    pm0[mine] = d_ref[0, mine] + mt(g0f[c], wb)

    raw_targets = (
        (i3 & inner, 2, (-1, -2)),
        (i2 & inner, 1, (-2,)),
        (i1, 0, (-1,)),
    )

    def start_raw(n):
        for when, slot, steps in raw_targets:
            emit_copies(
                when, [packed_to(slot + 1, n, zc.at[slot], ("raw", slot), step) for step in steps]
            )

    pack_first(pm0, kappa)
    emit_copies(i3 & top, [packed_to(3, n, zy, "y", -1) for n in range(2)])
    start_raw(0)
    first[1].wait_recv()
    pm0[other] = d_ref[0, other] + mt(g0f[o], wb)
    for n in range(2):
        pack_outer(pm0, n)
        emit_copies(i3 & top, [packed_to(3, 2 + n, zy, "y", -1)])

    first[2].wait_recv()
    gk[c, :rows] = times(g1f, body, own0).astype(BF16)
    gk[c, rows:] = kappa.astype(BF16)
    ahead_of_late = map_to(2, -2)
    late = map_to(2, -3)[:1]
    emit_copies(i3 & inner, map_to(2, -1))
    emit_copies(i2 & inner, map_to(1, -2))
    emit_copies(i1, map_to(0, -1))

    @pl.when(i3 & inner)
    def _():
        for one in ahead_of_late:
            one.start()

    start_raw(1)

    join = swap("gk", gk.at[c], gk.at[c])
    join.start()
    pm1[...] = d_ref[1]
    join.wait_recv()
    m0[...] = gk[...]
    m1[:, :rows] = g1f[...]
    m1[:, rows:] = -dh1f[:, rows:]

    def turn():
        for j in range(2):
            span = pl.ds(j * wide, wide)
            t0[span, :] = m0[j, :rows].T
            t1[span, :] = m1[j, :rows].T

    turn()

    handoffs = {}

    def arrive(when, name, ref, number, relay=None, relayed=None):
        here, there = recvs(name, 2), recvs(name, 2) + 1
        h = o if relayed is None else jnp.where(relayed, c, o)
        onward = copy(ref(h), ref(h), sends(("on", number)), there, mate)
        handoffs[name] = onward

        @pl.when(when)
        def _():
            copy(ref(h), ref(h), sends(("on", number)), here, mate).wait_recv()
            onward.start()

        if relay is not None:
            step, where = relay
            handed = copy(ref(h), ref(h), place[where](("relay", name)), here, at(step))
            emit_copies(when & (i == where), [handed])

    def collect(when, *names):
        @pl.when(when)
        def _():
            for name in names:
                handoffs[name].wait_recv()

    uses = (i0, inner & (i0 | i1), inner & jnp.logical_not(i3))
    relays = (None, (1, 0), (-2, 2))

    def block_arrives(slot, n, when=True):
        arrive(
            uses[slot] & when, (("raw", slot), n), lambda h: zc.at[slot, h, spans[n]],
            (slot % 2) * 4 + n, relays[slot], (None, i1, i0)[slot],
        )

    def map_arrives(slot, when=True):
        for n in range(2):
            arrive(
                uses[slot] & when, (("map", slot), n), lambda h: gc.at[slot, h, parts[n]],
                (slot % 2) * 4 + 2 + n, relays[slot] if slot == 1 or n == 1 else None,
                (None, i1, i0 if n == 1 else None)[slot],
            )

    def handed_on(slot):
        for n in range(2):
            handoffs[("raw", slot), n].wait_send()
            handoffs[("map", slot), n].wait_send()

    def swaps(slot):
        return [
            copy(xm0.at[slot, c], xm0.at[slot, c], sends("m0"), recvs(("m0", slot)), mate),
            copy(xm1.at[slot, c], xm1.at[slot, c], sends("m1"), recvs(("m1", slot)), mate),
        ]

    maps = ((m0, xm0, t0, pm0, 1.0), (m1, xm1, t1, pm1, -1.0))

    def compose(slot, n):
        m, x, _, _, sign = maps[n]
        own = m[c, :rows]
        edge = mm(fc[rows:], own)
        x[slot, c, rows:] = (m[c, rows:].astype(F32) + sign * edge).astype(BF16)
        x[slot, c, :rows] = times(gc.at[slot], body, own).astype(BF16)
        swaps(slot)[n].start()

    def extend(n):
        m, _, t, p, _ = maps[n]
        wb = mm(fc[:rows], m[c, :rows]).astype(BF16)
        for j in range(2):
            span = pl.ds(j * wide, wide)
            p[span] += mm(t[span, :], wb)

    def settle(slot, n):
        m, x, t, _, _ = maps[n]
        one = swaps(slot)[n]
        one.wait_recv()
        m[...] = x[slot]
        for j in range(2):
            t[pl.ds(j * wide, wide), :] = x[slot, j, :rows].T
        one.wait_send()

    later = i0 & top
    prompt = jnp.logical_not(later)
    lazy = i0 & inner
    across_mate = swap("pm1", held.at[c], held.at[c])
    started = jnp.logical_not(i3 & top)

    def y_arrives(n, when):
        arrive(
            started & when, ("y", n), lambda h: zy.at[h, fine[n]], (8, 9, 5, 10)[n], None, (i1 & inner) | i3
        )
        ref = zy.at[o, fine[n]]
        emit_copies(
            i0 & inner & when, [copy(ref, ref, place[0](("relay", n)), recvs(("y", n), 2), at(1))]
        )

    def block_whole(slot):
        for n in range(2):
            unpack_outer(zc.at[slot], fc, n)

    def merge(slot):
        raw, drawn = ("raw", slot), ("map", slot)
        use = uses[slot]
        collect(use, (raw, 0), (drawn, 0), (drawn, 1))

        @pl.when(use)
        def _():
            unpack_first(zc.at[slot], fc)
            compose(slot, 0)

            @pl.when(prompt)
            def _():
                compose(slot, 1)

        if slot == 0:
            block_arrives(1, 1)
            block_arrives(0, 1)
            block_arrives(2, 0, i1)
            map_arrives(2, i1)
            block_arrives(2, 1, i1)
        collect(use, (raw, 1))
        if slot == 0:
            y_arrives(0, later)
            y_arrives(1, later)

        @pl.when(use)
        def _():
            block_whole(slot)

            @pl.when(jnp.logical_not(lazy))
            def _():
                extend(0)

        if slot == 0:
            y_arrives(2, later)
        else:
            block_arrives(2, 0, lazy)
            map_arrives(2, lazy)
            block_arrives(2, 1, lazy)

        @pl.when(use)
        def _():
            settle(slot, 0)

            @pl.when(prompt)
            def _():
                extend(1)
                settle(slot, 1)

            handed_on(slot)

    block_arrives(1, 0)
    block_arrives(0, 0)
    map_arrives(1)
    map_arrives(0)
    merge(0)
    merge(1)
    block_arrives(2, 0, i2)
    map_arrives(2, i2)
    block_arrives(2, 1, i2)
    collect(uses[2], (("raw", 2), 0), (("raw", 2), 1))

    @pl.when(uses[2])
    def _():
        unpack_first(zc.at[2], fc)
        block_whole(2)
        extend(1)

        @pl.when(jnp.logical_not(lazy))
        def _():
            extend(0)

        @pl.when(lazy)
        def _():
            held[c] = pm1[...].astype(BF16)
            across_mate.start()

    y_arrives(0, lazy)
    y_arrives(1, lazy)
    y_arrives(2, lazy)
    collect(uses[2], (("map", 2), 0), (("map", 2), 1))

    @pl.when(uses[2])
    def _():
        compose(2, 0)

    y_arrives(3, lazy)

    @pl.when(uses[2])
    def _():
        compose(2, 1)


    @pl.when(lazy)
    def _():
        across_mate.wait_recv()
        wb = times(held, body, g0f[c]).astype(BF16)
        pm0[mine] = d_ref[0, mine] + mt(g0f[c], wb)
        pm0[other] = d_ref[0, other] + mt(g0f[o], wb)
        across_mate.wait_send()

    @pl.when(uses[2])
    def _():
        settle(2, 0)
        settle(2, 1)
        handed_on(2)

    @pl.when(i3 & inner)
    def _():
        for one in ahead_of_late:
            one.wait_send()
        for one in late:
            one.start()

    pending.append((i3 & inner, late))

    cov = a_ref[...].astype(BF16)

    def edges(step, sign, m):
        for j in range(2):
            kb[step, j] = sign * mm(full[rows:], m[j, :rows]) + m[j, rows:].astype(F32)
        cross_ref[step] = mm(cov, kb[step, c].astype(BF16))

    @pl.when(jnp.logical_not(started))
    def _():
        full[...] = jnp.zeros_like(full)

    for n in range(3):
        y_arrives(n, jnp.logical_not(i0))
    collect(started, ("y", 0), ("y", 1))

    @pl.when(started)
    def _():
        unpack_first(zy, full)

    def close(m, n):
        return mm(full[parts[n], parts[n]], m[c, parts[n]])

    def far(m, n):
        return mm(full[parts[n], parts[1 - n]], m[c, parts[1 - n]])

    y_arrives(3, later | jnp.logical_not(i0))
    edges(0, 1.0, m0)
    begun = [close(m0, n) for n in range(2)]

    @pl.when(prompt)
    def _():
        edges(1, -1.0, m1)
        for n in range(2):
            half_done[parts[n]] = close(m1, n)

    for n in range(2):
        collect(started, ("y", 2 + n))

        @pl.when(started)
        def _():
            unpack_outer(zy, full, n)

    leads = i0 & passes
    heads = i2 & top

    def start_y(n):
        emit_copies(heads, [packed_to(2, n, zy, "y", -2)])
        emit_copies(leads, [packed_to(0, n, zy, "y", -4), packed_to(0, n, zr, "r", 1)])

    w = jnp.concatenate([begun[n] + far(m0, n) for n in range(2)], axis=0).astype(BF16)
    pm0[mine] += mm(t0[mine, :], w)

    @pl.when(leads | heads)
    def _():
        pack_first(pm0, kb[0, c])

    start_y(0)
    start_y(1)
    pm0[other] += mm(t0[other, :], w)

    for n in range(2):

        @pl.when(leads | heads)
        def _():
            pack_outer(pm0, n)

        start_y(2 + n)
    emit_copies(heads, [packed_to(2, n, zy, "y", -1) for n in range(4)])
    emit_copies(leads, [packed_to(0, n, zy, "y", -2) for n in range(4)])

    @pl.when(later)
    def _():
        compose(0, 1)
        extend(1)
        settle(0, 1)
        edges(1, -1.0, m1)
        for n in range(2):
            half_done[parts[n]] = close(m1, n)

    for n in range(2):
        w1[parts[n]] = (half_done[parts[n]] + far(m1, n)).astype(BF16)

    for n in range(4):
        ref = zr.at[o, fine[n]]
        there = zy.at[o, fine[n]]
        forth = copy(ref, there, place[1](("r", n)), recvs(("y", n), 2), at(-2))

        @pl.when(i1 & passes)
        def _():
            copy(ref, ref, place[1](("r", n)), recvs(("r", n)), at(-2)).wait_recv()

        emit_copies(i1 & passes, [forth])

    @pl.when(started)
    def _():
        for n in range(4):
            handoffs["y", n].wait_send()

    for one in first:
        one.wait_send()
    join.wait_send()
    for when, copies in pending:

        @pl.when(when)
        def _():
            for one in copies:
                one.wait_send()


def finish(w1, t1, pm0, pm1, kb, cross_ref, out_hbm, cross_hbm, out, store):
    wide = out.shape[2]
    ends = pltpu.make_async_copy(cross_ref, cross_hbm, store.at[4])
    ends.start()
    stores = []

    def emit(step, j, value):
        span = pl.ds(j * wide, wide)
        out[step, span] = value + mt(kb[step, j].astype(BF16), cross_ref[step].astype(BF16))
        one = pltpu.make_async_copy(out.at[step, span], out_hbm.at[step, span], store.at[2 * step + j])
        one.start()
        stores.append(one)

    for j in range(2):
        emit(0, j, pm0[pl.ds(j * wide, wide)])
    for j in range(2):
        span = pl.ds(j * wide, wide)
        emit(1, j, pm1[span] + mm(t1[span, :], w1[...]))
    ends.wait()
    for one in stores:
        one.wait()


def shards(diagonal_block_inverse, step_map, arrow_map, arrow_cov):
    count, nodes, wide = diagonal_block_inverse.shape
    effects = arrow_map.shape[1]
    tall = nodes + effects
    packed = 4 * (wide // 2) + 2 * effects + MARK
    vmem = pl.BlockSpec(memory_space=pltpu.VMEM)
    hbm = pl.BlockSpec(memory_space=pltpu.HBM)
    held = pl.pallas_call(
        kernel,
        out_shape=(
            jax.ShapeDtypeStruct((nodes, wide), BF16),
            jax.ShapeDtypeStruct((nodes, nodes), BF16),
            jax.ShapeDtypeStruct((nodes, wide), F32),
            jax.ShapeDtypeStruct((nodes, wide), F32),
            jax.ShapeDtypeStruct((count, 2, effects, wide), F32),
            jax.ShapeDtypeStruct((count, effects, wide), F32),
        ),
        in_specs=[hbm] * 4,
        out_specs=(vmem,) * 6,
        scratch_shapes=[
            pltpu.VMEM((count, nodes, wide), F32),
            pltpu.VMEM((count, effects, wide), BF16),
            pltpu.VMEM((effects, effects), F32),
            pltpu.VMEM((2, nodes, wide), BF16),
            pltpu.VMEM((2, nodes, wide), BF16),
            pltpu.VMEM((2, tall, wide), BF16),
            pltpu.VMEM((2, tall, wide), BF16),
            pltpu.VMEM((nodes, nodes), BF16),
            pltpu.VMEM((2, tall, wide), BF16),
            pltpu.VMEM((2, tall, wide), BF16),
            pltpu.VMEM((3, 2, tall, wide), BF16),
            pltpu.VMEM((3, 2, tall, wide), BF16),
            pltpu.VMEM((packed, wide // 2), BF16),
            pltpu.VMEM((2, packed, wide // 2), BF16),
            pltpu.VMEM((2, packed, wide // 2), BF16),
            pltpu.VMEM((3, 2, packed, wide // 2), BF16),
            pltpu.VMEM((3, 2, nodes, wide), BF16),
            pltpu.VMEM((tall, nodes), BF16),
            pltpu.VMEM((tall, nodes), BF16),
            pltpu.VMEM((nodes, wide), F32),
            pltpu.VMEM((2, nodes, wide), BF16),
            pltpu.SemaphoreType.DMA((SENDS,)),
            pltpu.SemaphoreType.DMA((RECVS,)),
            pltpu.SemaphoreType.DMA((6,)),
        ],
        compiler_params=pltpu.CompilerParams(
            collective_id=0, has_side_effects=True, vmem_limit_bytes=28 * 1024 * 1024
        ),
    )(*(
        pltpu.with_memory_space_constraint(array, pltpu.HBM)
        for array in (diagonal_block_inverse, step_map, arrow_map, arrow_cov)
    ))
    return pl.pallas_call(
        finish,
        out_shape=(
            jax.ShapeDtypeStruct((count, nodes, wide), F32),
            jax.ShapeDtypeStruct((count, effects, wide), F32),
        ),
        in_specs=[vmem] * 6,
        out_specs=(hbm, hbm),
        scratch_shapes=[
            pltpu.VMEM((count, nodes, wide), F32),
            pltpu.SemaphoreType.DMA((5,)),
        ],
        compiler_params=pltpu.CompilerParams(vmem_limit_bytes=28 * 1024 * 1024),
    )(*held)


def solution(mesh):
    return jax.shard_map(
        shards,
        mesh=mesh,
        in_specs=(
            P(("rep", "tm"), None, "col"),
            P(("rep", "tm"), None, "col"),
            P(("rep", "tm"), None, "col"),
            P("rep", None),
        ),
        out_specs=(P(("rep", "tm"), None, "col"), P(("rep", "tm"), None, "col")),
        check_vma=False,
    )
```

```python
import jax
import jax.numpy as jnp
from jax import lax
from jax.experimental import pallas as pl
from jax.experimental.pallas import tpu as pltpu
from jax.sharding import PartitionSpec as P

MESH = pl.DeviceIdType.MESH
F32 = jnp.float32
BF16 = jnp.bfloat16
SENDS = 38
RECVS = 47
MARK = 16


def mm(left, right):
    return jnp.dot(left, right, preferred_element_type=F32)


def mt(left, right):
    return lax.dot_general(left, right, (((0,), (0,)), ((), ())), preferred_element_type=F32)


class Slots:
    def __init__(self, start, end):
        self.found = {}
        self.free = start
        self.end = end

    def __call__(self, name, width=1):
        if name not in self.found:
            self.found[name] = self.free
            self.free += width
            assert self.free <= self.end
        return self.found[name]


def kernel(
    d_hbm, g_hbm, h_hbm, a_hbm,
    w1, t1, pm0, pm1, kb, cross_ref,
    d_ref, h_ref, a_ref, g0f, g1f, dh1f, gk, t0, m0, m1, xm0, xm1,
    zs, zy, zr, zc, gc, fc, full, half_done, held,
    send, recv, load,
):
    rows = g0f.shape[1]
    wide = g0f.shape[2]
    tall = gk.shape[1]
    half = wide // 2
    edge_rows = tall - rows
    tm = lax.axis_index("tm")
    c = lax.axis_index("col")
    o = 1 - c
    quads = lax.axis_size("tm") // 4
    q = tm // 4
    i = tm % 4
    top = q == quads - 1
    inner = jnp.logical_not(top)
    passes = q > 0
    i0, i1, i2, i3 = (i == n for n in range(4))
    mate = {"col": o}
    recvs = Slots(0, RECVS)
    sends = Slots(0, 18)
    place = [Slots(18, SENDS) for _ in range(4)]

    def at(step):
        return {"tm": tm + step, "col": o}

    def copy(src, dst, sem, sem_there, device):
        return pltpu.make_async_remote_copy(
            src_ref=src, dst_ref=dst, send_sem=send.at[sem], recv_sem=recv.at[sem_there],
            device_id=device, device_id_type=MESH,
        )

    loads = [
        pltpu.make_async_copy(d_hbm.at[1], d_ref.at[1], load.at[0]),
        pltpu.make_async_copy(h_hbm, h_ref, load.at[1]),
        pltpu.make_async_copy(g_hbm.at[0], g0f.at[c], load.at[2]),
        pltpu.make_async_copy(g_hbm.at[1], g1f.at[c], load.at[3]),
        pltpu.make_async_copy(d_hbm.at[0], d_ref.at[0], load.at[4]),
        pltpu.make_async_copy(a_hbm, a_ref, load.at[5]),
    ]
    for one in loads:
        one.start()

    barrier = pltpu.get_barrier_semaphore()
    pl.semaphore_signal(barrier, inc=1, device_id=mate, device_id_type=MESH)

    def greet(when, steps):
        @pl.when(when)
        def _():
            for step in steps:
                pl.semaphore_signal(barrier, inc=1, device_id=at(step), device_id_type=MESH)

    greet(i0, (1, 2))
    greet(i0 & inner, (3, 4))
    greet(i1, (-1,))
    greet(i1 & inner, (2,))
    greet(i1 & top, (1,))
    greet(i2, (1,))
    greet(i2 & inner, (2,))
    greet(i3 & inner, (2,))

    def one_if(flag):
        return jnp.where(flag, 1, 0)

    targets = (
        1 + 2 * one_if(i3 & inner) + one_if(i2 & top) + one_if(i1 & passes) + 2 * one_if(i0 & passes)
    )

    loads[0].wait()
    loads[1].wait()
    dh1f[c, :rows] = d_ref[1].astype(BF16)
    dh1f[c, rows:] = h_ref[1]
    pl.semaphore_wait(barrier, 1 + targets)

    def swap(name, src, dst):
        return copy(src, dst, sends(name), recvs(name), mate)

    first = [
        swap("dh1", dh1f.at[c], dh1f.at[c]),
        swap("g0", g_hbm.at[0], g0f.at[c]),
        swap("g1", g_hbm.at[1], g1f.at[c]),
    ]
    for one in first:
        one.start()
    for one in loads[2:]:
        one.wait()

    def times(left, span, right):
        return mm(jnp.concatenate([left[0, span], left[1, span]], axis=1), right)

    body = pl.ds(0, rows)
    mine = pl.ds(pl.multiple_of(c * wide, wide), wide)
    other = pl.ds(pl.multiple_of(o * wide, wide), wide)
    edge_base = 2 * half
    mark_base = edge_base + 2 * edge_rows
    first_rows = mark_base + MARK
    top_span = pl.ds(0, first_rows)
    low_span = pl.ds(first_rows, zs.shape[0] - first_rows)
    spans = (top_span, low_span)
    middle = first_rows // 32 * 16
    fine = (
        pl.ds(0, middle), pl.ds(middle, first_rows - middle),
        pl.ds(first_rows, half), pl.ds(first_rows + half, half),
    )
    across = lax.broadcasted_iota(jnp.int32, (half, half), 1)
    down = lax.broadcasted_iota(jnp.int32, (half, half), 0)

    def pack_first(p, edge):
        r = pl.multiple_of(c * wide, wide)
        one = p[pl.ds(r, half), :half]
        two = p[pl.ds(r + half, half), half:]
        zs[:half] = jnp.where(down >= across, one, two).astype(BF16)
        zs[half:edge_base] = p[pl.ds(r, half), half:].astype(BF16)
        zs[edge_base : edge_base + edge_rows] = edge[:, :half].astype(BF16)
        zs[edge_base + edge_rows : mark_base] = edge[:, half:].astype(BF16)
        mark = jnp.sum(jnp.where(down == across, two, 0.0), axis=0, keepdims=True)
        zs[mark_base:first_rows] = jnp.broadcast_to(mark, (MARK, half)).astype(BF16)

    def pack_outer(p, n):
        to = fine[2 + n]

        @pl.when(c == 0)
        def _():
            zs[to] = p[pl.ds(wide + n * half, half), :half].astype(BF16)

        @pl.when(c == 1)
        def _():
            zs[to] = p[half:wide, pl.ds(n * half, half)].astype(BF16)

    def unpack_first(z, full):
        for j in range(2):
            base = j * wide
            lo = pl.ds(base, half)
            hi = pl.ds(base + half, half)
            both = z[j, :half].astype(F32)
            turned = both.T
            mark = z[j, mark_base:first_rows].astype(F32)[:1]
            full[lo, lo] = jnp.where(down >= across, both, turned).astype(BF16)
            full[hi, hi] = jnp.where(
                down < across, both, jnp.where(down == across, mark, turned)
            ).astype(BF16)
            side = z[j, half:edge_base]
            full[lo, hi] = side
            full[hi, lo] = side.T
            for n in range(2):
                full[rows:, pl.ds(base + n * half, half)] = z[
                    j, edge_base + n * edge_rows : edge_base + (n + 1) * edge_rows
                ]

    def unpack_outer(z, full, n):
        far = pl.ds(wide + n * half, half)
        for j in range(2):
            close = pl.ds(j * half, half)
            outer = z[j, fine[2 + n]]
            if j == 0:
                full[far, close] = outer
                full[close, far] = outer.T
            else:
                full[close, far] = outer
                full[far, close] = outer.T

    pending = []

    def emit_copies(when, copies):
        @pl.when(when)
        def _():
            for one in copies:
                one.start()

        pending.append((when, copies))

    def packed_to(where, n, buffer, there, step):
        span = (spans if there[0] == "raw" else fine)[n]
        return copy(
            zs.at[span], buffer.at[c, span],
            place[where]((there, step, n)), recvs((there, n), 1 if there == "r" else 2), at(step),
        )

    parts = (pl.ds(0, wide), pl.ds(wide, wide))

    def map_to(slot, step):
        return [
            copy(
                gk.at[c, parts[n]], gc.at[slot, c, parts[n]],
                place[slot + 1](("map", step, n)), recvs((("map", slot), n), 2), at(step),
            )
            for n in range(2)
        ]

    own0 = g0f[c]
    w = mm(dh1f[c], g0f[c, mine])
    first[0].wait_recv()
    w += mm(dh1f[o], g0f[c, other])
    wb = w[:rows].astype(BF16)
    kappa = w[rows:] - h_ref[0].astype(F32)
    pm0[mine] = d_ref[0, mine] + mt(g0f[c], wb)

    raw_targets = (
        (i3 & inner, 2, (-1, -2)),
        (i2 & inner, 1, (-2,)),
        (i1, 0, (-1,)),
    )

    def start_raw(n):
        for when, slot, steps in raw_targets:
            emit_copies(
                when, [packed_to(slot + 1, n, zc.at[slot], ("raw", slot), step) for step in steps]
            )

    pack_first(pm0, kappa)
    emit_copies(i3 & top, [packed_to(3, n, zy, "y", -1) for n in range(2)])
    start_raw(0)
    first[1].wait_recv()
    pm0[other] = d_ref[0, other] + mt(g0f[o], wb)
    for n in range(2):
        pack_outer(pm0, n)
        emit_copies(i3 & top, [packed_to(3, 2 + n, zy, "y", -1)])

    first[2].wait_recv()
    gk[c, :rows] = times(g1f, body, own0).astype(BF16)
    gk[c, rows:] = kappa.astype(BF16)
    ahead_of_late = map_to(2, -2)
    late = map_to(2, -3)[:1]
    emit_copies(i3 & inner, map_to(2, -1))
    emit_copies(i2 & inner, map_to(1, -2))
    emit_copies(i1, map_to(0, -1))

    @pl.when(i3 & inner)
    def _():
        for one in ahead_of_late:
            one.start()

    start_raw(1)

    join = swap("gk", gk.at[c], gk.at[c])
    join.start()
    pm1[...] = d_ref[1]
    join.wait_recv()
    m0[...] = gk[...]
    m1[:, :rows] = g1f[...]
    m1[:, rows:] = -dh1f[:, rows:]

    def turn():
        for j in range(2):
            span = pl.ds(j * wide, wide)
            t0[span, :] = m0[j, :rows].T
            t1[span, :] = m1[j, :rows].T

    turn()

    handoffs = {}

    def arrive(when, name, ref, number, relay=None, relayed=None):
        here, there = recvs(name, 2), recvs(name, 2) + 1
        h = o if relayed is None else jnp.where(relayed, c, o)
        onward = copy(ref(h), ref(h), sends(("on", number)), there, mate)
        handoffs[name] = onward

        @pl.when(when)
        def _():
            copy(ref(h), ref(h), sends(("on", number)), here, mate).wait_recv()
            onward.start()

        if relay is not None:
            step, where = relay
            handed = copy(ref(h), ref(h), place[where](("relay", name)), here, at(step))
            emit_copies(when & (i == where), [handed])

    def collect(when, *names):
        @pl.when(when)
        def _():
            for name in names:
                handoffs[name].wait_recv()

    uses = (i0, inner & (i0 | i1), inner & jnp.logical_not(i3))
    relays = (None, (1, 0), (-2, 2))

    def block_arrives(slot, n, when=True):
        arrive(
            uses[slot] & when, (("raw", slot), n), lambda h: zc.at[slot, h, spans[n]],
            (slot % 2) * 4 + n, relays[slot], (None, i1, i0)[slot],
        )

    def map_arrives(slot, when=True):
        for n in range(2):
            arrive(
                uses[slot] & when, (("map", slot), n), lambda h: gc.at[slot, h, parts[n]],
                (slot % 2) * 4 + 2 + n, relays[slot] if slot == 1 or n == 1 else None,
                (None, i1, i0 if n == 1 else None)[slot],
            )

    def handed_on(slot):
        for n in range(2):
            handoffs[("raw", slot), n].wait_send()
            handoffs[("map", slot), n].wait_send()

    def swaps(slot):
        return [
            copy(xm0.at[slot, c], xm0.at[slot, c], sends("m0"), recvs(("m0", slot)), mate),
            copy(xm1.at[slot, c], xm1.at[slot, c], sends("m1"), recvs(("m1", slot)), mate),
        ]

    maps = ((m0, xm0, t0, pm0, 1.0), (m1, xm1, t1, pm1, -1.0))

    def compose(slot, n):
        m, x, _, _, sign = maps[n]
        own = m[c, :rows]
        edge = mm(fc[rows:], own)
        x[slot, c, rows:] = (m[c, rows:].astype(F32) + sign * edge).astype(BF16)
        x[slot, c, :rows] = times(gc.at[slot], body, own).astype(BF16)
        swaps(slot)[n].start()

    def extend(n):
        m, _, t, p, _ = maps[n]
        wb = mm(fc[:rows], m[c, :rows]).astype(BF16)
        for j in range(2):
            span = pl.ds(j * wide, wide)
            p[span] += mm(t[span, :], wb)

    def settle(slot, n):
        m, x, t, _, _ = maps[n]
        one = swaps(slot)[n]
        one.wait_recv()
        if slot == 1:
            m[c] = x[slot, c]
        else:
            m[...] = x[slot]
        for j in range(2):
            t[pl.ds(j * wide, wide), :] = x[slot, j, :rows].T
        one.wait_send()

    later = i0 & top
    prompt = jnp.logical_not(later)
    lazy = i0 & inner
    across_mate = swap("pm1", held.at[c], held.at[c])
    started = jnp.logical_not(i3 & top)

    def y_arrives(n, when):
        arrive(
            started & when, ("y", n), lambda h: zy.at[h, fine[n]], (8, 9, 5, 10)[n], None, (i1 & inner) | i3
        )
        ref = zy.at[o, fine[n]]
        emit_copies(
            i0 & inner & when, [copy(ref, ref, place[0](("relay", n)), recvs(("y", n), 2), at(1))]
        )

    def block_whole(slot):
        for n in range(2):
            unpack_outer(zc.at[slot], fc, n)

    def merge(slot):
        raw, drawn = ("raw", slot), ("map", slot)
        use = uses[slot]
        collect(use, (raw, 0), (drawn, 0), (drawn, 1))

        @pl.when(use)
        def _():
            unpack_first(zc.at[slot], fc)
            compose(slot, 0)

            @pl.when(prompt)
            def _():
                compose(slot, 1)

        if slot == 0:
            block_arrives(1, 1)
            block_arrives(0, 1)
            block_arrives(2, 0, i1)
            map_arrives(2, i1)
            block_arrives(2, 1, i1)
        collect(use, (raw, 1))
        if slot == 0:
            y_arrives(0, later)
            y_arrives(1, later)

        @pl.when(use)
        def _():
            block_whole(slot)

            @pl.when(jnp.logical_not(lazy))
            def _():
                extend(0)

        if slot == 0:
            y_arrives(2, later)
        else:
            block_arrives(2, 0, lazy)
            map_arrives(2, lazy)
            block_arrives(2, 1, lazy)

        @pl.when(use)
        def _():
            settle(slot, 0)

            @pl.when(prompt)
            def _():
                extend(1)
                settle(slot, 1)

            handed_on(slot)

    block_arrives(1, 0)
    block_arrives(0, 0)
    map_arrives(1)
    map_arrives(0)
    merge(0)
    merge(1)
    block_arrives(2, 0, i2)
    map_arrives(2, i2)
    block_arrives(2, 1, i2)
    collect(uses[2], (("raw", 2), 0), (("raw", 2), 1))

    @pl.when(uses[2])
    def _():
        unpack_first(zc.at[2], fc)
        block_whole(2)
        extend(1)

        @pl.when(jnp.logical_not(lazy))
        def _():
            extend(0)

        @pl.when(lazy)
        def _():
            held[c] = pm1[...].astype(BF16)
            across_mate.start()

    y_arrives(0, lazy)
    y_arrives(1, lazy)
    y_arrives(2, lazy)
    collect(uses[2], (("map", 2), 0), (("map", 2), 1))

    @pl.when(uses[2])
    def _():
        compose(2, 0)
        compose(2, 1)

    y_arrives(3, lazy)

    @pl.when(lazy)
    def _():
        across_mate.wait_recv()
        wb = times(held, body, g0f[c]).astype(BF16)
        pm0[mine] = d_ref[0, mine] + mt(g0f[c], wb)
        pm0[other] = d_ref[0, other] + mt(g0f[o], wb)
        across_mate.wait_send()

    @pl.when(uses[2])
    def _():
        settle(2, 0)
        settle(2, 1)
        handed_on(2)

    @pl.when(i3 & inner)
    def _():
        for one in ahead_of_late:
            one.wait_send()
        for one in late:
            one.start()

    pending.append((i3 & inner, late))

    cov = a_ref[...].astype(BF16)

    def edges(step, sign, m):
        for j in range(2):
            kb[step, j] = sign * mm(full[rows:], m[j, :rows]) + m[j, rows:].astype(F32)
        cross_ref[step] = mm(cov, kb[step, c].astype(BF16))

    @pl.when(jnp.logical_not(started))
    def _():
        full[...] = jnp.zeros_like(full)

    for n in range(3):
        y_arrives(n, jnp.logical_not(i0))
    collect(started, ("y", 0), ("y", 1))

    @pl.when(started)
    def _():
        unpack_first(zy, full)

    def close(m, n):
        return mm(full[parts[n], parts[n]], m[c, parts[n]])

    def far(m, n):
        return mm(full[parts[n], parts[1 - n]], m[c, parts[1 - n]])

    y_arrives(3, later | jnp.logical_not(i0))
    edges(0, 1.0, m0)
    begun = [close(m0, n) for n in range(2)]

    @pl.when(prompt)
    def _():
        edges(1, -1.0, m1)
        for n in range(2):
            half_done[parts[n]] = close(m1, n)

    for n in range(2):
        collect(started, ("y", 2 + n))

        @pl.when(started)
        def _():
            unpack_outer(zy, full, n)

    leads = i0 & passes
    heads = i2 & top

    def start_y(n):
        emit_copies(heads, [packed_to(2, n, zy, "y", -2)])
        emit_copies(leads, [packed_to(0, n, zy, "y", -4), packed_to(0, n, zr, "r", 1)])

    w = jnp.concatenate([begun[n] + far(m0, n) for n in range(2)], axis=0).astype(BF16)
    pm0[mine] += mm(t0[mine, :], w)

    @pl.when(leads | heads)
    def _():
        pack_first(pm0, kb[0, c])

    start_y(0)
    start_y(1)
    pm0[other] += mm(t0[other, :], w)

    for n in range(2):

        @pl.when(leads | heads)
        def _():
            pack_outer(pm0, n)

        start_y(2 + n)
    emit_copies(heads, [packed_to(2, n, zy, "y", -1) for n in range(4)])
    emit_copies(leads, [packed_to(0, n, zy, "y", -2) for n in range(4)])

    @pl.when(later)
    def _():
        compose(0, 1)
        extend(1)
        settle(0, 1)
        edges(1, -1.0, m1)
        for n in range(2):
            half_done[parts[n]] = close(m1, n)

    for n in range(2):
        w1[parts[n]] = (half_done[parts[n]] + far(m1, n)).astype(BF16)

    for n in range(4):
        ref = zr.at[o, fine[n]]
        there = zy.at[o, fine[n]]
        forth = copy(ref, there, place[1](("r", n)), recvs(("y", n), 2), at(-2))

        @pl.when(i1 & passes)
        def _():
            copy(ref, ref, place[1](("r", n)), recvs(("r", n)), at(-2)).wait_recv()

        emit_copies(i1 & passes, [forth])

    @pl.when(started)
    def _():
        for n in range(4):
            handoffs["y", n].wait_send()

    for one in first:
        one.wait_send()
    join.wait_send()
    for when, copies in pending:

        @pl.when(when)
        def _():
            for one in copies:
                one.wait_send()


def finish(w1, t1, pm0, pm1, kb, cross_ref, out_hbm, cross_hbm, out, store):
    wide = out.shape[2]
    ends = pltpu.make_async_copy(cross_ref, cross_hbm, store.at[4])
    ends.start()
    stores = []

    def emit(step, j, value):
        span = pl.ds(j * wide, wide)
        out[step, span] = value + mt(kb[step, j].astype(BF16), cross_ref[step].astype(BF16))
        one = pltpu.make_async_copy(out.at[step, span], out_hbm.at[step, span], store.at[2 * step + j])
        one.start()
        stores.append(one)

    for j in range(2):
        emit(0, j, pm0[pl.ds(j * wide, wide)])
    for j in range(2):
        span = pl.ds(j * wide, wide)
        emit(1, j, pm1[span] + mm(t1[span, :], w1[...]))
    ends.wait()
    for one in stores:
        one.wait()


def shards(diagonal_block_inverse, step_map, arrow_map, arrow_cov):
    count, nodes, wide = diagonal_block_inverse.shape
    effects = arrow_map.shape[1]
    tall = nodes + effects
    packed = 4 * (wide // 2) + 2 * effects + MARK
    vmem = pl.BlockSpec(memory_space=pltpu.VMEM)
    hbm = pl.BlockSpec(memory_space=pltpu.HBM)
    held = pl.pallas_call(
        kernel,
        out_shape=(
            jax.ShapeDtypeStruct((nodes, wide), BF16),
            jax.ShapeDtypeStruct((nodes, nodes), BF16),
            jax.ShapeDtypeStruct((nodes, wide), F32),
            jax.ShapeDtypeStruct((nodes, wide), F32),
            jax.ShapeDtypeStruct((count, 2, effects, wide), F32),
            jax.ShapeDtypeStruct((count, effects, wide), F32),
        ),
        in_specs=[hbm] * 4,
        out_specs=(vmem,) * 6,
        scratch_shapes=[
            pltpu.VMEM((count, nodes, wide), F32),
            pltpu.VMEM((count, effects, wide), BF16),
            pltpu.VMEM((effects, effects), F32),
            pltpu.VMEM((2, nodes, wide), BF16),
            pltpu.VMEM((2, nodes, wide), BF16),
            pltpu.VMEM((2, tall, wide), BF16),
            pltpu.VMEM((2, tall, wide), BF16),
            pltpu.VMEM((nodes, nodes), BF16),
            pltpu.VMEM((2, tall, wide), BF16),
            pltpu.VMEM((2, tall, wide), BF16),
            pltpu.VMEM((3, 2, tall, wide), BF16),
            pltpu.VMEM((3, 2, tall, wide), BF16),
            pltpu.VMEM((packed, wide // 2), BF16),
            pltpu.VMEM((2, packed, wide // 2), BF16),
            pltpu.VMEM((2, packed, wide // 2), BF16),
            pltpu.VMEM((3, 2, packed, wide // 2), BF16),
            pltpu.VMEM((3, 2, nodes, wide), BF16),
            pltpu.VMEM((tall, nodes), BF16),
            pltpu.VMEM((tall, nodes), BF16),
            pltpu.VMEM((nodes, wide), F32),
            pltpu.VMEM((2, nodes, wide), BF16),
            pltpu.SemaphoreType.DMA((SENDS,)),
            pltpu.SemaphoreType.DMA((RECVS,)),
            pltpu.SemaphoreType.DMA((6,)),
        ],
        compiler_params=pltpu.CompilerParams(
            collective_id=0, has_side_effects=True, vmem_limit_bytes=28 * 1024 * 1024
        ),
    )(*(
        pltpu.with_memory_space_constraint(array, pltpu.HBM)
        for array in (diagonal_block_inverse, step_map, arrow_map, arrow_cov)
    ))
    return pl.pallas_call(
        finish,
        out_shape=(
            jax.ShapeDtypeStruct((count, nodes, wide), F32),
            jax.ShapeDtypeStruct((count, effects, wide), F32),
        ),
        in_specs=[vmem] * 6,
        out_specs=(hbm, hbm),
        scratch_shapes=[
            pltpu.VMEM((count, nodes, wide), F32),
            pltpu.SemaphoreType.DMA((5,)),
        ],
        compiler_params=pltpu.CompilerParams(vmem_limit_bytes=28 * 1024 * 1024),
    )(*held)


def solution(mesh):
    return jax.shard_map(
        shards,
        mesh=mesh,
        in_specs=(
            P(("rep", "tm"), None, "col"),
            P(("rep", "tm"), None, "col"),
            P(("rep", "tm"), None, "col"),
            P("rep", None),
        ),
        out_specs=(P(("rep", "tm"), None, "col"), P(("rep", "tm"), None, "col")),
        check_vma=False,
    )
```
